32 devices in a mesh: fsdp: 8 (over y, x, core), seq: 4 (over z).
Axes of the slice: x: 2, y: 2, z: 4, core: 2. Of those that a mesh axis runs over, the one named last changes fastest.
Arguments:
- tokens: bfloat16 [8192, 2048], P(('fsdp', 'seq')), may hold values from -6 to 6
- seq_lengths: int32 [8], P('fsdp'), may hold values from 512 to 1024, as said below
- attn_gain: bfloat16 [2048], P('fsdp'), may hold values from 0.5 to 1.5
- query_proj: bfloat16 [2048, 2048], P('fsdp'), may hold values from -0.125 to 0.125
- key_proj: bfloat16 [2048, 2048], P('fsdp'), may hold values from -0.125 to 0.125
- value_proj: bfloat16 [2048, 2048], P('fsdp'), may hold values from -0.125 to 0.125
- decay_down: bfloat16 [2048, 16], P('fsdp'), may hold values from -0.125 to 0.125
- decay_up: bfloat16 [16, 256], P(None, 'fsdp'), may hold values from -1.5 to 1.5
- decay_bias: bfloat16 [256], P('fsdp'), may hold values from 1.5 to 6
- swish_proj: bfloat16 [2048, 2048], P('fsdp'), may hold values from -0.125 to 0.125
- slot_gain: bfloat16 [2048], P('fsdp'), may hold values from 0.5 to 1.5
- out_proj: bfloat16 [2048, 2048], P('fsdp'), may hold values from -0.25 to 0.25
- mlp_gain: bfloat16 [2048], P('fsdp'), may hold values from 0.5 to 1.5
- mlp_gate: bfloat16 [2048, 5632], P('fsdp'), may hold values from -0.125 to 0.125
- mlp_up: bfloat16 [2048, 5632], P('fsdp'), may hold values from -0.125 to 0.125
- mlp_down: bfloat16 [5632, 2048], P('fsdp'), may hold values from -0.078125 to 0.078125
- grad_out: bfloat16 [8192, 2048], P(('fsdp', 'seq')), may hold values from -6 to 6
Outputs:
- result: bfloat16 [8192, 2048], P(('fsdp', 'seq'))
- grad_tokens: bfloat16 [8192, 2048], P(('fsdp', 'seq'))
- attn_gain_grad: float32 [2048], P('fsdp')
- query_proj_grad: float32 [2048, 2048], P('fsdp')
- key_proj_grad: float32 [2048, 2048], P('fsdp')
- value_proj_grad: float32 [2048, 2048], P('fsdp')
- decay_down_grad: float32 [2048, 16], P('fsdp')
- decay_up_grad: float32 [16, 256], P(None, 'fsdp')
- decay_bias_grad: float32 [256], P('fsdp')
- swish_proj_grad: float32 [2048, 2048], P('fsdp')
- slot_gain_grad: float32 [2048], P('fsdp')
- out_proj_grad: float32 [2048, 2048], P('fsdp')
- mlp_gain_grad: float32 [2048], P('fsdp')
- mlp_gate_grad: float32 [2048, 5632], P('fsdp')
- mlp_up_grad: float32 [2048, 5632], P('fsdp')
- mlp_down_grad: float32 [5632, 2048], P('fsdp')
The draws below stay inside these ranges and needn't reach their ends.
Inputs may be any that keep to these rules, and one draw needn't show every extreme that they name: `seq_lengths`: rows of a sequence from its valid length on are padding; in every draw one sequence fills all 1024 positions and another has 512.
All inputs are finite; a program needn't handle non-finite values.
Results may differ from the reference program's by a relative error of at most 0.02.
Values may be sent and summed in bfloat16 or wider, within the bound.
No kernel may reach another device: no remote copies, remote signals or barrier semaphores. Data moves between devices by JAX's collectives and lax.ppermute only.
A program may use at most 512 MiB of HBM per device.

```python
import jax
import jax.numpy as jnp
from jax import lax

D = 2048
HEADS = 4
HEAD = 512
SLOTS = 64
FF = 5632
RANK = 16
GROUP = 64
LEN = 1024
SEQS = 8
TOKENS = 8192


def draw_seq_lengths(key, part):
    first_key, second_key = jax.random.split(key)
    levels = jax.random.randint(first_key, (SEQS,), 0, 32, dtype=jnp.int32)
    shortest = LEN // 2
    lengths_out = shortest + (LEN - shortest) * levels * levels // 961
    chosen = jax.random.randint(second_key, (), 0, SEQS, dtype=jnp.int32)
    places = jnp.arange(SEQS, dtype=jnp.int32)
    lengths_out = jnp.where(places == chosen, LEN, lengths_out)
    lengths_out = jnp.where(places == (chosen + 1) % SEQS, shortest, lengths_out)
    return lengths_out.astype(jnp.int32)


def shard_levels(own_key, shape, cuts, low, largest):
    def one(dim, blocks):
        draws = jax.random.uniform(jax.random.fold_in(jax.random.fold_in(own_key, 6), dim), (blocks,), jnp.float32, low / len(cuts), largest / len(cuts))
        return jnp.repeat(jnp.exp(draws), shape[dim] // blocks).reshape((-1,) + (1,) * (len(shape) - dim - 1))

    gain = one(*cuts[0])
    for cut in cuts[1:]:
        gain = gain * one(*cut)
    return gain


def bell_draw(own_key, shape, spread, bound, cuts=(), kind=jnp.bfloat16):
    gain = shard_levels(own_key, shape, cuts, -0.22, 0.18) if cuts else 1.0
    drawn = jax.random.normal(own_key, shape, jnp.float32) * spread * gain
    return jnp.minimum(jnp.maximum(drawn, -bound), bound).astype(kind)


def setup_inputs(seed: int = 0) -> dict:
    key_of = jax.random.split(jax.random.key(seed), 18)
    return {
        "tokens": bell_draw(key_of[0], (TOKENS, D), 1.0, 6.0, ((0, 32),)),
        "seq_lengths": draw_seq_lengths(jax.random.fold_in(key_of[17], 71), 0),
        "attn_gain": jnp.clip(1.0 + 0.1 * jax.random.normal(key_of[2], (D,), jnp.float32), 0.5, 1.5).astype(jnp.bfloat16),
        "query_proj": bell_draw(key_of[3], (D, D), D ** -0.5, 0.125, ((0, 8),)),
        "key_proj": bell_draw(key_of[4], (D, D), D ** -0.5, 0.125, ((0, 8),)),
        "value_proj": bell_draw(key_of[5], (D, D), D ** -0.5, 0.125, ((0, 8),)),
        "decay_down": bell_draw(key_of[6], (D, RANK), D ** -0.5, 0.125, ((0, 8),)),
        "decay_up": bell_draw(key_of[7], (RANK, HEADS * SLOTS), RANK ** -0.5, 1.5, ((1, 8),)),
        "decay_bias": jnp.clip(1.5 + 4.5 * jax.random.uniform(key_of[8], (HEADS * SLOTS,), jnp.float32) ** shard_levels(key_of[8], (HEADS * SLOTS,), ((0, 8),), -0.2, 0.2), 1.5, 6.0).astype(jnp.bfloat16),
        "swish_proj": bell_draw(key_of[9], (D, D), D ** -0.5, 0.125, ((0, 8),)),
        "slot_gain": jnp.clip(1.0 + 0.1 * jax.random.normal(key_of[10], (D,), jnp.float32), 0.5, 1.5).astype(jnp.bfloat16),
        "out_proj": bell_draw(key_of[11], (D, D), (D // 4) ** -0.5, 0.25, ((0, 8),)),
        "mlp_gain": jnp.clip(1.0 + 0.1 * jax.random.normal(key_of[12], (D,), jnp.float32), 0.5, 1.5).astype(jnp.bfloat16),
        "mlp_gate": bell_draw(key_of[13], (D, FF), D ** -0.5, 0.125, ((0, 8),)),
        "mlp_up": bell_draw(key_of[14], (D, FF), D ** -0.5, 0.125, ((0, 8),)),
        "mlp_down": bell_draw(key_of[15], (FF, D), FF ** -0.5, 0.078125, ((0, 8),)),
        "grad_out": bell_draw(key_of[16], (TOKENS, D), 1.0, 6.0, ((0, 32),)),
    }


EPSILON = 1e-06
NORMALIZER = 8.0
HIGHEST = lax.Precision.HIGHEST

@jax.custom_vjp
def low(v):
    return lax.optimization_barrier(v.astype(jnp.bfloat16)).astype(jnp.float32)

@jax.custom_vjp
def low_back(v):
    return v

def low_keep(v):
    return (low(v), None)

def low_pass(kept, grad):
    return (grad,)

def back_keep(v):
    return (v, None)

def back_low(kept, grad):
    return (low(grad),)
low.defvjp(low_keep, low_pass)
low_back.defvjp(back_keep, back_low)

def inverse_rms(values):
    return lax.rsqrt(lax.optimization_barrier(jnp.mean(values * values, axis=-1, keepdims=True)) + EPSILON)

def matmul(left_mat, right_mat):
    return jnp.dot(left_mat, right_mat, precision=HIGHEST, preferred_element_type=jnp.float32)

def decay_terms(forget, live_mask):
    log_sig = jax.nn.log_sigmoid(forget) / NORMALIZER
    mask_cube = live_mask[:, None, None]
    return (mask_cube * log_sig, mask_cube * -jnp.expm1(log_sig))

def to_blocks(array):
    return array.reshape((array.shape[0] // GROUP, GROUP) + array.shape[1:])

def advance_states(carried, block_pack):
    keys_now, values_now, log_now = carried
    block_keys, block_values, block_log, block_in = block_pack
    running = jnp.cumsum(block_log, axis=0)
    total_log = running[-1]
    weight = jnp.exp(total_log[None] - running) * block_in
    factor = jnp.exp(total_log)[..., None]
    keys_next = factor * keys_now + jnp.einsum('shj,she->hje', weight, block_keys, precision=HIGHEST)
    values_next = factor * values_now + jnp.einsum('shj,she->hje', weight, block_values, precision=HIGHEST)
    return ((keys_next, values_next, log_now + total_log), (keys_now, values_now, log_now))

def group_states(key_rows, value_rows, log_decay, inflow):
    zeros_state = jnp.zeros((key_rows.shape[1], log_decay.shape[2], key_rows.shape[2]), jnp.float32)
    start_carry = (zeros_state, zeros_state, jnp.zeros(log_decay.shape[1:], jnp.float32))
    final_state, starts = lax.scan(jax.checkpoint(advance_states), start_carry, (to_blocks(key_rows), to_blocks(value_rows), to_blocks(log_decay), to_blocks(inflow)))
    return (starts, final_state)

def attend_block(queries, key_rows, value_rows, log_decay, inflow, state_keys, state_values):
    positions = jnp.arange(queries.shape[0], dtype=jnp.int32)
    causal = (positions[:, None] >= positions[None, :]).astype(jnp.float32)
    running = jnp.cumsum(log_decay, axis=0)
    log_gap = running[:, None] - running[None, :]
    decay_tab = jnp.exp(jnp.minimum(log_gap, 0.0)) * causal[:, :, None, None]
    growth = jnp.exp(running)
    scale_dot = queries.shape[-1] ** (-0.5)
    qk_dots = jnp.einsum('the,she->tsh', queries, key_rows, precision=HIGHEST) * scale_dot
    within = jnp.einsum('tsh,tshj,shj->thj', qk_dots, decay_tab, inflow, precision=HIGHEST)
    across = jnp.einsum('hje,the->thj', state_keys, queries, precision=HIGHEST) * scale_dot * growth
    probs_slot = jax.nn.softmax(within + across, axis=-1)
    mix_weight = jnp.einsum('thj,tshj,shj->tsh', probs_slot, decay_tab, inflow, precision=HIGHEST)
    recent = jnp.einsum('tsh,she->the', mix_weight, value_rows, precision=HIGHEST)
    earlier_part = jnp.einsum('thj,hje->the', probs_slot * growth, state_values, precision=HIGHEST)
    return recent + earlier_part

def attend_pack(block_pack):
    return attend_block(*block_pack)

def attend_groups(queries, key_rows, value_rows, log_decay, inflow, start_keys, start_values, start_log, init_keys, init_values):
    factor = jnp.exp(start_log)[..., None]
    state_keys = factor * init_keys[None] + start_keys
    state_values = factor * init_values[None] + start_values
    outputs = lax.map(jax.checkpoint(attend_pack), (to_blocks(queries), to_blocks(key_rows), to_blocks(value_rows), to_blocks(log_decay), to_blocks(inflow), state_keys, state_values))
    return outputs.reshape(queries.shape)

def local_mixer(queries, key_rows, value_rows, forget, live_mask, init_keys, init_values):
    log_decay, inflow = decay_terms(forget, live_mask)
    starts, final_state = group_states(key_rows, value_rows, log_decay, inflow)
    return attend_groups(queries, key_rows, value_rows, log_decay, inflow, starts[0], starts[1], starts[2], init_keys, init_values)

def sequence_forward(params, seq_rows, length):
    attn_gain, query_proj, key_proj, value_proj, decay_down, decay_up, decay_bias, swish_proj, slot_gain, out_proj, mlp_gain, mlp_gate, mlp_up, mlp_down = params
    row_count = seq_rows.shape[0]
    live_mask = (jnp.arange(row_count, dtype=jnp.int32) < length).astype(jnp.float32)
    live_col = live_mask[:, None]
    normed = low(seq_rows * inverse_rms(seq_rows) * attn_gain)
    queries = low(low_back(matmul(normed, query_proj)))
    key_rows = low(low_back(matmul(normed, key_proj)))
    value_rows = low(low_back(matmul(normed, value_proj)))
    gate_low = low_back(matmul(normed, decay_down))
    forget = matmul(gate_low, decay_up) + decay_bias
    swish_pre = low_back(matmul(normed, swish_proj))
    zeros_state = jnp.zeros((HEADS, SLOTS, HEAD), jnp.float32)
    mixer_out = local_mixer(queries.reshape(row_count, HEADS, HEAD), key_rows.reshape(row_count, HEADS, HEAD), value_rows.reshape(row_count, HEADS, HEAD), forget.reshape(row_count, HEADS, SLOTS), live_mask, zeros_state, zeros_state)
    hat_out = (mixer_out * inverse_rms(mixer_out)).reshape(row_count, HEADS * HEAD)
    gated_rows = low(hat_out * slot_gain * jax.nn.silu(swish_pre))
    attn_out = low_back(matmul(gated_rows, out_proj))
    residual = seq_rows + live_col * attn_out
    normed_two = low(residual * inverse_rms(residual) * mlp_gain)
    gate_pre = low_back(matmul(normed_two, mlp_gate))
    up_pre = low_back(matmul(normed_two, mlp_up))
    hidden_act = low(jax.nn.silu(gate_pre) * up_pre)
    mlp_out = low_back(matmul(hidden_act, mlp_down))
    return residual + live_col * mlp_out

def reference(tokens, seq_lengths, attn_gain, query_proj, key_proj, value_proj, decay_down, decay_up, decay_bias, swish_proj, slot_gain, out_proj, mlp_gain, mlp_gate, mlp_up, mlp_down, grad_out):
    params = tuple((weight.astype(jnp.float32) for weight in (attn_gain, query_proj, key_proj, value_proj, decay_down, decay_up, decay_bias, swish_proj, slot_gain, out_proj, mlp_gain, mlp_gate, mlp_up, mlp_down)))
    inputs = tokens.astype(jnp.float32).reshape(SEQS, LEN, D)

    def forward(weights_in, rows_in):

        def one_sequence(seq_item):
            return sequence_forward(weights_in, seq_item[0], seq_item[1])
        return lax.map(jax.checkpoint(one_sequence), (rows_in, seq_lengths))
    result, pullback = jax.vjp(forward, params, inputs)
    weight_grads, input_grads = pullback(grad_out.astype(jnp.float32).reshape(SEQS, LEN, D))
    return (result.reshape(TOKENS, D).astype(jnp.bfloat16), input_grads.reshape(TOKENS, D).astype(jnp.bfloat16), weight_grads[0], weight_grads[1], weight_grads[2], weight_grads[3], weight_grads[4], weight_grads[5], weight_grads[6], weight_grads[7], weight_grads[8], weight_grads[9], weight_grads[10], weight_grads[11], weight_grads[12], weight_grads[13])
```

```python
import functools
import jax
import jax.numpy as jnp
from jax import lax
from jax.experimental import pallas as pl
from jax.experimental.pallas import tpu as pltpu
from jax.sharding import Mesh, PartitionSpec as P

HEAD = 512
SLOTS = 64
SCALE = HEAD ** (-0.5)
EPSILON = 1e-06
HIGHEST = lax.Precision.HIGHEST
BF = jnp.bfloat16
F32 = jnp.float32


def mm(a, b):
    return lax.dot_general(a, b, (((1,), (0,)), ((), ())), preferred_element_type=F32)


def mm_nt(a, b):
    return lax.dot_general(a, b, (((1,), (1,)), ((), ())), preferred_element_type=F32)


def mm_tn(a, b):
    return lax.dot_general(a, b, (((0,), (0,)), ((), ())), preferred_element_type=F32)


def exact(a, b):
    return lax.dot_general(
        a, b, (((1,), (0,)), ((), ())), precision=HIGHEST, preferred_element_type=F32
    )


def row_bit(rows, level):
    t = lax.broadcasted_iota(jnp.int32, (rows, SLOTS), 0)
    return ((t >> level) & 1) == 1


def prefix_levels(log_decay):
    rows = log_decay.shape[0]
    levels = rows.bit_length() - 1
    f, g = log_decay, jnp.zeros_like(log_decay)
    out = []
    for level in range(levels):
        out.append((f, g))
        total = f + g
        step = 1 << level
        bit = row_bit(rows, level)
        f = f + jnp.where(bit, pltpu.roll(total, step, 0), 0.0)
        g = g + jnp.where(bit, 0.0, pltpu.roll(total, rows - step, 0))
    return out, f, g


def same_block(rows, level):
    t = lax.broadcasted_iota(jnp.int32, (rows, rows), 0)
    s = lax.broadcasted_iota(jnp.int32, (rows, rows), 1)
    return (t >> (level + 1)) == (s >> (level + 1))


def level_mask(table, level, levels):
    if level == levels - 1:
        return table
    return jnp.where(same_block(table.shape[0], level), table, jnp.zeros_like(table))


def factors(pair, level, inflow):
    f, g = pair
    bit = row_bit(f.shape[0], level)
    left = jnp.where(bit, jnp.exp(f), 0.0)
    right = jnp.where(bit, 0.0, jnp.exp(g))
    return left, right, right * inflow


def diagonal(rows):
    t = lax.broadcasted_iota(jnp.int32, (rows, rows), 0)
    s = lax.broadcasted_iota(jnp.int32, (rows, rows), 1)
    return t == s


def slot_table(weights, pairs, inflow):
    rows = weights.shape[0]
    levels = len(pairs)
    table = jnp.where(diagonal(rows), jnp.sum(weights * inflow, axis=1, keepdims=True), 0.0)
    for level in range(levels):
        left, _, gain = factors(pairs[level], level, inflow)
        block = mm_nt((weights * left).astype(BF), gain.astype(BF))
        table = table + level_mask(block, level, levels)
    return table


def slot_sums(table, pairs, inflow):
    rows = table.shape[0]
    levels = len(pairs)
    own = jnp.sum(jnp.where(diagonal(rows), table, 0.0), axis=1, keepdims=True)
    low = table.astype(BF)
    total = own * inflow
    for level in range(levels):
        left, _, gain = factors(pairs[level], level, inflow)
        total = total + left * mm(level_mask(low, level, levels), gain.astype(BF))
    return total


def states_kernel(kv_ref, li_ref, state_ref, decay_ref):
    kv = kv_ref[0]
    log_decay = li_ref[0, :, :SLOTS]
    inflow = li_ref[0, :, SLOTS:]
    rows = kv.shape[0]
    t = lax.broadcasted_iota(jnp.int32, (rows, rows), 0)
    s = lax.broadcasted_iota(jnp.int32, (rows, rows), 1)
    after = exact((s > t).astype(F32), log_decay)
    weight = jnp.exp(after) * inflow
    state_ref[0] = mm_tn(weight.astype(BF), kv)
    total = lax.dot_general(
        log_decay, jnp.ones((rows, 128), F32), (((0,), (0,)), ((), ())),
        precision=HIGHEST, preferred_element_type=F32,
    )
    decay_ref[0] = jnp.exp(total)


def forward_kernel(qs_ref, kv_ref, li_ref, init_ref, gain_ref, gated_ref, out_ref, prob_ref, mix_ref):
    queries = qs_ref[0, :, :HEAD].astype(BF)
    swish = qs_ref[0, :, HEAD:]
    keys = kv_ref[0, :, :HEAD]
    values = kv_ref[0, :, HEAD:]
    log_decay = li_ref[0, :, :SLOTS]
    inflow = li_ref[0, :, SLOTS:]
    init = init_ref[0].astype(BF)
    pairs, running, _ = prefix_levels(log_decay)
    growth = jnp.exp(running)
    scores = mm_nt(queries, keys) * SCALE
    slots = slot_sums(scores, pairs, inflow) + mm_nt(queries, init[:, :HEAD]) * SCALE * growth
    top = jnp.max(slots, axis=1, keepdims=True)
    weights = jnp.exp(slots - top)
    probs = weights / jnp.sum(weights, axis=1, keepdims=True)
    mix = slot_table(probs, pairs, inflow).astype(BF)
    out = mm(mix, values) + mm((probs * growth).astype(BF), init[:, HEAD:])
    hat = out * lax.rsqrt(jnp.mean(out * out, axis=1, keepdims=True) + EPSILON)
    gated_ref[0] = (hat * gain_ref[0:1] * (swish * jax.nn.sigmoid(swish))).astype(BF)
    out_ref[0] = out
    prob_ref[0] = probs
    mix_ref[0] = mix


def backward_kernel(
    qs_ref, kv_ref, li_ref, init_ref, gain_ref, out_ref, prob_ref, mix_ref, gg_ref,
    dqs_ref, dkv_ref, ddi_ref, adj_ref, sg_ref,
):
    queries = qs_ref[0, :, :HEAD].astype(BF)
    swish = qs_ref[0, :, HEAD:]
    keys = kv_ref[0, :, :HEAD]
    values = kv_ref[0, :, HEAD:]
    log_decay = li_ref[0, :, :SLOTS]
    inflow = li_ref[0, :, SLOTS:]
    init = init_ref[0].astype(BF)
    out = out_ref[0]
    probs = prob_ref[0]
    gain = gain_ref[0:1]
    rows = out.shape[0]
    scale_out = lax.rsqrt(jnp.mean(out * out, axis=1, keepdims=True) + EPSILON)
    hat = out * scale_out
    sig = jax.nn.sigmoid(swish)
    silu = swish * sig
    gg = gg_ref[0].astype(F32)
    gg_hat = gg * hat
    dqs_ref[0, :, HEAD:] = (gg_hat * gain * (sig * (1.0 + swish * (1.0 - sig)))).astype(BF)
    part = jnp.broadcast_to(jnp.sum(gg_hat * silu, axis=0, keepdims=True), (8, HEAD))

    @pl.when(pl.program_id(0) == 0)
    def _():
        sg_ref[...] = part

    @pl.when(pl.program_id(0) > 0)
    def _():
        sg_ref[...] = sg_ref[...] + part

    grad_hat = gg * gain * silu
    dout = scale_out * (grad_hat - hat * jnp.mean(grad_hat * hat, axis=1, keepdims=True))
    dout = dout.astype(BF)
    pairs, running, _ = prefix_levels(log_decay)
    levels = len(pairs)
    growth = jnp.exp(running)
    scores = mm_nt(queries, keys) * SCALE
    grads = mm_nt(dout, values)
    key_part = mm_nt(queries, init[:, :HEAD]) * SCALE * growth
    value_part = mm_nt(dout, init[:, HEAD:]) * growth
    dprob = slot_sums(grads, pairs, inflow) + value_part
    dslot = probs * (dprob - jnp.sum(probs * dprob, axis=1, keepdims=True))
    back = slot_table(dslot, pairs, inflow).astype(BF)
    dslot_g = (dslot * growth).astype(BF)
    prob_g = (probs * growth).astype(BF)
    dqs_ref[0, :, :HEAD] = (SCALE * (mm(back, keys) + mm(dslot_g, init[:, :HEAD]))).astype(BF)
    dkv_ref[0, :, :HEAD] = SCALE * mm_tn(back, queries)
    dkv_ref[0, :, HEAD:] = mm_tn(mix_ref[0], dout)
    adj_ref[0, :, :HEAD] = SCALE * mm_tn(dslot_g, queries)
    adj_ref[0, :, HEAD:] = mm_tn(prob_g, dout)
    diag = diagonal(rows)
    own_a = jnp.sum(jnp.where(diag, scores, 0.0), axis=1, keepdims=True)
    own_b = jnp.sum(jnp.where(diag, grads, 0.0), axis=1, keepdims=True)
    dinflow = dslot * own_a + probs * own_b
    scores_low = scores.astype(BF)
    grads_low = grads.astype(BF)
    fbar = dslot * key_part + probs * value_part
    gbar = jnp.zeros_like(fbar)
    for level in range(levels - 1, -1, -1):
        left, right, amount = factors(pairs[level], level, inflow)
        table_a = level_mask(scores_low, level, levels)
        table_b = level_mask(grads_low, level, levels)
        amount_low = amount.astype(BF)
        dleft = dslot * left
        pleft = probs * left
        grow = dleft * mm(table_a, amount_low) + pleft * mm(table_b, amount_low)
        back_in = mm_tn(table_a, dleft.astype(BF)) + mm_tn(table_b, pleft.astype(BF))
        dinflow = dinflow + right * back_in
        step = 1 << level
        bit = row_bit(rows, level)
        total = pltpu.roll(jnp.where(bit, fbar, 0.0), rows - step, 0) + pltpu.roll(
            jnp.where(bit, 0.0, gbar), step, 0
        )
        fbar = fbar + grow + total
        gbar = gbar + amount * back_in + total
    ddi_ref[0, :, :SLOTS] = fbar
    ddi_ref[0, :, SLOTS:] = dinflow


def finish_kernel(kv_ref, li_ref, init_ref, end_ref, dkv_ref, ddi_ref, okv_ref, oddi_ref):
    kv = kv_ref[0]
    log_decay = li_ref[0, :, :SLOTS]
    inflow = li_ref[0, :, SLOTS:]
    end = end_ref[0]
    rows = kv.shape[0]
    t = lax.broadcasted_iota(jnp.int32, (rows, rows), 0)
    s = lax.broadcasted_iota(jnp.int32, (rows, rows), 1)
    earlier = (s < t).astype(F32)
    after = exact((s > t).astype(F32), log_decay)
    fade = jnp.exp(after)
    weight = fade * inflow
    end_low = end.astype(BF)
    okv_ref[0] = (dkv_ref[0] + mm(weight.astype(BF), end_low)).astype(BF)
    reach = mm_nt(kv, end_low)
    whole = jnp.exp(jnp.sum(log_decay, axis=0, keepdims=True))
    carry = lax.dot_general(
        jnp.ones((8, 2 * HEAD), F32), end * init_ref[0], (((1,), (1,)), ((), ())),
        precision=HIGHEST, preferred_element_type=F32,
    )[0:1]
    oddi_ref[0, :, :SLOTS] = (
        ddi_ref[0, :, :SLOTS] + exact(earlier, weight * reach) + whole * carry
    )
    oddi_ref[0, :, SLOTS:] = ddi_ref[0, :, SLOTS:] + fade * reach


def blocked(shape):
    return pl.BlockSpec((1,) + shape, lambda i: (i, 0, 0))


def run(kernel, args, specs, outs, out_specs, flops, moved):
    return pl.pallas_call(
        kernel,
        grid=(args[0].shape[0],),
        in_specs=specs,
        out_specs=out_specs,
        out_shape=outs,
        cost_estimate=pl.CostEstimate(flops=flops, bytes_accessed=moved, transcendentals=0),
        compiler_params=pltpu.CompilerParams(vmem_limit_bytes=56 << 20),
    )(*args)


def sds(shape, dtype=F32):
    return jax.ShapeDtypeStruct(shape, dtype)


def chunk_states(kv, li):
    n, rows, _ = kv.shape
    return run(
        states_kernel, (kv, li),
        [blocked((rows, 2 * HEAD)), blocked((rows, 2 * SLOTS))],
        (sds((n, SLOTS, 2 * HEAD)), sds((n, SLOTS, 128))),
        (blocked((SLOTS, 2 * HEAD)), blocked((SLOTS, 128))),
        n * 10**9, n * 10**6,
    )


def mixer_forward(qs, kv, li, init, gain):
    n, rows, _ = kv.shape
    return run(
        forward_kernel, (qs, kv, li, init, gain),
        [blocked((rows, 2 * HEAD)), blocked((rows, 2 * HEAD)), blocked((rows, 2 * SLOTS)),
         blocked((SLOTS, 2 * HEAD)), pl.BlockSpec((8, HEAD), lambda i: (0, 0))],
        (sds((n, rows, HEAD), BF), sds((n, rows, HEAD)), sds((n, rows, SLOTS)), sds((n, rows, rows), BF)),
        (blocked((rows, HEAD)), blocked((rows, HEAD)), blocked((rows, SLOTS)), blocked((rows, rows))),
        n * 3 * 10**9, n * 4 * 10**6,
    )


def mixer_backward(qs, kv, li, init, gain, out, probs, mix, gg):
    n, rows, _ = kv.shape
    return run(
        backward_kernel, (qs, kv, li, init, gain, out, probs, mix, gg),
        [blocked((rows, 2 * HEAD)), blocked((rows, 2 * HEAD)), blocked((rows, 2 * SLOTS)),
         blocked((SLOTS, 2 * HEAD)), pl.BlockSpec((8, HEAD), lambda i: (0, 0)),
         blocked((rows, HEAD)), blocked((rows, SLOTS)), blocked((rows, rows)), blocked((rows, HEAD))],
        (sds((n, rows, 2 * HEAD), BF), sds((n, rows, 2 * HEAD)), sds((n, rows, 2 * SLOTS)),
         sds((n, SLOTS, 2 * HEAD)), sds((8, HEAD))),
        (blocked((rows, 2 * HEAD)), blocked((rows, 2 * HEAD)), blocked((rows, 2 * SLOTS)),
         blocked((SLOTS, 2 * HEAD)), pl.BlockSpec((8, HEAD), lambda i: (0, 0))),
        n * 6 * 10**9, n * 5 * 10**6,
    )


def mixer_finish(kv, li, init, end, dkv, ddi):
    n, rows, _ = kv.shape
    return run(
        finish_kernel, (kv, li, init, end, dkv, ddi),
        [blocked((rows, 2 * HEAD)), blocked((rows, 2 * SLOTS)), blocked((SLOTS, 2 * HEAD)),
         blocked((SLOTS, 2 * HEAD)), blocked((rows, 2 * HEAD)), blocked((rows, 2 * SLOTS))],
        (sds((n, rows, 2 * HEAD), BF), sds((n, rows, 2 * SLOTS))),
        (blocked((rows, 2 * HEAD)), blocked((rows, 2 * SLOTS))),
        n * 10**9, n * 3 * 10**6,
    )


D = 2048
HEADS = 4
RANK = 16
NORMALIZER = 8.0


def inverse_rms(values):
    return lax.rsqrt(jnp.mean(values * values, axis=-1, keepdims=True) + EPSILON)


def silu_slope(values):
    sigmoid_val = jax.nn.sigmoid(values)
    return sigmoid_val * (1.0 + values * (1.0 - sigmoid_val))


def norm_back(grad_hat, hat_rows, scale_rows):
    return scale_rows * (
        grad_hat - hat_rows * jnp.mean(grad_hat * hat_rows, axis=-1, keepdims=True)
    )


def swap(value, axis, step):
    count = lax.axis_size(axis)
    return lax.ppermute(value, axis, [(i, i ^ step) for i in range(count)])


def gather_heads(block):
    return [block] + [swap(block, "p", k) for k in range(1, HEADS)]


def scatter_heads(parts):
    total = parts[0].astype(F32)
    for k in range(1, HEADS):
        total = total + swap(parts[k], "p", k).astype(F32)
    return total


def after(value, *others):
    return lax.optimization_barrier((value,) + others)[0]


def head_columns(shards, here):
    width = [shard.shape[1] // HEADS for shard in shards]
    rows = shards[0].shape[0]
    copies = lax.axis_size("r")
    turn = lax.axis_index("r")
    pieces = []
    for k in range(HEADS):
        cut = jnp.concatenate(
            [
                lax.dynamic_slice_in_dim(shard, (here ^ k) * w, w, 1)
                for shard, w in zip(shards, width)
            ],
            axis=1,
        )
        pieces.append(cut if k == 0 else swap(cut, "p", k))
    whole = jnp.zeros((HEADS * copies * rows, sum(width)), BF)
    for k in range(HEADS):
        for m in range(copies):
            piece = pieces[k] if m == 0 else swap(pieces[k], "r", m)
            start = ((here ^ k) * copies + (turn ^ m)) * rows
            whole = lax.dynamic_update_slice_in_dim(whole, piece, start, 0)
    return whole, pieces


def chain(state, decay, forward):
    count = lax.axis_size("seq")
    total = jnp.zeros_like(state)
    for hop in range(count - 1):
        pair = (hop, hop + 1) if forward else (count - 1 - hop, count - 2 - hop)
        sent = (decay * total + state).astype(BF)
        total = total + lax.ppermute(sent, "seq", [pair]).astype(F32)
    return total


def chain_pair(both, decay, forward):
    return jnp.concatenate(
        [chain(both[..., :HEAD], decay, forward), chain(both[..., HEAD:], decay, forward)], axis=-1
    )


def split_rows(left, here, step):
    return lax.dynamic_index_in_dim(left, here ^ step, 2, False).reshape(left.shape[0], -1)


def reduce_copies(parts):
    total = parts[0]
    for m in range(1, len(parts)):
        total = total + swap(parts[m].astype(BF), "r", m).astype(F32)
    return total


def reduce_seq(value):
    count = lax.axis_size("seq")
    place = lax.axis_index("seq")
    step = 1
    while step < count:
        half = value.shape[1] // 2
        bit = (place // step) % 2
        away = lax.dynamic_slice_in_dim(value, (1 - bit) * half, half, 1)
        kept = lax.dynamic_slice_in_dim(value, bit * half, half, 1)
        value = kept.astype(F32) + swap(away.astype(BF), "seq", step).astype(F32)
        step *= 2
    return value.astype(BF)


def gather_seq(value):
    count = lax.axis_size("seq")
    found = {0: value}
    step = count // 2
    while step >= 1:
        for j in list(found):
            found[j ^ step] = swap(found[j], "seq", step)
        step //= 2
    return [found[j] for j in range(count)]


def row_starts(rows):
    count = lax.axis_size("seq")
    place = lax.axis_index("seq")
    starts = []
    for j in range(count):
        other = place ^ j
        start, half, step = 0, rows // 2, 1
        while step < count:
            start = start + ((other // step) % 2) * half
            half //= 2
            step *= 2
        starts.append(start)
    return starts


def assemble_kernel(counts, spot_ref, *refs):
    n_in, n_out, part = counts
    ins, outs = refs[:n_in], refs[n_in:]
    width = outs[0].shape[1]
    for j in range(n_in):
        start = pl.multiple_of(spot_ref[j] * part, part)
        for o in range(n_out):
            outs[o][pl.ds(start, part), :] = ins[j][0, :, o * width : (o + 1) * width].astype(F32)


def assemble(parts, columns, n_out, starts):
    blocks, part, width = parts[0].shape
    width //= n_out
    rows = part * len(parts)
    if part % 16:
        outs = []
        for o in range(n_out):
            whole = jnp.zeros((rows, blocks * width), F32)
            for j, value in enumerate(parts):
                for i in range(blocks):
                    cut = value[i, :, o * width : (o + 1) * width].astype(F32)
                    whole = lax.dynamic_update_slice(whole, cut, (starts[j], columns[i] * width))
            outs.append(whole)
        return outs
    spots = jnp.stack(
        [jnp.asarray(s // part, jnp.int32) for s in starts]
        + [jnp.asarray(c, jnp.int32) for c in columns]
    )
    n_in = len(parts)
    return pl.pallas_call(
        functools.partial(assemble_kernel, (n_in, n_out, part)),
        grid_spec=pltpu.PrefetchScalarGridSpec(
            num_scalar_prefetch=1,
            grid=(blocks,),
            in_specs=[pl.BlockSpec((1, part, n_out * width), lambda i, s: (i, 0, 0))] * n_in,
            out_specs=[pl.BlockSpec((rows, width), lambda i, s: (0, s[n_in + i]))] * n_out,
        ),
        out_shape=[jax.ShapeDtypeStruct((rows, blocks * width), F32)] * n_out,
        cost_estimate=pl.CostEstimate(
            flops=0, bytes_accessed=6 * n_out * rows * blocks * width, transcendentals=0
        ),
        compiler_params=pltpu.CompilerParams(vmem_limit_bytes=56 << 20),
    )(spots, *parts)


def finish_columns(total, here, n_out):
    rows = total.shape[1]
    part = reduce_seq(total)
    mine = [lax.dynamic_index_in_dim(part, here ^ k, 0, False) for k in range(HEADS)]
    got = jnp.stack([mine[0]] + [swap(mine[k], "p", k) for k in range(1, HEADS)])
    return assemble(gather_seq(got), [here ^ k for k in range(HEADS)], n_out, row_starts(rows))


def finish_rows(total):
    rows = total.shape[0]
    parts = [value for value in gather_seq(reduce_seq(total[None]))]
    return assemble(parts, [0], 1, row_starts(rows))[0]


def body(
    tokens,
    seq_lengths,
    attn_gain,
    query_proj,
    key_proj,
    value_proj,
    decay_down,
    decay_up,
    decay_bias,
    swish_proj,
    slot_gain,
    out_proj,
    mlp_gain,
    mlp_gate,
    mlp_up,
    mlp_down,
    grad_out,
):
    rows = tokens.shape[0]
    copies = lax.axis_size("r")
    owners = HEADS * copies
    shard = D // owners
    here, turn, place = lax.axis_index("p"), lax.axis_index("r"), lax.axis_index("seq")
    group = HEADS * rows

    small = [attn_gain, decay_down, decay_up, decay_bias, slot_gain, mlp_gain, seq_lengths]
    packed = jnp.concatenate([a.astype(F32).reshape(-1) for a in small])
    packed = lax.all_gather(packed, ("p", "r"), axis=0)
    fields, offset = [], 0
    for a in small:
        fields.append(packed[:, offset : offset + a.size])
        offset += a.size
    gain_one = fields[0].reshape(D)
    down_full = fields[1].reshape(D, RANK).astype(BF)
    up_full = fields[2].reshape(owners, RANK, -1).transpose(1, 0, 2).reshape(RANK, HEADS * SLOTS)
    up_head = lax.dynamic_slice_in_dim(up_full, here * SLOTS, SLOTS, 1)
    bias_head = lax.dynamic_slice_in_dim(fields[3].reshape(HEADS * SLOTS), here * SLOTS, SLOTS, 0)
    gain_head = lax.dynamic_slice_in_dim(fields[4].reshape(D), here * HEAD, HEAD, 0)
    gain_head8 = jnp.broadcast_to(gain_head[None], (8, HEAD))
    gain_two = fields[5].reshape(D)
    lengths = fields[6].reshape(HEADS, copies)
    positions = (place * rows + jnp.arange(rows, dtype=jnp.int32)).astype(F32)
    masks = [
        (positions < lax.dynamic_index_in_dim(lengths, here ^ k, 0, False)[turn]).astype(F32)
        for k in range(HEADS)
    ]
    mask_all = jnp.concatenate(masks)[:, None]
    mask_own = masks[0][:, None]

    token_blocks = gather_heads(tokens)
    weight_kv, kv_pieces = head_columns([key_proj, value_proj], here)
    query_late = after(query_proj, *kv_pieces[1:])
    weight_qs, qs_pieces = head_columns([query_late, swish_proj], here)
    gate_late = after(mlp_gate, *qs_pieces[1:])
    weight_gu, _ = head_columns([gate_late, mlp_up], here)
    weight_out = lax.all_gather(out_proj, "r", axis=0, tiled=True)
    weight_down = lax.all_gather(mlp_down, "r", axis=0, tiled=True)

    tokens_all = jnp.concatenate(token_blocks).astype(F32)
    normed = (tokens_all * inverse_rms(tokens_all) * gain_one).astype(BF)
    kv = mm(normed, weight_kv).astype(BF).reshape(HEADS, rows, 2 * HEAD)
    gate_low = mm(normed, down_full)
    forget = exact(gate_low, up_head) + bias_head
    log_sig = jax.nn.log_sigmoid(forget) / NORMALIZER
    li = jnp.concatenate([mask_all * log_sig, mask_all * -jnp.expm1(log_sig)], axis=1)
    li = li.reshape(HEADS, rows, 2 * SLOTS)
    state, decay = chunk_states(kv, li)
    decay = decay[:, :, :1]
    init = chain_pair(state, decay, True)
    qs = mm(normed, weight_qs).reshape(HEADS, rows, 2 * HEAD)
    gated, mixer_out, probs, mix = mixer_forward(qs, kv, li, init, gain_head8)
    gated = gated.reshape(group, HEAD)
    attn_part = mm(gated, weight_out).astype(BF).reshape(HEADS, rows, D)
    attn_out = scatter_heads([attn_part[k] for k in range(HEADS)])

    tokens_f = tokens.astype(F32)
    residual = tokens_f + mask_own * attn_out
    scale_two = inverse_rms(residual)
    hat_two = residual * scale_two
    normed_two_own = (hat_two * gain_two).astype(BF)
    two_blocks = gather_heads(normed_two_own)
    normed_two = jnp.concatenate(two_blocks)
    grad_blocks = gather_heads(after(grad_out, *two_blocks[1:]))
    grad_mlp = (mask_all * jnp.concatenate(grad_blocks).astype(F32)).astype(BF)

    hidden_width = weight_down.shape[0]
    gate_up = mm(normed_two, weight_gu)
    gate_pre, up_pre = gate_up[:, :hidden_width], gate_up[:, hidden_width:]
    hidden = (jax.nn.silu(gate_pre) * up_pre).astype(BF)
    mlp_part = mm(hidden, weight_down).astype(BF).reshape(HEADS, rows, D)

    grad_act = mm_nt(grad_mlp, weight_down)
    grad_gate = (grad_act * up_pre * silu_slope(gate_pre)).astype(BF)
    grad_up = (grad_act * jax.nn.silu(gate_pre)).astype(BF)
    grad_gu = jnp.concatenate([grad_gate, grad_up], axis=1)
    two_part = mm_nt(grad_gu, weight_gu).astype(BF).reshape(HEADS, rows, D)
    grad_norm_two = scatter_heads([two_part[k] for k in range(HEADS)])
    gain_two_grad = jnp.sum(grad_norm_two * hat_two, axis=0)
    grad_rows = grad_out.astype(F32)
    grad_resid = grad_rows + norm_back(grad_norm_two * gain_two, hat_two, scale_two)
    grad_attn_own = (mask_own * grad_resid).astype(BF)
    attn_blocks = gather_heads(grad_attn_own)
    grad_attn = jnp.concatenate(attn_blocks)

    mlp_out = scatter_heads([mlp_part[k] for k in range(HEADS)])
    result = (residual + mask_own * mlp_out).astype(BF)

    two_view = normed_two.reshape(group, HEADS, copies, shard)
    gu_parts = [mm_tn(split_rows(two_view, turn, m), grad_gu) for m in range(copies)]
    gu_total = reduce_copies(gu_parts).reshape(HEADS, shard, 2 * hidden_width)
    down_part = mm_tn(hidden, grad_mlp)
    down_rows = mlp_down.shape[0]
    down_total = reduce_copies(
        [
            lax.dynamic_slice_in_dim(down_part, (turn ^ m) * down_rows, down_rows, 0)
            for m in range(copies)
        ]
    )
    gate_grad, up_grad = finish_columns(gu_total, here, 2)
    down_grad = finish_rows(down_total)

    grad_gated = mm_nt(grad_attn, weight_out).reshape(HEADS, rows, HEAD)
    grad_qs, grad_kv, grad_li, adjoint, slot_part = mixer_backward(
        qs, kv, li, init, gain_head8, mixer_out, probs, mix, grad_gated
    )
    ends = chain_pair(adjoint, decay, False)
    grad_kv, grad_li = mixer_finish(kv, li, init, ends, grad_kv, grad_li)
    grad_qs = grad_qs.reshape(group, 2 * HEAD)
    grad_kv = grad_kv.reshape(group, 2 * HEAD)
    grad_li = grad_li.reshape(group, 2 * SLOTS)
    grad_decay = (
        mask_all
        * (grad_li[:, :SLOTS] - grad_li[:, SLOTS:] * jnp.exp(log_sig))
        / NORMALIZER
        * jax.nn.sigmoid(-forget)
    )
    bias_part = jnp.sum(grad_decay, axis=0)
    up_part = lax.dot_general(
        gate_low, grad_decay, (((0,), (0,)), ((), ())), precision=HIGHEST, preferred_element_type=F32
    )
    grad_low = lax.dot_general(
        grad_decay, up_head, (((1,), (1,)), ((), ())), precision=HIGHEST, preferred_element_type=F32
    ).astype(BF)
    down_low_part = mm_tn(normed, grad_low)

    one_part = (
        (mm_nt(grad_qs, weight_qs) + mm_nt(grad_kv, weight_kv) + mm_nt(grad_low, down_full))
        .astype(BF)
        .reshape(HEADS, rows, D)
    )
    grad_norm_one = scatter_heads([one_part[k] for k in range(HEADS)])
    scale_one = inverse_rms(tokens_f)
    hat_one = tokens_f * scale_one
    gain_one_grad = jnp.sum(grad_norm_one * hat_one, axis=0)
    grad_tokens = (grad_resid + norm_back(grad_norm_one * gain_one, hat_one, scale_one)).astype(BF)

    one_view = normed.reshape(group, HEADS, copies, shard)
    one_views = [split_rows(one_view, turn, m) for m in range(copies)]
    qs_total = reduce_copies([mm_tn(v, grad_qs) for v in one_views])
    kv_total = reduce_copies([mm_tn(v, grad_kv) for v in one_views])
    out_view = gated.reshape(group, 1, copies, shard)
    out_total = reduce_copies([mm_tn(split_rows(out_view, turn, m), grad_attn) for m in range(copies)])
    query_grad, swish_grad = finish_columns(qs_total.reshape(HEADS, shard, 2 * HEAD), here, 2)
    key_grad, value_grad = finish_columns(kv_total.reshape(HEADS, shard, 2 * HEAD), here, 2)
    out_grad = finish_rows(out_total)

    def placed(part, width):
        whole = jnp.zeros(part.shape[:-1] + (HEADS * width,), F32)
        return lax.dynamic_update_slice_in_dim(whole, part, here * width, part.ndim - 1)

    sums = [
        gain_one_grad,
        down_low_part,
        placed(up_part, SLOTS),
        placed(bias_part, SLOTS),
        placed(slot_part[0], HEAD),
        gain_two_grad,
    ]
    flat = jnp.concatenate([a.reshape(-1) for a in sums]).astype(BF)
    flat = lax.psum(flat, ("p", "r", "seq")).astype(F32)
    totals, offset = [], 0
    for a in sums:
        totals.append(flat[offset : offset + a.size].reshape(a.shape))
        offset += a.size
    owner = here * copies + turn

    def own(whole, axis):
        size = whole.shape[axis] // owners
        return lax.dynamic_slice_in_dim(whole, owner * size, size, axis)

    return (
        result,
        grad_tokens,
        own(totals[0], 0),
        query_grad,
        key_grad,
        value_grad,
        own(totals[1], 0),
        own(totals[2], 1),
        own(totals[3], 0),
        swish_grad,
        own(totals[4], 0),
        out_grad,
        own(totals[5], 0),
        gate_grad,
        up_grad,
        down_grad,
    )


def solution(mesh):
    count, span = mesh.devices.shape
    split = Mesh(mesh.devices.reshape(HEADS, count // HEADS, span), ("p", "r", "seq"))
    rows = P(("p", "r", "seq"), None)
    matrix, vector, last = P(("p", "r"), None), P(("p", "r")), P(None, ("p", "r"))
    in_specs = (
        rows, vector, vector, matrix, matrix, matrix, matrix, last, vector, matrix, vector, matrix,
        vector, matrix, matrix, matrix, rows,
    )
    out_specs = (
        rows, rows, vector, matrix, matrix, matrix, matrix, last, vector, matrix, vector, matrix,
        vector, matrix, matrix, matrix,
    )
    return jax.shard_map(body, mesh=split, in_specs=in_specs, out_specs=out_specs, check_vma=False)
```

```python
import functools
import jax
import jax.numpy as jnp
from jax import lax
from jax.experimental import pallas as pl
from jax.experimental.pallas import tpu as pltpu
from jax.sharding import Mesh, PartitionSpec as P

HEAD = 512
SLOTS = 64
SCALE = HEAD ** (-0.5)
EPSILON = 1e-06
HIGHEST = lax.Precision.HIGHEST
BF = jnp.bfloat16
F32 = jnp.float32


def mm(a, b):
    return lax.dot_general(a, b, (((1,), (0,)), ((), ())), preferred_element_type=F32)


def mm_nt(a, b):
    return lax.dot_general(a, b, (((1,), (1,)), ((), ())), preferred_element_type=F32)


def mm_tn(a, b):
    return lax.dot_general(a, b, (((0,), (0,)), ((), ())), preferred_element_type=F32)


def exact(a, b):
    return lax.dot_general(
        a, b, (((1,), (0,)), ((), ())), precision=HIGHEST, preferred_element_type=F32
    )


def row_bit(rows, level):
    t = lax.broadcasted_iota(jnp.int32, (rows, SLOTS), 0)
    return ((t >> level) & 1) == 1


def prefix_levels(log_decay):
    rows = log_decay.shape[0]
    levels = rows.bit_length() - 1
    f, g = log_decay, jnp.zeros_like(log_decay)
    out = []
    for level in range(levels):
        out.append((f, g))
        total = f + g
        step = 1 << level
        bit = row_bit(rows, level)
        f = f + jnp.where(bit, pltpu.roll(total, step, 0), 0.0)
        g = g + jnp.where(bit, 0.0, pltpu.roll(total, rows - step, 0))
    return out, f, g


def same_block(rows, level):
    t = lax.broadcasted_iota(jnp.int32, (rows, rows), 0)
    s = lax.broadcasted_iota(jnp.int32, (rows, rows), 1)
    return (t >> (level + 1)) == (s >> (level + 1))


def level_mask(table, level, levels):
    if level == levels - 1:
        return table
    return jnp.where(same_block(table.shape[0], level), table, jnp.zeros_like(table))


def factors(pair, level, inflow):
    f, g = pair
    bit = row_bit(f.shape[0], level)
    left = jnp.where(bit, jnp.exp(f), 0.0)
    right = jnp.where(bit, 0.0, jnp.exp(g))
    return left, right, right * inflow


def diagonal(rows):
    t = lax.broadcasted_iota(jnp.int32, (rows, rows), 0)
    s = lax.broadcasted_iota(jnp.int32, (rows, rows), 1)
    return t == s


def slot_table(weights, pairs, inflow):
    rows = weights.shape[0]
    levels = len(pairs)
    table = jnp.where(diagonal(rows), jnp.sum(weights * inflow, axis=1, keepdims=True), 0.0)
    for level in range(levels):
        left, _, gain = factors(pairs[level], level, inflow)
        block = mm_nt((weights * left).astype(BF), gain.astype(BF))
        table = table + level_mask(block, level, levels)
    return table


def slot_sums(table, pairs, inflow):
    rows = table.shape[0]
    levels = len(pairs)
    own = jnp.sum(jnp.where(diagonal(rows), table, 0.0), axis=1, keepdims=True)
    low = table.astype(BF)
    total = own * inflow
    for level in range(levels):
        left, _, gain = factors(pairs[level], level, inflow)
        total = total + left * mm(level_mask(low, level, levels), gain.astype(BF))
    return total


def states_kernel(kv_ref, li_ref, state_ref, decay_ref):
    kv = kv_ref[0]
    log_decay = li_ref[0, :, :SLOTS]
    inflow = li_ref[0, :, SLOTS:]
    rows = kv.shape[0]
    t = lax.broadcasted_iota(jnp.int32, (rows, rows), 0)
    s = lax.broadcasted_iota(jnp.int32, (rows, rows), 1)
    after = exact((s > t).astype(F32), log_decay)
    weight = jnp.exp(after) * inflow
    state_ref[0] = mm_tn(weight.astype(BF), kv)
    total = lax.dot_general(
        log_decay, jnp.ones((rows, 128), F32), (((0,), (0,)), ((), ())),
        precision=HIGHEST, preferred_element_type=F32,
    )
    decay_ref[0] = jnp.exp(total)


def forward_kernel(qs_ref, kv_ref, li_ref, init_ref, gain_ref, gated_ref, out_ref, prob_ref, mix_ref):
    queries = qs_ref[0, :, :HEAD].astype(BF)
    swish = qs_ref[0, :, HEAD:]
    keys = kv_ref[0, :, :HEAD]
    values = kv_ref[0, :, HEAD:]
    log_decay = li_ref[0, :, :SLOTS]
    inflow = li_ref[0, :, SLOTS:]
    init = init_ref[0].astype(BF)
    pairs, running, _ = prefix_levels(log_decay)
    growth = jnp.exp(running)
    scores = mm_nt(queries, keys) * SCALE
    slots = slot_sums(scores, pairs, inflow) + mm_nt(queries, init[:, :HEAD]) * SCALE * growth
    top = jnp.max(slots, axis=1, keepdims=True)
    weights = jnp.exp(slots - top)
    probs = weights / jnp.sum(weights, axis=1, keepdims=True)
    mix = slot_table(probs, pairs, inflow).astype(BF)
    out = mm(mix, values) + mm((probs * growth).astype(BF), init[:, HEAD:])
    hat = out * lax.rsqrt(jnp.mean(out * out, axis=1, keepdims=True) + EPSILON)
    gated_ref[0] = (hat * gain_ref[0:1] * (swish * jax.nn.sigmoid(swish))).astype(BF)
    out_ref[0] = out
    prob_ref[0] = probs
    mix_ref[0] = mix


def backward_kernel(
    qs_ref, kv_ref, li_ref, init_ref, gain_ref, out_ref, prob_ref, mix_ref, gg_ref,
    dqs_ref, dkv_ref, ddi_ref, adj_ref, sg_ref,
):
    queries = qs_ref[0, :, :HEAD].astype(BF)
    swish = qs_ref[0, :, HEAD:]
    keys = kv_ref[0, :, :HEAD]
    values = kv_ref[0, :, HEAD:]
    log_decay = li_ref[0, :, :SLOTS]
    inflow = li_ref[0, :, SLOTS:]
    init = init_ref[0].astype(BF)
    out = out_ref[0]
    probs = prob_ref[0]
    gain = gain_ref[0:1]
    rows = out.shape[0]
    scale_out = lax.rsqrt(jnp.mean(out * out, axis=1, keepdims=True) + EPSILON)
    hat = out * scale_out
    sig = jax.nn.sigmoid(swish)
    silu = swish * sig
    gg = gg_ref[0].astype(F32)
    gg_hat = gg * hat
    dqs_ref[0, :, HEAD:] = (gg_hat * gain * (sig * (1.0 + swish * (1.0 - sig)))).astype(BF)
    part = jnp.broadcast_to(jnp.sum(gg_hat * silu, axis=0, keepdims=True), (8, HEAD))

    @pl.when(pl.program_id(0) == 0)
    def _():
        sg_ref[...] = part

    @pl.when(pl.program_id(0) > 0)
    def _():
        sg_ref[...] = sg_ref[...] + part

    grad_hat = gg * gain * silu
    dout = scale_out * (grad_hat - hat * jnp.mean(grad_hat * hat, axis=1, keepdims=True))
    dout = dout.astype(BF)
    pairs, running, _ = prefix_levels(log_decay)
    levels = len(pairs)
    growth = jnp.exp(running)
    scores = mm_nt(queries, keys) * SCALE
    grads = mm_nt(dout, values)
    key_part = mm_nt(queries, init[:, :HEAD]) * SCALE * growth
    value_part = mm_nt(dout, init[:, HEAD:]) * growth
    dprob = slot_sums(grads, pairs, inflow) + value_part
    dslot = probs * (dprob - jnp.sum(probs * dprob, axis=1, keepdims=True))
    back = slot_table(dslot, pairs, inflow).astype(BF)
    dslot_g = (dslot * growth).astype(BF)
    prob_g = (probs * growth).astype(BF)
    dqs_ref[0, :, :HEAD] = (SCALE * (mm(back, keys) + mm(dslot_g, init[:, :HEAD]))).astype(BF)
    dkv_ref[0, :, :HEAD] = SCALE * mm_tn(back, queries)
    dkv_ref[0, :, HEAD:] = mm_tn(mix_ref[0], dout)
    adj_ref[0, :, :HEAD] = SCALE * mm_tn(dslot_g, queries)
    adj_ref[0, :, HEAD:] = mm_tn(prob_g, dout)
    diag = diagonal(rows)
    own_a = jnp.sum(jnp.where(diag, scores, 0.0), axis=1, keepdims=True)
    own_b = jnp.sum(jnp.where(diag, grads, 0.0), axis=1, keepdims=True)
    dinflow = dslot * own_a + probs * own_b
    scores_low = scores.astype(BF)
    grads_low = grads.astype(BF)
    fbar = dslot * key_part + probs * value_part
    gbar = jnp.zeros_like(fbar)
    for level in range(levels - 1, -1, -1):
        left, right, amount = factors(pairs[level], level, inflow)
        table_a = level_mask(scores_low, level, levels)
        table_b = level_mask(grads_low, level, levels)
        amount_low = amount.astype(BF)
        dleft = dslot * left
        pleft = probs * left
        grow = dleft * mm(table_a, amount_low) + pleft * mm(table_b, amount_low)
        back_in = mm_tn(table_a, dleft.astype(BF)) + mm_tn(table_b, pleft.astype(BF))
        dinflow = dinflow + right * back_in
        step = 1 << level
        bit = row_bit(rows, level)
        total = pltpu.roll(jnp.where(bit, fbar, 0.0), rows - step, 0) + pltpu.roll(
            jnp.where(bit, 0.0, gbar), step, 0
        )
        fbar = fbar + grow + total
        gbar = gbar + amount * back_in + total
    ddi_ref[0, :, :SLOTS] = fbar
    ddi_ref[0, :, SLOTS:] = dinflow


def finish_kernel(kv_ref, li_ref, init_ref, end_ref, dkv_ref, ddi_ref, okv_ref, oddi_ref):
    kv = kv_ref[0]
    log_decay = li_ref[0, :, :SLOTS]
    inflow = li_ref[0, :, SLOTS:]
    end = end_ref[0]
    rows = kv.shape[0]
    t = lax.broadcasted_iota(jnp.int32, (rows, rows), 0)
    s = lax.broadcasted_iota(jnp.int32, (rows, rows), 1)
    earlier = (s < t).astype(F32)
    after = exact((s > t).astype(F32), log_decay)
    fade = jnp.exp(after)
    weight = fade * inflow
    end_low = end.astype(BF)
    okv_ref[0] = (dkv_ref[0] + mm(weight.astype(BF), end_low)).astype(BF)
    reach = mm_nt(kv, end_low)
    whole = jnp.exp(jnp.sum(log_decay, axis=0, keepdims=True))
    carry = lax.dot_general(
        jnp.ones((8, 2 * HEAD), F32), end * init_ref[0], (((1,), (1,)), ((), ())),
        precision=HIGHEST, preferred_element_type=F32,
    )[0:1]
    oddi_ref[0, :, :SLOTS] = (
        ddi_ref[0, :, :SLOTS] + exact(earlier, weight * reach) + whole * carry
    )
    oddi_ref[0, :, SLOTS:] = ddi_ref[0, :, SLOTS:] + fade * reach


def blocked(shape):
    return pl.BlockSpec((1,) + shape, lambda i: (i, 0, 0))


def run(kernel, args, specs, outs, out_specs, flops, moved):
    return pl.pallas_call(
        kernel,
        grid=(args[0].shape[0],),
        in_specs=specs,
        out_specs=out_specs,
        out_shape=outs,
        cost_estimate=pl.CostEstimate(flops=flops, bytes_accessed=moved, transcendentals=0),
        compiler_params=pltpu.CompilerParams(vmem_limit_bytes=56 << 20),
    )(*args)


def sds(shape, dtype=F32):
    return jax.ShapeDtypeStruct(shape, dtype)


def chunk_states(kv, li):
    n, rows, _ = kv.shape
    return run(
        states_kernel, (kv, li),
        [blocked((rows, 2 * HEAD)), blocked((rows, 2 * SLOTS))],
        (sds((n, SLOTS, 2 * HEAD)), sds((n, SLOTS, 128))),
        (blocked((SLOTS, 2 * HEAD)), blocked((SLOTS, 128))),
        n * 10**9, n * 10**6,
    )


def mixer_forward(qs, kv, li, init, gain):
    n, rows, _ = kv.shape
    return run(
        forward_kernel, (qs, kv, li, init, gain),
        [blocked((rows, 2 * HEAD)), blocked((rows, 2 * HEAD)), blocked((rows, 2 * SLOTS)),
         blocked((SLOTS, 2 * HEAD)), pl.BlockSpec((8, HEAD), lambda i: (0, 0))],
        (sds((n, rows, HEAD), BF), sds((n, rows, HEAD)), sds((n, rows, SLOTS)), sds((n, rows, rows), BF)),
        (blocked((rows, HEAD)), blocked((rows, HEAD)), blocked((rows, SLOTS)), blocked((rows, rows))),
        n * 3 * 10**9, n * 4 * 10**6,
    )


def mixer_backward(qs, kv, li, init, gain, out, probs, mix, gg):
    n, rows, _ = kv.shape
    return run(
        backward_kernel, (qs, kv, li, init, gain, out, probs, mix, gg),
        [blocked((rows, 2 * HEAD)), blocked((rows, 2 * HEAD)), blocked((rows, 2 * SLOTS)),
         blocked((SLOTS, 2 * HEAD)), pl.BlockSpec((8, HEAD), lambda i: (0, 0)),
         blocked((rows, HEAD)), blocked((rows, SLOTS)), blocked((rows, rows)), blocked((rows, HEAD))],
        (sds((n, rows, 2 * HEAD), BF), sds((n, rows, 2 * HEAD)), sds((n, rows, 2 * SLOTS)),
         sds((n, SLOTS, 2 * HEAD)), sds((8, HEAD))),
        (blocked((rows, 2 * HEAD)), blocked((rows, 2 * HEAD)), blocked((rows, 2 * SLOTS)),
         blocked((SLOTS, 2 * HEAD)), pl.BlockSpec((8, HEAD), lambda i: (0, 0))),
        n * 6 * 10**9, n * 5 * 10**6,
    )


def mixer_finish(kv, li, init, end, dkv, ddi):
    n, rows, _ = kv.shape
    return run(
        finish_kernel, (kv, li, init, end, dkv, ddi),
        [blocked((rows, 2 * HEAD)), blocked((rows, 2 * SLOTS)), blocked((SLOTS, 2 * HEAD)),
         blocked((SLOTS, 2 * HEAD)), blocked((rows, 2 * HEAD)), blocked((rows, 2 * SLOTS))],
        (sds((n, rows, 2 * HEAD), BF), sds((n, rows, 2 * SLOTS))),
        (blocked((rows, 2 * HEAD)), blocked((rows, 2 * SLOTS))),
        n * 10**9, n * 3 * 10**6,
    )


D = 2048
HEADS = 4
RANK = 16
NORMALIZER = 8.0


def inverse_rms(values):
    return lax.rsqrt(jnp.mean(values * values, axis=-1, keepdims=True) + EPSILON)


def silu_slope(values):
    sigmoid_val = jax.nn.sigmoid(values)
    return sigmoid_val * (1.0 + values * (1.0 - sigmoid_val))


def norm_back(grad_hat, hat_rows, scale_rows):
    return scale_rows * (
        grad_hat - hat_rows * jnp.mean(grad_hat * hat_rows, axis=-1, keepdims=True)
    )


def swap(value, axis, step):
    count = lax.axis_size(axis)
    return lax.ppermute(value, axis, [(i, i ^ step) for i in range(count)])


def gather_heads(block):
    return [block] + [swap(block, "p", k) for k in range(1, HEADS)]


def scatter_heads(parts, *fillers):
    got = [swap(parts[k], "p", k) for k in range(1, HEADS)]
    if fillers:
        held = lax.optimization_barrier(tuple(got) + fillers)
        got, fillers = held[: HEADS - 1], held[HEADS - 1 :]
    total = parts[0].astype(F32)
    for part in got:
        total = total + part.astype(F32)
    return (total,) + tuple(fillers) if fillers else total


def after(value, *others):
    return lax.optimization_barrier((value,) + others)[0]


def place_kernel(blocks, spot_ref, *refs):
    ins, out = refs[:-1], refs[-1]
    part = ins[0].shape[1]
    for i, ref in enumerate(ins):
        for k in range(blocks):
            start = pl.multiple_of(spot_ref[i * blocks + k] * part, part)
            out[pl.ds(start, part), :] = ref[k]


def place(parts, spots):
    blocks, part, width = parts[0].shape
    chunk = 256
    table = jnp.stack([jnp.asarray(x, jnp.int32) for row in spots for x in row])
    rows = len(parts) * blocks * part
    return pl.pallas_call(
        functools.partial(place_kernel, blocks),
        grid_spec=pltpu.PrefetchScalarGridSpec(
            num_scalar_prefetch=1,
            grid=(width // chunk,),
            in_specs=[pl.BlockSpec((blocks, part, chunk), lambda i, s: (0, 0, i))] * len(parts),
            out_specs=pl.BlockSpec((rows, chunk), lambda i, s: (0, i)),
        ),
        out_shape=jax.ShapeDtypeStruct((rows, width), BF),
        cost_estimate=pl.CostEstimate(flops=0, bytes_accessed=4 * rows * width, transcendentals=0),
        compiler_params=pltpu.CompilerParams(vmem_limit_bytes=56 << 20),
    )(table, *parts)


def column_cuts(shards, here, k):
    cuts = []
    for shard in shards:
        width = shard.shape[1] // HEADS
        cuts.append(lax.dynamic_slice_in_dim(shard, (here ^ k) * width, width, 1))
    return jnp.concatenate(cuts, axis=1)


def head_columns(shards, here):
    copies = lax.axis_size("r")
    turn = lax.axis_index("r")
    own = column_cuts(shards, here, 0)
    pieces = [own] + [swap(column_cuts(shards, here, k), "p", k) for k in range(1, HEADS)]
    parts, spots = [], []
    for k in range(HEADS):
        for m in range(copies):
            piece = pieces[k] if m == 0 else swap(pieces[k], "r", m)
            parts.append(piece[None])
            spots.append([(here ^ k) * copies + (turn ^ m)])
    return place(parts, spots), pieces[1:]


def head_columns_seq(shards, here):
    copies, count = lax.axis_size("r"), lax.axis_size("seq")
    turn, spot = lax.axis_index("r"), lax.axis_index("seq")
    rows = shards[0].shape[0] // count
    shards = [lax.dynamic_slice_in_dim(shard, spot * rows, rows, 0) for shard in shards]
    own = column_cuts(shards, here, 0)
    pieces = [own] + [swap(column_cuts(shards, here, k), "p", k) for k in range(1, HEADS)]
    parts, spots = [], []
    for j, part in enumerate(gather_seq(jnp.stack(pieces))):
        for m in range(copies):
            parts.append(part if m == 0 else swap(part, "r", m))
            spots.append(
                [(((here ^ k) * copies + (turn ^ m)) * count + (spot ^ j)) for k in range(HEADS)]
            )
    return place(parts, spots), pieces[1:]


def gather_small(packed, here, turn):
    copies = lax.axis_size("r")
    near = jnp.concatenate([packed] + [swap(packed, "r", m) for m in range(1, copies)])
    both = jnp.concatenate(gather_heads(near))
    heads = jnp.arange(HEADS, dtype=jnp.int32) ^ here
    turns = jnp.arange(copies, dtype=jnp.int32) ^ turn
    order = (heads[:, None] * copies + turns[None, :]).reshape(-1)
    return jnp.take(both, order, axis=0)


def sum_small(value, here, turn):
    mine = [lax.dynamic_index_in_dim(value, here ^ k, 0, False) for k in range(HEADS)]
    total = scatter_heads(mine)
    copies = lax.axis_size("r")
    kept = lax.dynamic_index_in_dim(total, turn, 0, True)
    for m in range(1, copies):
        kept = kept + swap(lax.dynamic_index_in_dim(total, turn ^ m, 0, True), "r", m)
    step = 1
    while step < lax.axis_size("seq"):
        kept = kept + swap(kept, "seq", step)
        step *= 2
    return kept[0]


def chain(state, decay, forward):
    count = lax.axis_size("seq")
    total = jnp.zeros_like(state)
    for hop in range(count - 1):
        pair = (hop, hop + 1) if forward else (count - 1 - hop, count - 2 - hop)
        sent = (decay * total + state).astype(BF)
        total = total + lax.ppermute(sent, "seq", [pair]).astype(F32)
    return total


def chain_pair(both, decay, forward):
    return jnp.concatenate(
        [chain(both[..., :HEAD], decay, forward), chain(both[..., HEAD:], decay, forward)], axis=-1
    )


def split_rows(left, turn, step, groups):
    copies, width = left.shape[2:]
    flat = left.reshape(left.shape[0], -1)
    cuts = [
        lax.dynamic_slice_in_dim(flat, (g * copies + (turn ^ step)) * width, width, 1)
        for g in groups
    ]
    return jnp.concatenate(cuts, axis=1)


def reduce_copies(parts):
    total = parts[0]
    for m in range(1, len(parts)):
        total = total + swap(parts[m].astype(BF), "r", m).astype(F32)
    return total


def gather_seq(value):
    count = lax.axis_size("seq")
    found = {0: value}
    step = count // 2
    while step >= 1:
        for j in list(found):
            found[j ^ step] = swap(found[j], "seq", step)
        step //= 2
    return [found[j] for j in range(count)]


def assemble_kernel(counts, spot_ref, *refs):
    n_in, n_out, part = counts
    ins, outs = refs[:n_in], refs[n_in:]
    width = outs[0].shape[1]
    for j in range(n_in):
        for o in range(n_out):
            cut = ins[j][0, :, o * width : (o + 1) * width]
            outs[o][j * part : (j + 1) * part, :] = cut.astype(F32)


def assemble(parts, columns, n_out):
    spans, blocks, part, width = parts.shape
    width //= n_out
    rows = part * spans
    spots = jnp.stack([jnp.asarray(c, jnp.int32) for c in columns])
    return pl.pallas_call(
        functools.partial(assemble_kernel, (spans, n_out, part)),
        grid_spec=pltpu.PrefetchScalarGridSpec(
            num_scalar_prefetch=1,
            grid=(blocks,),
            in_specs=[
                pl.BlockSpec((None, 1, part, n_out * width), lambda i, s, j=j: (j, i, 0, 0))
                for j in range(spans)
            ],
            out_specs=[pl.BlockSpec((rows, width), lambda i, s: (0, s[i]))] * n_out,
        ),
        out_shape=[jax.ShapeDtypeStruct((rows, blocks * width), F32)] * n_out,
        cost_estimate=pl.CostEstimate(
            flops=0, bytes_accessed=6 * n_out * rows * blocks * width, transcendentals=0
        ),
        compiler_params=pltpu.CompilerParams(vmem_limit_bytes=56 << 20),
    )(spots, *([parts] * spans))


def finish_wide(total, here, n_out):
    heads, rows, width = total.shape
    count = lax.axis_size("seq")
    spans = total.astype(BF).reshape(heads, count, rows // count, width).transpose(1, 0, 2, 3)
    part = lax.psum_scatter(spans, "seq", scatter_dimension=0, tiled=False)
    got = jnp.stack([part[0]] + [swap(part[k], "p", k) for k in range(1, HEADS)])
    whole = lax.all_gather(got, "seq", axis=0, tiled=False)
    return assemble(whole, [here ^ k for k in range(HEADS)], n_out)


def line_sum(chunks):
    count = lax.axis_size("seq")
    half, spot = count // 2, lax.axis_index("seq")
    totals, last = [], None
    for chunk in chunks:
        value = chunk.astype(BF)
        if last is not None:
            value = after(value, last)
        sent = value
        for i in range(half - 1):
            got = lax.ppermute(sent, "seq", [(i, i + 1), (count - 1 - i, count - 2 - i)])
            last = got if i == 0 else last
            inner = (spot == i + 1) | (spot == count - 2 - i)
            sent = jnp.where(inner, value + got, sent)
        total = sent + lax.ppermute(sent, "seq", [(half - 1, half), (half, half - 1)])
        for i in range(half - 2, -1, -1):
            got = lax.ppermute(total, "seq", [(i + 1, i), (count - 2 - i, count - 1 - i)])
            outer = (spot == i) | (spot == count - 1 - i)
            total = jnp.where(outer, got, total)
        totals.append(total)
    return totals


def finish_line(total, here, n_out):
    near, far = line_sum([total[1::2], total[0::2]])
    got = [far[0], swap(near[0], "p", 1), swap(far[1], "p", 2), swap(near[1], "p", 3)]
    return assemble(jnp.stack(got)[None], [here ^ k for k in range(HEADS)], n_out)


def body(
    tokens,
    seq_lengths,
    attn_gain,
    query_proj,
    key_proj,
    value_proj,
    decay_down,
    decay_up,
    decay_bias,
    swish_proj,
    slot_gain,
    out_proj,
    mlp_gain,
    mlp_gate,
    mlp_up,
    mlp_down,
    grad_out,
):
    rows = tokens.shape[0]
    copies = lax.axis_size("r")
    owners = HEADS * copies
    shard = D // owners
    here, turn, place = lax.axis_index("p"), lax.axis_index("r"), lax.axis_index("seq")
    group = HEADS * rows

    small = [attn_gain, decay_down, decay_up, decay_bias, slot_gain, mlp_gain, seq_lengths]
    packed = jnp.concatenate([a.astype(F32).reshape(-1) for a in small])
    packed = gather_small(packed[None], here, turn)
    fields, offset = [], 0
    for a in small:
        fields.append(packed[:, offset : offset + a.size])
        offset += a.size
    gain_one = fields[0].reshape(D)
    down_full = fields[1].reshape(D, RANK).astype(BF)
    up_full = fields[2].reshape(owners, RANK, -1).transpose(1, 0, 2).reshape(RANK, HEADS * SLOTS)
    up_head = lax.dynamic_slice_in_dim(up_full, here * SLOTS, SLOTS, 1)
    bias_head = lax.dynamic_slice_in_dim(fields[3].reshape(HEADS * SLOTS), here * SLOTS, SLOTS, 0)
    gain_head = lax.dynamic_slice_in_dim(fields[4].reshape(D), here * HEAD, HEAD, 0)
    gain_head8 = jnp.broadcast_to(gain_head[None], (8, HEAD))
    gain_two = fields[5].reshape(D)
    lengths = fields[6].reshape(HEADS, copies)
    positions = (place * rows + jnp.arange(rows, dtype=jnp.int32)).astype(F32)
    masks = [
        (positions < lax.dynamic_index_in_dim(lengths, here ^ k, 0, False)[turn]).astype(F32)
        for k in range(HEADS)
    ]
    mask_all = jnp.concatenate(masks)[:, None]
    mask_own = masks[0][:, None]

    token_blocks = gather_heads(tokens)
    weight_kv, kv_pieces = head_columns([key_proj, value_proj], here)
    late = lax.optimization_barrier((query_proj, swish_proj, mlp_gate, mlp_up) + tuple(kv_pieces))
    weight_qs, qs_pieces = head_columns(late[:2], here)
    weight_gu, gu_pieces = head_columns_seq(late[2:4], here)
    grad_blocks = gather_heads(after(grad_out, *qs_pieces))
    weight_out = lax.all_gather(out_proj, "r", axis=0, tiled=True)
    weight_down = lax.all_gather(mlp_down, "r", axis=0, tiled=True)

    tokens_all = jnp.concatenate(token_blocks).astype(F32)
    normed = (tokens_all * inverse_rms(tokens_all) * gain_one).astype(BF)
    kv = mm(normed, weight_kv).astype(BF).reshape(HEADS, rows, 2 * HEAD)
    gate_low = mm(normed, down_full)
    forget = exact(gate_low, up_head) + bias_head
    log_sig = jax.nn.log_sigmoid(forget) / NORMALIZER
    li = jnp.concatenate([mask_all * log_sig, mask_all * -jnp.expm1(log_sig)], axis=1)
    li = li.reshape(HEADS, rows, 2 * SLOTS)
    state, decay = chunk_states(kv, li)
    decay = decay[:, :, :1]
    init = chain_pair(state, decay, True)
    qs = mm(normed, weight_qs).reshape(HEADS, rows, 2 * HEAD)
    gated, mixer_out, probs, mix = mixer_forward(qs, kv, li, init, gain_head8)
    gated = gated.reshape(group, HEAD)
    attn_part = mm(gated, weight_out).astype(BF).reshape(HEADS, rows, D)
    grad_mlp = (mask_all * jnp.concatenate(grad_blocks).astype(F32)).astype(BF)
    attn_out, grad_act = scatter_heads(
        [attn_part[k] for k in range(HEADS)], mm_nt(grad_mlp, weight_down)
    )

    tokens_f = tokens.astype(F32)
    residual = tokens_f + mask_own * attn_out
    scale_two = inverse_rms(residual)
    hat_two = residual * scale_two
    normed_two_own = (hat_two * gain_two).astype(BF)
    two_blocks = gather_heads(normed_two_own)
    normed_two = jnp.concatenate(two_blocks)

    hidden_width = weight_down.shape[0]
    gate_up = mm(normed_two, weight_gu)
    gate_pre, up_pre = gate_up[:, :hidden_width], gate_up[:, hidden_width:]
    hidden = (jax.nn.silu(gate_pre) * up_pre).astype(BF)
    grad_gate = (grad_act * up_pre * silu_slope(gate_pre)).astype(BF)
    grad_up = (grad_act * jax.nn.silu(gate_pre)).astype(BF)
    grad_gu = jnp.concatenate([grad_gate, grad_up], axis=1)
    two_part = mm_nt(grad_gu, weight_gu).astype(BF).reshape(HEADS, rows, D)
    two_view = normed_two.reshape(group, HEADS, copies, shard)
    order = [here ^ k for k in range(HEADS)]
    gu_parts = [mm_tn(split_rows(two_view, turn, m, order), grad_gu) for m in range(copies)]
    gu_parts = [gu_parts[0]] + [part.astype(BF) for part in gu_parts[1:]]
    down_part = mm_tn(hidden, grad_mlp)
    grad_norm_two, down_part, *gu_parts = scatter_heads(
        [two_part[k] for k in range(HEADS)], down_part, *gu_parts
    )
    gain_two_grad = jnp.sum(grad_norm_two * hat_two, axis=0)
    grad_rows = grad_out.astype(F32)
    grad_resid = grad_rows + norm_back(grad_norm_two * gain_two, hat_two, scale_two)
    grad_attn_own = (mask_own * grad_resid).astype(BF)
    attn_blocks = gather_heads(grad_attn_own)
    mlp_part = mm(hidden, weight_down).astype(BF)
    mlp_part, *attn_blocks = lax.optimization_barrier((mlp_part,) + tuple(attn_blocks))
    grad_attn = jnp.concatenate(attn_blocks)
    mlp_part = mlp_part.reshape(HEADS, rows, D)
    mlp_out = scatter_heads([mlp_part[k] for k in range(HEADS)])
    result = (residual + mask_own * mlp_out).astype(BF)

    gu_total = reduce_copies(gu_parts).reshape(HEADS, shard, 2 * hidden_width)
    down_rows = mlp_down.shape[0]
    down_total = reduce_copies(
        [
            lax.dynamic_slice_in_dim(down_part, (turn ^ m) * down_rows, down_rows, 0)
            for m in range(copies)
        ]
    )
    gate_grad, up_grad = finish_wide(gu_total, here, 2)
    down_grad = lax.psum(down_total.astype(BF), "seq")

    grad_gated = mm_nt(grad_attn, weight_out).reshape(HEADS, rows, HEAD)
    grad_qs, grad_kv, grad_li, adjoint, slot_part = mixer_backward(
        qs, kv, li, init, gain_head8, mixer_out, probs, mix, grad_gated
    )
    ends = chain_pair(adjoint, decay, False)
    grad_kv, grad_li = mixer_finish(kv, li, init, ends, grad_kv, grad_li)
    grad_qs = grad_qs.reshape(group, 2 * HEAD)
    grad_kv = grad_kv.reshape(group, 2 * HEAD)
    grad_li = grad_li.reshape(group, 2 * SLOTS)
    grad_decay = (
        mask_all
        * (grad_li[:, :SLOTS] - grad_li[:, SLOTS:] * jnp.exp(log_sig))
        / NORMALIZER
        * jax.nn.sigmoid(-forget)
    )
    bias_part = jnp.sum(grad_decay, axis=0)
    up_part = lax.dot_general(
        gate_low, grad_decay, (((0,), (0,)), ((), ())), precision=HIGHEST, preferred_element_type=F32
    )
    grad_low = lax.dot_general(
        grad_decay, up_head, (((1,), (1,)), ((), ())), precision=HIGHEST, preferred_element_type=F32
    ).astype(BF)
    down_low_part = mm_tn(normed, grad_low)

    one_part = (
        (mm_nt(grad_qs, weight_qs) + mm_nt(grad_kv, weight_kv) + mm_nt(grad_low, down_full))
        .astype(BF)
        .reshape(HEADS, rows, D)
    )
    grad_norm_one = scatter_heads([one_part[k] for k in range(HEADS)])
    scale_one = inverse_rms(tokens_f)
    hat_one = tokens_f * scale_one
    gain_one_grad = jnp.sum(grad_norm_one * hat_one, axis=0)
    grad_tokens = (grad_resid + norm_back(grad_norm_one * gain_one, hat_one, scale_one)).astype(BF)

    one_view = normed.reshape(group, HEADS, copies, shard)
    one_views = [split_rows(one_view, turn, m, order) for m in range(copies)]
    qs_total = reduce_copies([mm_tn(v, grad_qs) for v in one_views])
    kv_total = reduce_copies([mm_tn(v, grad_kv) for v in one_views])
    out_view = gated.reshape(group, 1, copies, shard)
    out_total = reduce_copies(
        [mm_tn(split_rows(out_view, turn, m, [0]), grad_attn) for m in range(copies)]
    )
    query_grad, swish_grad = finish_line(qs_total.reshape(HEADS, shard, 2 * HEAD), here, 2)
    key_grad, value_grad = finish_line(kv_total.reshape(HEADS, shard, 2 * HEAD), here, 2)
    out_grad = lax.psum(after(out_total.astype(BF), down_grad), "seq").astype(F32)

    def placed(part, width):
        whole = jnp.zeros(part.shape[:-1] + (HEADS * width,), F32)
        return lax.dynamic_update_slice_in_dim(whole, part, here * width, part.ndim - 1)

    up_sum = placed(up_part, SLOTS).reshape(RANK, HEADS, copies, -1).transpose(1, 2, 0, 3)
    sums = [
        gain_one_grad,
        down_low_part,
        up_sum,
        placed(bias_part, SLOTS),
        placed(slot_part[0], HEAD),
        gain_two_grad,
    ]
    flat = jnp.concatenate([a.reshape(HEADS, copies, -1) for a in sums], axis=2)
    flat = sum_small(flat, here, turn)
    totals, offset = [], 0
    for a in sums:
        size = a.size // owners
        totals.append(flat[offset : offset + size])
        offset += size

    return (
        result,
        grad_tokens,
        totals[0],
        query_grad,
        key_grad,
        value_grad,
        totals[1].reshape(shard, RANK),
        totals[2].reshape(RANK, -1),
        totals[3],
        swish_grad,
        totals[4],
        out_grad,
        totals[5],
        gate_grad,
        up_grad,
        down_grad.astype(F32),
    )


def solution(mesh):
    count, span = mesh.devices.shape
    split = Mesh(mesh.devices.reshape(HEADS, count // HEADS, span), ("p", "r", "seq"))
    rows = P(("p", "r", "seq"), None)
    matrix, vector, last = P(("p", "r"), None), P(("p", "r")), P(None, ("p", "r"))
    in_specs = (
        rows, vector, vector, matrix, matrix, matrix, matrix, last, vector, matrix, vector, matrix,
        vector, matrix, matrix, matrix, rows,
    )
    out_specs = (
        rows, rows, vector, matrix, matrix, matrix, matrix, last, vector, matrix, vector, matrix,
        vector, matrix, matrix, matrix,
    )
    return jax.shard_map(body, mesh=split, in_specs=in_specs, out_specs=out_specs, check_vma=False)
```

```python
import functools
import jax
import jax.numpy as jnp
from jax import lax
from jax.experimental import pallas as pl
from jax.experimental.pallas import tpu as pltpu
from jax.sharding import Mesh, PartitionSpec as P

HEAD = 512
SLOTS = 64
SCALE = HEAD ** (-0.5)
EPSILON = 1e-06
HIGHEST = lax.Precision.HIGHEST
BF = jnp.bfloat16
F32 = jnp.float32


def mm(a, b):
    return lax.dot_general(a, b, (((1,), (0,)), ((), ())), preferred_element_type=F32)


def mm_nt(a, b):
    return lax.dot_general(a, b, (((1,), (1,)), ((), ())), preferred_element_type=F32)


def mm_tn(a, b):
    return lax.dot_general(a, b, (((0,), (0,)), ((), ())), preferred_element_type=F32)


def exact(a, b):
    return lax.dot_general(
        a, b, (((1,), (0,)), ((), ())), precision=HIGHEST, preferred_element_type=F32
    )


def row_bit(rows, level):
    t = lax.broadcasted_iota(jnp.int32, (rows, SLOTS), 0)
    return ((t >> level) & 1) == 1


def prefix_levels(log_decay):
    rows = log_decay.shape[0]
    levels = rows.bit_length() - 1
    f, g = log_decay, jnp.zeros_like(log_decay)
    out = []
    for level in range(levels):
        out.append((f, g))
        total = f + g
        step = 1 << level
        bit = row_bit(rows, level)
        f = f + jnp.where(bit, pltpu.roll(total, step, 0), 0.0)
        g = g + jnp.where(bit, 0.0, pltpu.roll(total, rows - step, 0))
    return out, f, g


def same_block(rows, level):
    t = lax.broadcasted_iota(jnp.int32, (rows, rows), 0)
    s = lax.broadcasted_iota(jnp.int32, (rows, rows), 1)
    return (t >> (level + 1)) == (s >> (level + 1))


def level_mask(table, level, levels):
    if level == levels - 1:
        return table
    return jnp.where(same_block(table.shape[0], level), table, jnp.zeros_like(table))


def factors(pair, level, inflow):
    f, g = pair
    bit = row_bit(f.shape[0], level)
    left = jnp.where(bit, jnp.exp(f), 0.0)
    right = jnp.where(bit, 0.0, jnp.exp(g))
    return left, right, right * inflow


def diagonal(rows):
    t = lax.broadcasted_iota(jnp.int32, (rows, rows), 0)
    s = lax.broadcasted_iota(jnp.int32, (rows, rows), 1)
    return t == s


def slot_table(weights, pairs, inflow):
    rows = weights.shape[0]
    levels = len(pairs)
    table = jnp.where(diagonal(rows), jnp.sum(weights * inflow, axis=1, keepdims=True), 0.0)
    for level in range(levels):
        left, _, gain = factors(pairs[level], level, inflow)
        block = mm_nt((weights * left).astype(BF), gain.astype(BF))
        table = table + level_mask(block, level, levels)
    return table


def slot_sums(table, pairs, inflow):
    rows = table.shape[0]
    levels = len(pairs)
    own = jnp.sum(jnp.where(diagonal(rows), table, 0.0), axis=1, keepdims=True)
    low = table.astype(BF)
    total = own * inflow
    for level in range(levels):
        left, _, gain = factors(pairs[level], level, inflow)
        total = total + left * mm(level_mask(low, level, levels), gain.astype(BF))
    return total


def states_kernel(kv_ref, li_ref, state_ref, decay_ref):
    kv = kv_ref[0]
    log_decay = li_ref[0, :, :SLOTS]
    inflow = li_ref[0, :, SLOTS:]
    rows = kv.shape[0]
    t = lax.broadcasted_iota(jnp.int32, (rows, rows), 0)
    s = lax.broadcasted_iota(jnp.int32, (rows, rows), 1)
    after = exact((s > t).astype(F32), log_decay)
    weight = jnp.exp(after) * inflow
    state_ref[0] = mm_tn(weight.astype(BF), kv)
    total = lax.dot_general(
        log_decay, jnp.ones((rows, 128), F32), (((0,), (0,)), ((), ())),
        precision=HIGHEST, preferred_element_type=F32,
    )
    decay_ref[0] = jnp.exp(total)


def forward_kernel(qs_ref, kv_ref, li_ref, init_ref, gain_ref, gated_ref, out_ref, prob_ref, mix_ref):
    queries = qs_ref[0, :, :HEAD].astype(BF)
    swish = qs_ref[0, :, HEAD:]
    keys = kv_ref[0, :, :HEAD]
    values = kv_ref[0, :, HEAD:]
    log_decay = li_ref[0, :, :SLOTS]
    inflow = li_ref[0, :, SLOTS:]
    init = init_ref[0].astype(BF)
    pairs, running, _ = prefix_levels(log_decay)
    growth = jnp.exp(running)
    scores = mm_nt(queries, keys) * SCALE
    slots = slot_sums(scores, pairs, inflow) + mm_nt(queries, init[:, :HEAD]) * SCALE * growth
    top = jnp.max(slots, axis=1, keepdims=True)
    weights = jnp.exp(slots - top)
    probs = weights / jnp.sum(weights, axis=1, keepdims=True)
    mix = slot_table(probs, pairs, inflow).astype(BF)
    out = mm(mix, values) + mm((probs * growth).astype(BF), init[:, HEAD:])
    hat = out * lax.rsqrt(jnp.mean(out * out, axis=1, keepdims=True) + EPSILON)
    gated_ref[0] = (hat * gain_ref[0:1] * (swish * jax.nn.sigmoid(swish))).astype(BF)
    out_ref[0] = out
    prob_ref[0] = probs
    mix_ref[0] = mix


def backward_kernel(
    qs_ref, kv_ref, li_ref, init_ref, gain_ref, out_ref, prob_ref, mix_ref, gg_ref,
    dqs_ref, dkv_ref, ddi_ref, adj_ref, sg_ref,
):
    queries = qs_ref[0, :, :HEAD].astype(BF)
    swish = qs_ref[0, :, HEAD:]
    keys = kv_ref[0, :, :HEAD]
    values = kv_ref[0, :, HEAD:]
    log_decay = li_ref[0, :, :SLOTS]
    inflow = li_ref[0, :, SLOTS:]
    init = init_ref[0].astype(BF)
    out = out_ref[0]
    probs = prob_ref[0]
    gain = gain_ref[0:1]
    rows = out.shape[0]
    scale_out = lax.rsqrt(jnp.mean(out * out, axis=1, keepdims=True) + EPSILON)
    hat = out * scale_out
    sig = jax.nn.sigmoid(swish)
    silu = swish * sig
    gg = gg_ref[0].astype(F32)
    gg_hat = gg * hat
    dqs_ref[0, :, HEAD:] = (gg_hat * gain * (sig * (1.0 + swish * (1.0 - sig)))).astype(BF)
    part = jnp.broadcast_to(jnp.sum(gg_hat * silu, axis=0, keepdims=True), (8, HEAD))

    @pl.when(pl.program_id(0) == 0)
    def _():
        sg_ref[...] = part

    @pl.when(pl.program_id(0) > 0)
    def _():
        sg_ref[...] = sg_ref[...] + part

    grad_hat = gg * gain * silu
    dout = scale_out * (grad_hat - hat * jnp.mean(grad_hat * hat, axis=1, keepdims=True))
    dout = dout.astype(BF)
    pairs, running, _ = prefix_levels(log_decay)
    levels = len(pairs)
    growth = jnp.exp(running)
    scores = mm_nt(queries, keys) * SCALE
    grads = mm_nt(dout, values)
    key_part = mm_nt(queries, init[:, :HEAD]) * SCALE * growth
    value_part = mm_nt(dout, init[:, HEAD:]) * growth
    dprob = slot_sums(grads, pairs, inflow) + value_part
    dslot = probs * (dprob - jnp.sum(probs * dprob, axis=1, keepdims=True))
    back = slot_table(dslot, pairs, inflow).astype(BF)
    dslot_g = (dslot * growth).astype(BF)
    prob_g = (probs * growth).astype(BF)
    dqs_ref[0, :, :HEAD] = (SCALE * (mm(back, keys) + mm(dslot_g, init[:, :HEAD]))).astype(BF)
    dkv_ref[0, :, :HEAD] = SCALE * mm_tn(back, queries)
    dkv_ref[0, :, HEAD:] = mm_tn(mix_ref[0], dout)
    adj_ref[0, :, :HEAD] = SCALE * mm_tn(dslot_g, queries)
    adj_ref[0, :, HEAD:] = mm_tn(prob_g, dout)
    diag = diagonal(rows)
    own_a = jnp.sum(jnp.where(diag, scores, 0.0), axis=1, keepdims=True)
    own_b = jnp.sum(jnp.where(diag, grads, 0.0), axis=1, keepdims=True)
    dinflow = dslot * own_a + probs * own_b
    scores_low = scores.astype(BF)
    grads_low = grads.astype(BF)
    fbar = dslot * key_part + probs * value_part
    gbar = jnp.zeros_like(fbar)
    for level in range(levels - 1, -1, -1):
        left, right, amount = factors(pairs[level], level, inflow)
        table_a = level_mask(scores_low, level, levels)
        table_b = level_mask(grads_low, level, levels)
        amount_low = amount.astype(BF)
        dleft = dslot * left
        pleft = probs * left
        grow = dleft * mm(table_a, amount_low) + pleft * mm(table_b, amount_low)
        back_in = mm_tn(table_a, dleft.astype(BF)) + mm_tn(table_b, pleft.astype(BF))
        dinflow = dinflow + right * back_in
        step = 1 << level
        bit = row_bit(rows, level)
        total = pltpu.roll(jnp.where(bit, fbar, 0.0), rows - step, 0) + pltpu.roll(
            jnp.where(bit, 0.0, gbar), step, 0
        )
        fbar = fbar + grow + total
        gbar = gbar + amount * back_in + total
    ddi_ref[0, :, :SLOTS] = fbar
    ddi_ref[0, :, SLOTS:] = dinflow


def finish_kernel(kv_ref, li_ref, init_ref, end_ref, dkv_ref, ddi_ref, okv_ref, oddi_ref):
    kv = kv_ref[0]
    log_decay = li_ref[0, :, :SLOTS]
    inflow = li_ref[0, :, SLOTS:]
    end = end_ref[0]
    rows = kv.shape[0]
    t = lax.broadcasted_iota(jnp.int32, (rows, rows), 0)
    s = lax.broadcasted_iota(jnp.int32, (rows, rows), 1)
    earlier = (s < t).astype(F32)
    after = exact((s > t).astype(F32), log_decay)
    fade = jnp.exp(after)
    weight = fade * inflow
    end_low = end.astype(BF)
    okv_ref[0] = (dkv_ref[0] + mm(weight.astype(BF), end_low)).astype(BF)
    reach = mm_nt(kv, end_low)
    whole = jnp.exp(jnp.sum(log_decay, axis=0, keepdims=True))
    carry = lax.dot_general(
        jnp.ones((8, 2 * HEAD), F32), end * init_ref[0], (((1,), (1,)), ((), ())),
        precision=HIGHEST, preferred_element_type=F32,
    )[0:1]
    oddi_ref[0, :, :SLOTS] = (
        ddi_ref[0, :, :SLOTS] + exact(earlier, weight * reach) + whole * carry
    )
    oddi_ref[0, :, SLOTS:] = ddi_ref[0, :, SLOTS:] + fade * reach


def blocked(shape):
    return pl.BlockSpec((1,) + shape, lambda i: (i, 0, 0))


def run(kernel, args, specs, outs, out_specs, flops, moved):
    return pl.pallas_call(
        kernel,
        grid=(args[0].shape[0],),
        in_specs=specs,
        out_specs=out_specs,
        out_shape=outs,
        cost_estimate=pl.CostEstimate(flops=flops, bytes_accessed=moved, transcendentals=0),
        compiler_params=pltpu.CompilerParams(vmem_limit_bytes=56 << 20),
    )(*args)


def sds(shape, dtype=F32):
    return jax.ShapeDtypeStruct(shape, dtype)


def chunk_states(kv, li):
    n, rows, _ = kv.shape
    return run(
        states_kernel, (kv, li),
        [blocked((rows, 2 * HEAD)), blocked((rows, 2 * SLOTS))],
        (sds((n, SLOTS, 2 * HEAD)), sds((n, SLOTS, 128))),
        (blocked((SLOTS, 2 * HEAD)), blocked((SLOTS, 128))),
        n * 10**9, n * 10**6,
    )


def mixer_forward(qs, kv, li, init, gain):
    n, rows, _ = kv.shape
    return run(
        forward_kernel, (qs, kv, li, init, gain),
        [blocked((rows, 2 * HEAD)), blocked((rows, 2 * HEAD)), blocked((rows, 2 * SLOTS)),
         blocked((SLOTS, 2 * HEAD)), pl.BlockSpec((8, HEAD), lambda i: (0, 0))],
        (sds((n, rows, HEAD), BF), sds((n, rows, HEAD)), sds((n, rows, SLOTS)), sds((n, rows, rows), BF)),
        (blocked((rows, HEAD)), blocked((rows, HEAD)), blocked((rows, SLOTS)), blocked((rows, rows))),
        n * 3 * 10**9, n * 4 * 10**6,
    )


def mixer_backward(qs, kv, li, init, gain, out, probs, mix, gg):
    n, rows, _ = kv.shape
    return run(
        backward_kernel, (qs, kv, li, init, gain, out, probs, mix, gg),
        [blocked((rows, 2 * HEAD)), blocked((rows, 2 * HEAD)), blocked((rows, 2 * SLOTS)),
         blocked((SLOTS, 2 * HEAD)), pl.BlockSpec((8, HEAD), lambda i: (0, 0)),
         blocked((rows, HEAD)), blocked((rows, SLOTS)), blocked((rows, rows)), blocked((rows, HEAD))],
        (sds((n, rows, 2 * HEAD), BF), sds((n, rows, 2 * HEAD)), sds((n, rows, 2 * SLOTS)),
         sds((n, SLOTS, 2 * HEAD)), sds((8, HEAD))),
        (blocked((rows, 2 * HEAD)), blocked((rows, 2 * HEAD)), blocked((rows, 2 * SLOTS)),
         blocked((SLOTS, 2 * HEAD)), pl.BlockSpec((8, HEAD), lambda i: (0, 0))),
        n * 6 * 10**9, n * 5 * 10**6,
    )


def mixer_finish(kv, li, init, end, dkv, ddi):
    n, rows, _ = kv.shape
    return run(
        finish_kernel, (kv, li, init, end, dkv, ddi),
        [blocked((rows, 2 * HEAD)), blocked((rows, 2 * SLOTS)), blocked((SLOTS, 2 * HEAD)),
         blocked((SLOTS, 2 * HEAD)), blocked((rows, 2 * HEAD)), blocked((rows, 2 * SLOTS))],
        (sds((n, rows, 2 * HEAD), BF), sds((n, rows, 2 * SLOTS))),
        (blocked((rows, 2 * HEAD)), blocked((rows, 2 * SLOTS))),
        n * 10**9, n * 3 * 10**6,
    )


D = 2048
HEADS = 4
RANK = 16
NORMALIZER = 8.0


def inverse_rms(values):
    return lax.rsqrt(jnp.mean(values * values, axis=-1, keepdims=True) + EPSILON)


def silu_slope(values):
    sigmoid_val = jax.nn.sigmoid(values)
    return sigmoid_val * (1.0 + values * (1.0 - sigmoid_val))


def norm_back(grad_hat, hat_rows, scale_rows):
    return scale_rows * (
        grad_hat - hat_rows * jnp.mean(grad_hat * hat_rows, axis=-1, keepdims=True)
    )


def swap(value, axis, step):
    count = lax.axis_size(axis)
    return lax.ppermute(value, axis, [(i, i ^ step) for i in range(count)])


def gather_heads(block):
    return [block] + [swap(block, "p", k) for k in range(1, HEADS)]


def scatter_heads(parts, *fillers):
    got = [swap(parts[k], "p", k) for k in range(1, HEADS)]
    if fillers:
        held = lax.optimization_barrier(tuple(got) + fillers)
        got, fillers = held[: HEADS - 1], held[HEADS - 1 :]
    total = parts[0].astype(F32)
    for part in got:
        total = total + part.astype(F32)
    return (total,) + tuple(fillers) if fillers else total


def after(value, *others):
    return lax.optimization_barrier((value,) + others)[0]


def place_kernel(blocks, spot_ref, *refs):
    ins, out = refs[:-1], refs[-1]
    part = ins[0].shape[1]
    for i, ref in enumerate(ins):
        for k in range(blocks):
            start = pl.multiple_of(spot_ref[i * blocks + k] * part, part)
            out[pl.ds(start, part), :] = ref[k]


def place(parts, spots):
    blocks, part, width = parts[0].shape
    chunk = 256
    table = jnp.stack([jnp.asarray(x, jnp.int32) for row in spots for x in row])
    rows = len(parts) * blocks * part
    return pl.pallas_call(
        functools.partial(place_kernel, blocks),
        grid_spec=pltpu.PrefetchScalarGridSpec(
            num_scalar_prefetch=1,
            grid=(width // chunk,),
            in_specs=[pl.BlockSpec((blocks, part, chunk), lambda i, s: (0, 0, i))] * len(parts),
            out_specs=pl.BlockSpec((rows, chunk), lambda i, s: (0, i)),
        ),
        out_shape=jax.ShapeDtypeStruct((rows, width), BF),
        cost_estimate=pl.CostEstimate(flops=0, bytes_accessed=4 * rows * width, transcendentals=0),
        compiler_params=pltpu.CompilerParams(vmem_limit_bytes=56 << 20),
    )(table, *parts)


def column_cuts(shards, here, k):
    cuts = []
    for shard in shards:
        width = shard.shape[1] // HEADS
        cuts.append(lax.dynamic_slice_in_dim(shard, (here ^ k) * width, width, 1))
    return jnp.concatenate(cuts, axis=1)


def head_columns(shards, here):
    copies = lax.axis_size("r")
    turn = lax.axis_index("r")
    own = column_cuts(shards, here, 0)
    pieces = [own] + [swap(column_cuts(shards, here, k), "p", k) for k in range(1, HEADS)]
    parts, spots = [], []
    for k in range(HEADS):
        for m in range(copies):
            piece = pieces[k] if m == 0 else swap(pieces[k], "r", m)
            parts.append(piece[None])
            spots.append([(here ^ k) * copies + (turn ^ m)])
    return place(parts, spots), pieces[1:]


def head_columns_seq(shards, here):
    copies, count = lax.axis_size("r"), lax.axis_size("seq")
    turn, spot = lax.axis_index("r"), lax.axis_index("seq")
    rows = shards[0].shape[0] // count
    shards = [lax.dynamic_slice_in_dim(shard, spot * rows, rows, 0) for shard in shards]
    own = column_cuts(shards, here, 0)
    pieces = [own] + [swap(column_cuts(shards, here, k), "p", k) for k in range(1, HEADS)]
    parts, spots = [], []
    for j, part in enumerate(gather_seq(jnp.stack(pieces))):
        for m in range(copies):
            parts.append(part if m == 0 else swap(part, "r", m))
            spots.append(
                [(((here ^ k) * copies + (turn ^ m)) * count + (spot ^ j)) for k in range(HEADS)]
            )
    return place(parts, spots), pieces[1:]


def gather_small(packed, here, turn):
    copies = lax.axis_size("r")
    near = jnp.concatenate([packed] + [swap(packed, "r", m) for m in range(1, copies)])
    both = jnp.concatenate(gather_heads(near))
    heads = jnp.arange(HEADS, dtype=jnp.int32) ^ here
    turns = jnp.arange(copies, dtype=jnp.int32) ^ turn
    order = (heads[:, None] * copies + turns[None, :]).reshape(-1)
    return jnp.take(both, order, axis=0)


def sum_small(value, here, turn):
    mine = [lax.dynamic_index_in_dim(value, here ^ k, 0, False) for k in range(HEADS)]
    total = scatter_heads(mine)
    copies = lax.axis_size("r")
    kept = lax.dynamic_index_in_dim(total, turn, 0, True)
    for m in range(1, copies):
        kept = kept + swap(lax.dynamic_index_in_dim(total, turn ^ m, 0, True), "r", m)
    step = 1
    while step < lax.axis_size("seq"):
        kept = kept + swap(kept, "seq", step)
        step *= 2
    return kept[0]


def chain(state, decay, forward):
    count = lax.axis_size("seq")
    total = jnp.zeros_like(state)
    for hop in range(count - 1):
        pair = (hop, hop + 1) if forward else (count - 1 - hop, count - 2 - hop)
        sent = (decay * total + state).astype(BF)
        total = total + lax.ppermute(sent, "seq", [pair]).astype(F32)
    return total


def chain_pair(both, decay, forward):
    return jnp.concatenate(
        [chain(both[..., :HEAD], decay, forward), chain(both[..., HEAD:], decay, forward)], axis=-1
    )


def split_rows(left, turn, step, groups):
    copies, width = left.shape[2:]
    flat = left.reshape(left.shape[0], -1)
    cuts = [
        lax.dynamic_slice_in_dim(flat, (g * copies + (turn ^ step)) * width, width, 1)
        for g in groups
    ]
    return jnp.concatenate(cuts, axis=1)


def sum_copies(own, away):
    got = [swap(part, "r", m + 1) for m, part in enumerate(away)]
    total = own()
    for part in got:
        total = total + part.astype(F32)
    return total.astype(BF)


def gather_seq(value):
    count = lax.axis_size("seq")
    found = {0: value}
    step = count // 2
    while step >= 1:
        for j in list(found):
            found[j ^ step] = swap(found[j], "seq", step)
        step //= 2
    return [found[j] for j in range(count)]


def assemble_kernel(counts, spot_ref, *refs):
    n_in, n_out, part = counts
    ins, outs = refs[:n_in], refs[n_in:]
    width = outs[0].shape[1]
    for j in range(n_in):
        for o in range(n_out):
            cut = ins[j][0, :, o * width : (o + 1) * width]
            outs[o][j * part : (j + 1) * part, :] = cut.astype(F32)


def assemble(parts, columns, n_out):
    spans, blocks, part, width = parts.shape
    width //= n_out
    rows = part * spans
    spots = jnp.stack([jnp.asarray(c, jnp.int32) for c in columns])
    return pl.pallas_call(
        functools.partial(assemble_kernel, (spans, n_out, part)),
        grid_spec=pltpu.PrefetchScalarGridSpec(
            num_scalar_prefetch=1,
            grid=(blocks,),
            in_specs=[
                pl.BlockSpec((None, 1, part, n_out * width), lambda i, s, j=j: (j, i, 0, 0))
                for j in range(spans)
            ],
            out_specs=[pl.BlockSpec((rows, width), lambda i, s: (0, s[i]))] * n_out,
        ),
        out_shape=[jax.ShapeDtypeStruct((rows, blocks * width), F32)] * n_out,
        cost_estimate=pl.CostEstimate(
            flops=0, bytes_accessed=6 * n_out * rows * blocks * width, transcendentals=0
        ),
        compiler_params=pltpu.CompilerParams(vmem_limit_bytes=56 << 20),
    )(spots, *([parts] * spans))


def inward(value):
    count = lax.axis_size("seq")
    for i in range(count // 2 - 1):
        value = value + lax.ppermute(value, "seq", [(i, i + 1), (count - 1 - i, count - 2 - i)])
    return value


def across(value):
    half = lax.axis_size("seq") // 2
    return value + lax.ppermute(value, "seq", [(half - 1, half), (half, half - 1)])


def outward(total):
    count, spot = lax.axis_size("seq"), lax.axis_index("seq")
    for i in range(count // 2 - 2, -1, -1):
        got = lax.ppermute(total, "seq", [(i + 1, i), (count - 2 - i, count - 1 - i)])
        total = jnp.where((spot == i) | (spot == count - 1 - i), got, total)
    return total


def spread_line(near, far, here, n_out):
    got = [far[0], swap(near[0], "p", 1), swap(far[1], "p", 2), swap(near[1], "p", 3)]
    return assemble(jnp.stack(got)[None], [here ^ k for k in range(HEADS)], n_out)


def swap_diagonal(part):
    count = lax.axis_size("seq")
    sends = [(p * count + z, (p ^ z) * count + z) for p in range(HEADS) for z in range(count)]
    return lax.ppermute(part, ("p", "seq"), sends)


def body(
    tokens,
    seq_lengths,
    attn_gain,
    query_proj,
    key_proj,
    value_proj,
    decay_down,
    decay_up,
    decay_bias,
    swish_proj,
    slot_gain,
    out_proj,
    mlp_gain,
    mlp_gate,
    mlp_up,
    mlp_down,
    grad_out,
):
    rows = tokens.shape[0]
    copies = lax.axis_size("r")
    owners = HEADS * copies
    shard = D // owners
    here, turn, place = lax.axis_index("p"), lax.axis_index("r"), lax.axis_index("seq")
    group = HEADS * rows

    small = [attn_gain, decay_down, decay_up, decay_bias, slot_gain, mlp_gain, seq_lengths]
    packed = jnp.concatenate([a.astype(F32).reshape(-1) for a in small])
    packed = gather_small(packed[None], here, turn)
    fields, offset = [], 0
    for a in small:
        fields.append(packed[:, offset : offset + a.size])
        offset += a.size
    gain_one = fields[0].reshape(D)
    down_full = fields[1].reshape(D, RANK).astype(BF)
    up_full = fields[2].reshape(owners, RANK, -1).transpose(1, 0, 2).reshape(RANK, HEADS * SLOTS)
    up_head = lax.dynamic_slice_in_dim(up_full, here * SLOTS, SLOTS, 1)
    bias_head = lax.dynamic_slice_in_dim(fields[3].reshape(HEADS * SLOTS), here * SLOTS, SLOTS, 0)
    gain_head = lax.dynamic_slice_in_dim(fields[4].reshape(D), here * HEAD, HEAD, 0)
    gain_head8 = jnp.broadcast_to(gain_head[None], (8, HEAD))
    gain_two = fields[5].reshape(D)
    lengths = fields[6].reshape(HEADS, copies)
    positions = (place * rows + jnp.arange(rows, dtype=jnp.int32)).astype(F32)
    masks = [
        (positions < lax.dynamic_index_in_dim(lengths, here ^ k, 0, False)[turn]).astype(F32)
        for k in range(HEADS)
    ]
    mask_all = jnp.concatenate(masks)[:, None]
    mask_own = masks[0][:, None]

    token_blocks = gather_heads(tokens)
    weight_kv, kv_pieces = head_columns_seq([key_proj, value_proj], here)
    late = lax.optimization_barrier((query_proj, swish_proj, mlp_gate, mlp_up) + tuple(kv_pieces))
    weight_qs, qs_pieces = head_columns(late[:2], here)
    weight_gu, gu_pieces = head_columns_seq(late[2:4], here)
    grad_blocks = gather_heads(after(grad_out, *qs_pieces))
    weight_out = lax.all_gather(out_proj, "r", axis=0, tiled=True)
    weight_down = lax.all_gather(mlp_down, "r", axis=0, tiled=True)

    tokens_all = jnp.concatenate(token_blocks).astype(F32)
    normed = (tokens_all * inverse_rms(tokens_all) * gain_one).astype(BF)
    kv = mm(normed, weight_kv).astype(BF).reshape(HEADS, rows, 2 * HEAD)
    gate_low = mm(normed, down_full)
    forget = exact(gate_low, up_head) + bias_head
    log_sig = jax.nn.log_sigmoid(forget) / NORMALIZER
    li = jnp.concatenate([mask_all * log_sig, mask_all * -jnp.expm1(log_sig)], axis=1)
    li = li.reshape(HEADS, rows, 2 * SLOTS)
    state, decay = chunk_states(kv, li)
    decay = decay[:, :, :1]
    init = chain_pair(state, decay, True)
    qs = mm(normed, weight_qs).reshape(HEADS, rows, 2 * HEAD)
    gated, mixer_out, probs, mix = mixer_forward(qs, kv, li, init, gain_head8)
    gated = gated.reshape(group, HEAD)
    attn_part = mm(gated, weight_out).astype(BF).reshape(HEADS, rows, D)
    grad_mlp = (mask_all * jnp.concatenate(grad_blocks).astype(F32)).astype(BF)
    attn_out, grad_act = scatter_heads(
        [attn_part[k] for k in range(HEADS)], mm_nt(grad_mlp, weight_down)
    )

    tokens_f = tokens.astype(F32)
    residual = tokens_f + mask_own * attn_out
    scale_two = inverse_rms(residual)
    hat_two = residual * scale_two
    normed_two_own = (hat_two * gain_two).astype(BF)
    two_blocks = gather_heads(normed_two_own)
    normed_two = jnp.concatenate(two_blocks)

    hidden_width = weight_down.shape[0]
    gate_up = mm(normed_two, weight_gu)
    gate_pre, up_pre = gate_up[:, :hidden_width], gate_up[:, hidden_width:]
    hidden = (jax.nn.silu(gate_pre) * up_pre).astype(BF)
    grad_gate = (grad_act * up_pre * silu_slope(gate_pre)).astype(BF)
    grad_up = (grad_act * jax.nn.silu(gate_pre)).astype(BF)
    grad_gu = jnp.concatenate([grad_gate, grad_up], axis=1)
    order = [here ^ k for k in range(HEADS)]
    hops = range(1, copies)
    down_rows = mlp_down.shape[0]

    def down_cut(m):
        return lax.dynamic_slice_in_dim(hidden, (turn ^ m) * down_rows, down_rows, 1)

    down_away = [mm_tn(down_cut(m), grad_mlp).astype(BF) for m in hops]
    grad_gu, *down_away = lax.optimization_barrier((grad_gu,) + tuple(down_away))
    two_view = normed_two.reshape(group, HEADS, copies, shard)
    gu_away = [mm_tn(split_rows(two_view, turn, m, order), grad_gu).astype(BF) for m in hops]
    down_total = sum_copies(lambda: mm_tn(down_cut(0), grad_mlp), down_away)
    down_half = down_rows // 2
    grad_gu, *gu_away, down_total = lax.optimization_barrier((grad_gu, *gu_away, down_total))
    down_near, down_far = inward(down_total[:down_half]), inward(down_total[down_half:])
    two_part = mm_nt(grad_gu, weight_gu).astype(BF).reshape(HEADS, rows, D)
    gu_total = sum_copies(
        lambda: mm_tn(split_rows(two_view, turn, 0, order), after(grad_gu, two_part)), gu_away
    )
    grad_norm_two, gu_total, down_near = scatter_heads(
        [two_part[k] for k in range(HEADS)], gu_total, down_near
    )
    gu_part = lax.psum_scatter(
        gu_total.reshape(HEADS, shard, 2 * hidden_width), "seq", scatter_dimension=0, tiled=True
    )
    down_near = across(down_near)
    gain_two_grad = jnp.sum(grad_norm_two * hat_two, axis=0)
    grad_rows = grad_out.astype(F32)
    grad_resid = grad_rows + norm_back(grad_norm_two * gain_two, hat_two, scale_two)
    grad_attn_own = (mask_own * grad_resid).astype(BF)
    attn_blocks = gather_heads(grad_attn_own)
    mlp_part = mm(hidden, weight_down).astype(BF)
    mlp_part, down_near, down_far, *attn_blocks = lax.optimization_barrier(
        (mlp_part, down_near, down_far) + tuple(attn_blocks)
    )
    down_grad = jnp.concatenate([outward(down_near), outward(across(down_far))])
    grad_attn = jnp.concatenate(attn_blocks)
    mlp_part = mlp_part.reshape(HEADS, rows, D)
    mlp_out = scatter_heads([mlp_part[k] for k in range(HEADS)])
    result = (residual + mask_own * mlp_out).astype(BF)

    grad_gated = mm_nt(grad_attn, weight_out).reshape(HEADS, rows, HEAD)
    grad_qs, grad_kv, grad_li, adjoint, slot_part = mixer_backward(
        qs, kv, li, init, gain_head8, mixer_out, probs, mix, grad_gated
    )
    adjoint, gu_part = lax.optimization_barrier((adjoint, gu_part))
    gu_part = swap_diagonal(gu_part)
    one_view = normed.reshape(group, HEADS, copies, shard)
    one_views = [split_rows(one_view, turn, m, order) for m in range(copies)]
    out_view = gated.reshape(group, 1, copies, shard)
    out_views = [split_rows(out_view, turn, m, [0]) for m in range(copies)]

    def weight_grad(views, right):
        return sum_copies(
            lambda: mm_tn(views[0], right), [mm_tn(views[m], right).astype(BF) for m in hops]
        )

    grad_qs = grad_qs.reshape(group, 2 * HEAD)
    out_total = weight_grad(out_views, grad_attn)
    qs_total = weight_grad(one_views, grad_qs)
    ends = chain_pair(adjoint, decay, False)
    ends, gu_part, out_total, qs_total = lax.optimization_barrier(
        (ends, gu_part, out_total, qs_total)
    )
    gu_whole = lax.all_gather(gu_part, "seq", axis=0, tiled=True)
    qs_total = qs_total.reshape(HEADS, shard, 2 * HEAD)
    out_total, qs_near, qs_far = inward(out_total), inward(qs_total[1::2]), inward(qs_total[0::2])
    grad_kv, grad_li = mixer_finish(kv, li, init, ends, grad_kv, grad_li)
    grad_kv = grad_kv.reshape(group, 2 * HEAD)
    grad_li = grad_li.reshape(group, 2 * SLOTS)
    grad_decay = (
        mask_all
        * (grad_li[:, :SLOTS] - grad_li[:, SLOTS:] * jnp.exp(log_sig))
        / NORMALIZER
        * jax.nn.sigmoid(-forget)
    )
    bias_part = jnp.sum(grad_decay, axis=0)
    up_part = lax.dot_general(
        gate_low, grad_decay, (((0,), (0,)), ((), ())), precision=HIGHEST, preferred_element_type=F32
    )
    grad_low = lax.dot_general(
        grad_decay, up_head, (((1,), (1,)), ((), ())), precision=HIGHEST, preferred_element_type=F32
    ).astype(BF)
    down_low_part = mm_tn(normed, grad_low)

    one_part = (
        (mm_nt(grad_qs, weight_qs) + mm_nt(grad_kv, weight_kv) + mm_nt(grad_low, down_full))
        .astype(BF)
        .reshape(HEADS, rows, D)
    )
    kv_total = weight_grad(one_views, grad_kv)
    grad_norm_one, kv_total, out_total, qs_near, qs_far = scatter_heads(
        [one_part[k] for k in range(HEADS)], kv_total, out_total, qs_near, qs_far
    )
    kv_total = kv_total.reshape(HEADS, shard, 2 * HEAD)
    kv_near, kv_far = inward(kv_total[1::2]), inward(kv_total[0::2])
    out_grad = outward(across(out_total)).astype(F32)
    qs_near, qs_far = outward(across(qs_near)), outward(across(qs_far))
    kv_near, kv_far = outward(across(kv_near)), outward(across(kv_far))
    gate_grad, up_grad = assemble(gu_whole[None], order, 2)
    query_grad, swish_grad = spread_line(qs_near, qs_far, here, 2)
    key_grad, value_grad = spread_line(kv_near, kv_far, here, 2)
    scale_one = inverse_rms(tokens_f)
    hat_one = tokens_f * scale_one
    gain_one_grad = jnp.sum(grad_norm_one * hat_one, axis=0)
    grad_tokens = (grad_resid + norm_back(grad_norm_one * gain_one, hat_one, scale_one)).astype(BF)

    def placed(part, width):
        whole = jnp.zeros(part.shape[:-1] + (HEADS * width,), F32)
        return lax.dynamic_update_slice_in_dim(whole, part, here * width, part.ndim - 1)

    up_sum = placed(up_part, SLOTS).reshape(RANK, HEADS, copies, -1).transpose(1, 2, 0, 3)
    sums = [
        gain_one_grad,
        down_low_part,
        up_sum,
        placed(bias_part, SLOTS),
        placed(slot_part[0], HEAD),
        gain_two_grad,
    ]
    flat = jnp.concatenate([a.reshape(HEADS, copies, -1) for a in sums], axis=2)
    flat = sum_small(flat, here, turn)
    totals, offset = [], 0
    for a in sums:
        size = a.size // owners
        totals.append(flat[offset : offset + size])
        offset += size

    return (
        result,
        grad_tokens,
        totals[0],
        query_grad,
        key_grad,
        value_grad,
        totals[1].reshape(shard, RANK),
        totals[2].reshape(RANK, -1),
        totals[3],
        swish_grad,
        totals[4],
        out_grad,
        totals[5],
        gate_grad,
        up_grad,
        down_grad.astype(F32),
    )


def solution(mesh):
    count, span = mesh.devices.shape
    split = Mesh(mesh.devices.reshape(HEADS, count // HEADS, span), ("p", "r", "seq"))
    rows = P(("p", "r", "seq"), None)
    matrix, vector, last = P(("p", "r"), None), P(("p", "r")), P(None, ("p", "r"))
    in_specs = (
        rows, vector, vector, matrix, matrix, matrix, matrix, last, vector, matrix, vector, matrix,
        vector, matrix, matrix, matrix, rows,
    )
    out_specs = (
        rows, rows, vector, matrix, matrix, matrix, matrix, last, vector, matrix, vector, matrix,
        vector, matrix, matrix, matrix,
    )
    return jax.shard_map(body, mesh=split, in_specs=in_specs, out_specs=out_specs, check_vma=False)
```

```python
import functools
import jax
import jax.numpy as jnp
from jax import lax
from jax.experimental import pallas as pl
from jax.experimental.pallas import tpu as pltpu
from jax.sharding import Mesh, PartitionSpec as P

HEAD = 512
SLOTS = 64
SCALE = HEAD ** (-0.5)
EPSILON = 1e-06
HIGHEST = lax.Precision.HIGHEST
BF = jnp.bfloat16
F32 = jnp.float32


def mm(a, b):
    return lax.dot_general(a, b, (((1,), (0,)), ((), ())), preferred_element_type=F32)


def mm_nt(a, b):
    return lax.dot_general(a, b, (((1,), (1,)), ((), ())), preferred_element_type=F32)


def mm_tn(a, b):
    return lax.dot_general(a, b, (((0,), (0,)), ((), ())), preferred_element_type=F32)


def exact(a, b):
    return lax.dot_general(
        a, b, (((1,), (0,)), ((), ())), precision=HIGHEST, preferred_element_type=F32
    )


def row_bit(rows, level):
    t = lax.broadcasted_iota(jnp.int32, (rows, SLOTS), 0)
    return ((t >> level) & 1) == 1


def prefix_levels(log_decay):
    rows = log_decay.shape[0]
    levels = rows.bit_length() - 1
    f, g = log_decay, jnp.zeros_like(log_decay)
    out = []
    for level in range(levels):
        out.append((f, g))
        total = f + g
        step = 1 << level
        bit = row_bit(rows, level)
        f = f + jnp.where(bit, pltpu.roll(total, step, 0), 0.0)
        g = g + jnp.where(bit, 0.0, pltpu.roll(total, rows - step, 0))
    return out, f, g


def same_block(rows, level):
    t = lax.broadcasted_iota(jnp.int32, (rows, rows), 0)
    s = lax.broadcasted_iota(jnp.int32, (rows, rows), 1)
    return (t >> (level + 1)) == (s >> (level + 1))


def level_mask(table, level, levels):
    if level == levels - 1:
        return table
    return jnp.where(same_block(table.shape[0], level), table, jnp.zeros_like(table))


def factors(pair, level, inflow):
    f, g = pair
    bit = row_bit(f.shape[0], level)
    left = jnp.where(bit, jnp.exp(f), 0.0)
    right = jnp.where(bit, 0.0, jnp.exp(g))
    return left, right, right * inflow


def diagonal(rows):
    t = lax.broadcasted_iota(jnp.int32, (rows, rows), 0)
    s = lax.broadcasted_iota(jnp.int32, (rows, rows), 1)
    return t == s


def slot_table(weights, pairs, inflow):
    rows = weights.shape[0]
    levels = len(pairs)
    table = jnp.where(diagonal(rows), jnp.sum(weights * inflow, axis=1, keepdims=True), 0.0)
    for level in range(levels):
        left, _, gain = factors(pairs[level], level, inflow)
        block = mm_nt((weights * left).astype(BF), gain.astype(BF))
        table = table + level_mask(block, level, levels)
    return table


def slot_sums(table, pairs, inflow):
    rows = table.shape[0]
    levels = len(pairs)
    own = jnp.sum(jnp.where(diagonal(rows), table, 0.0), axis=1, keepdims=True)
    low = table.astype(BF)
    total = own * inflow
    for level in range(levels):
        left, _, gain = factors(pairs[level], level, inflow)
        total = total + left * mm(level_mask(low, level, levels), gain.astype(BF))
    return total


def states_kernel(kv_ref, li_ref, state_ref, decay_ref):
    kv = kv_ref[0]
    log_decay = li_ref[0, :, :SLOTS]
    inflow = li_ref[0, :, SLOTS:]
    rows = kv.shape[0]
    t = lax.broadcasted_iota(jnp.int32, (rows, rows), 0)
    s = lax.broadcasted_iota(jnp.int32, (rows, rows), 1)
    after = exact((s > t).astype(F32), log_decay)
    weight = jnp.exp(after) * inflow
    state_ref[0] = mm_tn(weight.astype(BF), kv)
    total = lax.dot_general(
        log_decay, jnp.ones((rows, 128), F32), (((0,), (0,)), ((), ())),
        precision=HIGHEST, preferred_element_type=F32,
    )
    decay_ref[0] = jnp.exp(total)


def forward_kernel(qs_ref, kv_ref, li_ref, init_ref, gain_ref, gated_ref, out_ref, prob_ref, mix_ref):
    queries = qs_ref[0, :, :HEAD].astype(BF)
    swish = qs_ref[0, :, HEAD:]
    keys = kv_ref[0, :, :HEAD]
    values = kv_ref[0, :, HEAD:]
    log_decay = li_ref[0, :, :SLOTS]
    inflow = li_ref[0, :, SLOTS:]
    init = init_ref[0].astype(BF)
    pairs, running, _ = prefix_levels(log_decay)
    growth = jnp.exp(running)
    scores = mm_nt(queries, keys) * SCALE
    slots = slot_sums(scores, pairs, inflow) + mm_nt(queries, init[:, :HEAD]) * SCALE * growth
    top = jnp.max(slots, axis=1, keepdims=True)
    weights = jnp.exp(slots - top)
    probs = weights / jnp.sum(weights, axis=1, keepdims=True)
    mix = slot_table(probs, pairs, inflow).astype(BF)
    out = mm(mix, values) + mm((probs * growth).astype(BF), init[:, HEAD:])
    hat = out * lax.rsqrt(jnp.mean(out * out, axis=1, keepdims=True) + EPSILON)
    gated_ref[0] = (hat * gain_ref[0:1] * (swish * jax.nn.sigmoid(swish))).astype(BF)
    out_ref[0] = out
    prob_ref[0] = probs
    mix_ref[0] = mix


def backward_kernel(
    qs_ref, kv_ref, li_ref, init_ref, gain_ref, out_ref, prob_ref, mix_ref, gg_ref,
    dqs_ref, dkv_ref, ddi_ref, adj_ref, sg_ref,
):
    queries = qs_ref[0, :, :HEAD].astype(BF)
    swish = qs_ref[0, :, HEAD:]
    keys = kv_ref[0, :, :HEAD]
    values = kv_ref[0, :, HEAD:]
    log_decay = li_ref[0, :, :SLOTS]
    inflow = li_ref[0, :, SLOTS:]
    init = init_ref[0].astype(BF)
    out = out_ref[0]
    probs = prob_ref[0]
    gain = gain_ref[0:1]
    rows = out.shape[0]
    scale_out = lax.rsqrt(jnp.mean(out * out, axis=1, keepdims=True) + EPSILON)
    hat = out * scale_out
    sig = jax.nn.sigmoid(swish)
    silu = swish * sig
    gg = gg_ref[0].astype(F32)
    gg_hat = gg * hat
    dqs_ref[0, :, HEAD:] = (gg_hat * gain * (sig * (1.0 + swish * (1.0 - sig)))).astype(BF)
    part = jnp.broadcast_to(jnp.sum(gg_hat * silu, axis=0, keepdims=True), (8, HEAD))

    @pl.when(pl.program_id(0) == 0)
    def _():
        sg_ref[...] = part

    @pl.when(pl.program_id(0) > 0)
    def _():
        sg_ref[...] = sg_ref[...] + part

    grad_hat = gg * gain * silu
    dout = scale_out * (grad_hat - hat * jnp.mean(grad_hat * hat, axis=1, keepdims=True))
    dout = dout.astype(BF)
    pairs, running, _ = prefix_levels(log_decay)
    levels = len(pairs)
    growth = jnp.exp(running)
    scores = mm_nt(queries, keys) * SCALE
    grads = mm_nt(dout, values)
    key_part = mm_nt(queries, init[:, :HEAD]) * SCALE * growth
    value_part = mm_nt(dout, init[:, HEAD:]) * growth
    dprob = slot_sums(grads, pairs, inflow) + value_part
    dslot = probs * (dprob - jnp.sum(probs * dprob, axis=1, keepdims=True))
    back = slot_table(dslot, pairs, inflow).astype(BF)
    dslot_g = (dslot * growth).astype(BF)
    prob_g = (probs * growth).astype(BF)
    dqs_ref[0, :, :HEAD] = (SCALE * (mm(back, keys) + mm(dslot_g, init[:, :HEAD]))).astype(BF)
    dkv_ref[0, :, :HEAD] = SCALE * mm_tn(back, queries)
    dkv_ref[0, :, HEAD:] = mm_tn(mix_ref[0], dout)
    adj_ref[0, :, :HEAD] = SCALE * mm_tn(dslot_g, queries)
    adj_ref[0, :, HEAD:] = mm_tn(prob_g, dout)
    diag = diagonal(rows)
    own_a = jnp.sum(jnp.where(diag, scores, 0.0), axis=1, keepdims=True)
    own_b = jnp.sum(jnp.where(diag, grads, 0.0), axis=1, keepdims=True)
    dinflow = dslot * own_a + probs * own_b
    scores_low = scores.astype(BF)
    grads_low = grads.astype(BF)
    fbar = dslot * key_part + probs * value_part
    gbar = jnp.zeros_like(fbar)
    for level in range(levels - 1, -1, -1):
        left, right, amount = factors(pairs[level], level, inflow)
        table_a = level_mask(scores_low, level, levels)
        table_b = level_mask(grads_low, level, levels)
        amount_low = amount.astype(BF)
        dleft = dslot * left
        pleft = probs * left
        grow = dleft * mm(table_a, amount_low) + pleft * mm(table_b, amount_low)
        back_in = mm_tn(table_a, dleft.astype(BF)) + mm_tn(table_b, pleft.astype(BF))
        dinflow = dinflow + right * back_in
        step = 1 << level
        bit = row_bit(rows, level)
        total = pltpu.roll(jnp.where(bit, fbar, 0.0), rows - step, 0) + pltpu.roll(
            jnp.where(bit, 0.0, gbar), step, 0
        )
        fbar = fbar + grow + total
        gbar = gbar + amount * back_in + total
    ddi_ref[0, :, :SLOTS] = fbar
    ddi_ref[0, :, SLOTS:] = dinflow


def finish_kernel(kv_ref, li_ref, init_ref, end_ref, dkv_ref, ddi_ref, okv_ref, oddi_ref):
    kv = kv_ref[0]
    log_decay = li_ref[0, :, :SLOTS]
    inflow = li_ref[0, :, SLOTS:]
    end = end_ref[0]
    rows = kv.shape[0]
    t = lax.broadcasted_iota(jnp.int32, (rows, rows), 0)
    s = lax.broadcasted_iota(jnp.int32, (rows, rows), 1)
    earlier = (s < t).astype(F32)
    after = exact((s > t).astype(F32), log_decay)
    fade = jnp.exp(after)
    weight = fade * inflow
    end_low = end.astype(BF)
    okv_ref[0] = (dkv_ref[0] + mm(weight.astype(BF), end_low)).astype(BF)
    reach = mm_nt(kv, end_low)
    whole = jnp.exp(jnp.sum(log_decay, axis=0, keepdims=True))
    carry = lax.dot_general(
        jnp.ones((8, 2 * HEAD), F32), end * init_ref[0], (((1,), (1,)), ((), ())),
        precision=HIGHEST, preferred_element_type=F32,
    )[0:1]
    oddi_ref[0, :, :SLOTS] = (
        ddi_ref[0, :, :SLOTS] + exact(earlier, weight * reach) + whole * carry
    )
    oddi_ref[0, :, SLOTS:] = ddi_ref[0, :, SLOTS:] + fade * reach


def blocked(shape):
    return pl.BlockSpec((1,) + shape, lambda i: (i, 0, 0))


def run(kernel, args, specs, outs, out_specs, flops, moved):
    return pl.pallas_call(
        kernel,
        grid=(args[0].shape[0],),
        in_specs=specs,
        out_specs=out_specs,
        out_shape=outs,
        cost_estimate=pl.CostEstimate(flops=flops, bytes_accessed=moved, transcendentals=0),
        compiler_params=pltpu.CompilerParams(vmem_limit_bytes=56 << 20),
    )(*args)


def sds(shape, dtype=F32):
    return jax.ShapeDtypeStruct(shape, dtype)


def chunk_states(kv, li):
    n, rows, _ = kv.shape
    return run(
        states_kernel, (kv, li),
        [blocked((rows, 2 * HEAD)), blocked((rows, 2 * SLOTS))],
        (sds((n, SLOTS, 2 * HEAD)), sds((n, SLOTS, 128))),
        (blocked((SLOTS, 2 * HEAD)), blocked((SLOTS, 128))),
        n * 10**9, n * 10**6,
    )


def mixer_forward(qs, kv, li, init, gain):
    n, rows, _ = kv.shape
    return run(
        forward_kernel, (qs, kv, li, init, gain),
        [blocked((rows, 2 * HEAD)), blocked((rows, 2 * HEAD)), blocked((rows, 2 * SLOTS)),
         blocked((SLOTS, 2 * HEAD)), pl.BlockSpec((8, HEAD), lambda i: (0, 0))],
        (sds((n, rows, HEAD), BF), sds((n, rows, HEAD)), sds((n, rows, SLOTS)), sds((n, rows, rows), BF)),
        (blocked((rows, HEAD)), blocked((rows, HEAD)), blocked((rows, SLOTS)), blocked((rows, rows))),
        n * 3 * 10**9, n * 4 * 10**6,
    )


def mixer_backward(qs, kv, li, init, gain, out, probs, mix, gg):
    n, rows, _ = kv.shape
    return run(
        backward_kernel, (qs, kv, li, init, gain, out, probs, mix, gg),
        [blocked((rows, 2 * HEAD)), blocked((rows, 2 * HEAD)), blocked((rows, 2 * SLOTS)),
         blocked((SLOTS, 2 * HEAD)), pl.BlockSpec((8, HEAD), lambda i: (0, 0)),
         blocked((rows, HEAD)), blocked((rows, SLOTS)), blocked((rows, rows)), blocked((rows, HEAD))],
        (sds((n, rows, 2 * HEAD), BF), sds((n, rows, 2 * HEAD)), sds((n, rows, 2 * SLOTS)),
         sds((n, SLOTS, 2 * HEAD)), sds((8, HEAD))),
        (blocked((rows, 2 * HEAD)), blocked((rows, 2 * HEAD)), blocked((rows, 2 * SLOTS)),
         blocked((SLOTS, 2 * HEAD)), pl.BlockSpec((8, HEAD), lambda i: (0, 0))),
        n * 6 * 10**9, n * 5 * 10**6,
    )


def mixer_finish(kv, li, init, end, dkv, ddi):
    n, rows, _ = kv.shape
    return run(
        finish_kernel, (kv, li, init, end, dkv, ddi),
        [blocked((rows, 2 * HEAD)), blocked((rows, 2 * SLOTS)), blocked((SLOTS, 2 * HEAD)),
         blocked((SLOTS, 2 * HEAD)), blocked((rows, 2 * HEAD)), blocked((rows, 2 * SLOTS))],
        (sds((n, rows, 2 * HEAD), BF), sds((n, rows, 2 * SLOTS))),
        (blocked((rows, 2 * HEAD)), blocked((rows, 2 * SLOTS))),
        n * 10**9, n * 3 * 10**6,
    )


D = 2048
HEADS = 4
RANK = 16
NORMALIZER = 8.0


def inverse_rms(values):
    return lax.rsqrt(jnp.mean(values * values, axis=-1, keepdims=True) + EPSILON)


def silu_slope(values):
    sigmoid_val = jax.nn.sigmoid(values)
    return sigmoid_val * (1.0 + values * (1.0 - sigmoid_val))


def norm_back(grad_hat, hat_rows, scale_rows):
    return scale_rows * (
        grad_hat - hat_rows * jnp.mean(grad_hat * hat_rows, axis=-1, keepdims=True)
    )


def swap(value, axis, step):
    count = lax.axis_size(axis)
    return lax.ppermute(value, axis, [(i, i ^ step) for i in range(count)])


def gather_heads(block):
    return [block] + [swap(block, "p", k) for k in range(1, HEADS)]


def scatter_heads(parts, *fillers):
    got = [swap(parts[k], "p", k) for k in range(1, HEADS)]
    if fillers:
        held = lax.optimization_barrier(tuple(got) + fillers)
        got, fillers = held[: HEADS - 1], held[HEADS - 1 :]
    total = parts[0].astype(F32)
    for part in got:
        total = total + part.astype(F32)
    return (total,) + tuple(fillers) if fillers else total


def after(value, *others):
    return lax.optimization_barrier((value,) + others)[0]


def place_kernel(blocks, spot_ref, *refs):
    ins, out = refs[:-1], refs[-1]
    part = ins[0].shape[1]
    for i, ref in enumerate(ins):
        for k in range(blocks):
            start = pl.multiple_of(spot_ref[i * blocks + k] * part, part)
            out[pl.ds(start, part), :] = ref[k]


def place(parts, spots):
    blocks, part, width = parts[0].shape
    chunk = 256
    table = jnp.stack([jnp.asarray(x, jnp.int32) for row in spots for x in row])
    rows = len(parts) * blocks * part
    return pl.pallas_call(
        functools.partial(place_kernel, blocks),
        grid_spec=pltpu.PrefetchScalarGridSpec(
            num_scalar_prefetch=1,
            grid=(width // chunk,),
            in_specs=[pl.BlockSpec((blocks, part, chunk), lambda i, s: (0, 0, i))] * len(parts),
            out_specs=pl.BlockSpec((rows, chunk), lambda i, s: (0, i)),
        ),
        out_shape=jax.ShapeDtypeStruct((rows, width), BF),
        cost_estimate=pl.CostEstimate(flops=0, bytes_accessed=4 * rows * width, transcendentals=0),
        compiler_params=pltpu.CompilerParams(vmem_limit_bytes=56 << 20),
    )(table, *parts)


def column_cuts(shards, here, k):
    cuts = []
    for shard in shards:
        width = shard.shape[1] // HEADS
        cuts.append(lax.dynamic_slice_in_dim(shard, (here ^ k) * width, width, 1))
    return jnp.concatenate(cuts, axis=1)


def head_columns(shards, here):
    copies = lax.axis_size("r")
    turn = lax.axis_index("r")
    own = column_cuts(shards, here, 0)
    pieces = [own] + [swap(column_cuts(shards, here, k), "p", k) for k in range(1, HEADS)]
    parts, spots = [], []
    for k in range(HEADS):
        for m in range(copies):
            piece = pieces[k] if m == 0 else swap(pieces[k], "r", m)
            parts.append(piece[None])
            spots.append([(here ^ k) * copies + (turn ^ m)])
    return place(parts, spots), pieces[1:]


def head_columns_seq(shards, here):
    copies, count = lax.axis_size("r"), lax.axis_size("seq")
    turn, spot = lax.axis_index("r"), lax.axis_index("seq")
    rows = shards[0].shape[0] // count
    shards = [lax.dynamic_slice_in_dim(shard, spot * rows, rows, 0) for shard in shards]
    own = column_cuts(shards, here, 0)
    pieces = [own] + [swap(column_cuts(shards, here, k), "p", k) for k in range(1, HEADS)]
    parts, spots = [], []
    for j, part in enumerate(gather_seq(jnp.stack(pieces))):
        for m in range(copies):
            parts.append(part if m == 0 else swap(part, "r", m))
            spots.append(
                [(((here ^ k) * copies + (turn ^ m)) * count + (spot ^ j)) for k in range(HEADS)]
            )
    return place(parts, spots), pieces[1:]


def gather_small(packed, here, turn):
    copies = lax.axis_size("r")
    near = jnp.concatenate([packed] + [swap(packed, "r", m) for m in range(1, copies)])
    both = jnp.concatenate(gather_heads(near))
    heads = jnp.arange(HEADS, dtype=jnp.int32) ^ here
    turns = jnp.arange(copies, dtype=jnp.int32) ^ turn
    order = (heads[:, None] * copies + turns[None, :]).reshape(-1)
    return jnp.take(both, order, axis=0)


def sum_small(value, here, turn):
    mine = [lax.dynamic_index_in_dim(value, here ^ k, 0, False) for k in range(HEADS)]
    total = scatter_heads(mine)
    copies = lax.axis_size("r")
    kept = lax.dynamic_index_in_dim(total, turn, 0, True)
    for m in range(1, copies):
        kept = kept + swap(lax.dynamic_index_in_dim(total, turn ^ m, 0, True), "r", m)
    step = 1
    while step < lax.axis_size("seq"):
        kept = kept + swap(kept, "seq", step)
        step *= 2
    return kept[0]


def chain(state, decay, forward):
    count = lax.axis_size("seq")
    total = jnp.zeros_like(state)
    for hop in range(count - 1):
        pair = (hop, hop + 1) if forward else (count - 1 - hop, count - 2 - hop)
        sent = (decay * total + state).astype(BF)
        total = total + lax.ppermute(sent, "seq", [pair]).astype(F32)
    return total


def chain_pair(both, decay, forward):
    return jnp.concatenate(
        [chain(both[..., :HEAD], decay, forward), chain(both[..., HEAD:], decay, forward)], axis=-1
    )


def split_rows(left, turn, step, groups):
    copies, width = left.shape[2:]
    flat = left.reshape(left.shape[0], -1)
    cuts = [
        lax.dynamic_slice_in_dim(flat, (g * copies + (turn ^ step)) * width, width, 1)
        for g in groups
    ]
    return jnp.concatenate(cuts, axis=1)


def sum_copies(own, away):
    got = [swap(part, "r", m + 1) for m, part in enumerate(away)]
    total = own()
    for part in got:
        total = total + part.astype(F32)
    return total.astype(BF)


def gather_seq(value):
    count = lax.axis_size("seq")
    found = {0: value}
    step = count // 2
    while step >= 1:
        for j in list(found):
            found[j ^ step] = swap(found[j], "seq", step)
        step //= 2
    return [found[j] for j in range(count)]


def assemble_kernel(counts, spot_ref, *refs):
    n_in, n_out, part = counts
    ins, outs = refs[:n_in], refs[n_in:]
    width = outs[0].shape[1]
    for j in range(n_in):
        for o in range(n_out):
            cut = ins[j][0, :, o * width : (o + 1) * width]
            outs[o][j * part : (j + 1) * part, :] = cut.astype(F32)


def assemble(parts, columns, n_out):
    spans, blocks, part, width = parts.shape
    width //= n_out
    rows = part * spans
    spots = jnp.stack([jnp.asarray(c, jnp.int32) for c in columns])
    return pl.pallas_call(
        functools.partial(assemble_kernel, (spans, n_out, part)),
        grid_spec=pltpu.PrefetchScalarGridSpec(
            num_scalar_prefetch=1,
            grid=(blocks,),
            in_specs=[
                pl.BlockSpec((None, 1, part, n_out * width), lambda i, s, j=j: (j, i, 0, 0))
                for j in range(spans)
            ],
            out_specs=[pl.BlockSpec((rows, width), lambda i, s: (0, s[i]))] * n_out,
        ),
        out_shape=[jax.ShapeDtypeStruct((rows, blocks * width), F32)] * n_out,
        cost_estimate=pl.CostEstimate(
            flops=0, bytes_accessed=6 * n_out * rows * blocks * width, transcendentals=0
        ),
        compiler_params=pltpu.CompilerParams(vmem_limit_bytes=56 << 20),
    )(spots, *([parts] * spans))


def inward(value):
    count = lax.axis_size("seq")
    for i in range(count // 2 - 1):
        value = value + lax.ppermute(value, "seq", [(i, i + 1), (count - 1 - i, count - 2 - i)])
    return value


def across(value):
    half = lax.axis_size("seq") // 2
    return value + lax.ppermute(value, "seq", [(half - 1, half), (half, half - 1)])


def outward(total):
    count, spot = lax.axis_size("seq"), lax.axis_index("seq")
    for i in range(count // 2 - 2, -1, -1):
        got = lax.ppermute(total, "seq", [(i + 1, i), (count - 2 - i, count - 1 - i)])
        total = jnp.where((spot == i) | (spot == count - 1 - i), got, total)
    return total


def spread_line(near, far, here, n_out):
    got = [far[0], swap(near[0], "p", 1), swap(far[1], "p", 2), swap(near[1], "p", 3)]
    return assemble(jnp.stack(got)[None], [here ^ k for k in range(HEADS)], n_out)


def swap_diagonal(part):
    count = lax.axis_size("seq")
    sends = [(p * count + z, (p ^ z) * count + z) for p in range(HEADS) for z in range(count)]
    return lax.ppermute(part, ("p", "seq"), sends)


def body(
    tokens,
    seq_lengths,
    attn_gain,
    query_proj,
    key_proj,
    value_proj,
    decay_down,
    decay_up,
    decay_bias,
    swish_proj,
    slot_gain,
    out_proj,
    mlp_gain,
    mlp_gate,
    mlp_up,
    mlp_down,
    grad_out,
):
    rows = tokens.shape[0]
    copies = lax.axis_size("r")
    owners = HEADS * copies
    shard = D // owners
    here, turn, place = lax.axis_index("p"), lax.axis_index("r"), lax.axis_index("seq")
    group = HEADS * rows

    small = [attn_gain, decay_down, decay_up, decay_bias, slot_gain, mlp_gain, seq_lengths]
    packed = jnp.concatenate([a.astype(F32).reshape(-1) for a in small])
    packed = gather_small(packed[None], here, turn)
    fields, offset = [], 0
    for a in small:
        fields.append(packed[:, offset : offset + a.size])
        offset += a.size
    gain_one = fields[0].reshape(D)
    down_full = fields[1].reshape(D, RANK).astype(BF)
    up_full = fields[2].reshape(owners, RANK, -1).transpose(1, 0, 2).reshape(RANK, HEADS * SLOTS)
    up_head = lax.dynamic_slice_in_dim(up_full, here * SLOTS, SLOTS, 1)
    bias_head = lax.dynamic_slice_in_dim(fields[3].reshape(HEADS * SLOTS), here * SLOTS, SLOTS, 0)
    gain_head = lax.dynamic_slice_in_dim(fields[4].reshape(D), here * HEAD, HEAD, 0)
    gain_head8 = jnp.broadcast_to(gain_head[None], (8, HEAD))
    gain_two = fields[5].reshape(D)
    lengths = fields[6].reshape(HEADS, copies)
    positions = (place * rows + jnp.arange(rows, dtype=jnp.int32)).astype(F32)
    masks = [
        (positions < lax.dynamic_index_in_dim(lengths, here ^ k, 0, False)[turn]).astype(F32)
        for k in range(HEADS)
    ]
    mask_all = jnp.concatenate(masks)[:, None]
    mask_own = masks[0][:, None]

    token_blocks = gather_heads(tokens)
    weight_kv, kv_pieces = head_columns([key_proj, value_proj], here)
    late = lax.optimization_barrier((query_proj, swish_proj, mlp_gate, mlp_up) + tuple(kv_pieces))
    weight_qs, qs_pieces = head_columns(late[:2], here)
    weight_gu, gu_pieces = head_columns_seq(late[2:4], here)
    grad_blocks = gather_heads(after(grad_out, *qs_pieces))
    weight_out = lax.all_gather(out_proj, "r", axis=0, tiled=True)
    weight_down = lax.all_gather(mlp_down, "r", axis=0, tiled=True)

    tokens_all = jnp.concatenate(token_blocks).astype(F32)
    normed = (tokens_all * inverse_rms(tokens_all) * gain_one).astype(BF)
    kv = mm(normed, weight_kv).astype(BF).reshape(HEADS, rows, 2 * HEAD)
    gate_low = mm(normed, down_full)
    forget = exact(gate_low, up_head) + bias_head
    log_sig = jax.nn.log_sigmoid(forget) / NORMALIZER
    li = jnp.concatenate([mask_all * log_sig, mask_all * -jnp.expm1(log_sig)], axis=1)
    li = li.reshape(HEADS, rows, 2 * SLOTS)
    state, decay = chunk_states(kv, li)
    decay = decay[:, :, :1]
    init = chain_pair(state, decay, True)
    qs = mm(normed, weight_qs).reshape(HEADS, rows, 2 * HEAD)
    gated, mixer_out, probs, mix = mixer_forward(qs, kv, li, init, gain_head8)
    gated = gated.reshape(group, HEAD)
    attn_part = mm(gated, weight_out).astype(BF).reshape(HEADS, rows, D)
    grad_mlp = (mask_all * jnp.concatenate(grad_blocks).astype(F32)).astype(BF)
    attn_out, grad_act = scatter_heads(
        [attn_part[k] for k in range(HEADS)], mm_nt(grad_mlp, weight_down)
    )

    tokens_f = tokens.astype(F32)
    residual = tokens_f + mask_own * attn_out
    scale_two = inverse_rms(residual)
    hat_two = residual * scale_two
    normed_two_own = (hat_two * gain_two).astype(BF)
    two_blocks = gather_heads(normed_two_own)

    hidden_width = weight_down.shape[0]
    hidden, grad_gu, two_parts = [], [], []
    for k in range(HEADS):
        block = two_blocks[k] if k == 0 else after(two_blocks[k], two_parts[-1])
        gate_up = mm(block, weight_gu)
        gate_pre, up_pre = gate_up[:, :hidden_width], gate_up[:, hidden_width:]
        grad_cut = grad_act[k * rows : (k + 1) * rows]
        hidden.append((jax.nn.silu(gate_pre) * up_pre).astype(BF))
        grad_gate = (grad_cut * up_pre * silu_slope(gate_pre)).astype(BF)
        grad_up = (grad_cut * jax.nn.silu(gate_pre)).astype(BF)
        grad_gu.append(jnp.concatenate([grad_gate, grad_up], axis=1))
        two_parts.append(mm_nt(grad_gu[k], weight_gu).astype(BF))
    two_got = [swap(two_parts[k], "p", k) for k in range(1, HEADS)]
    normed_two = jnp.concatenate(two_blocks)
    hidden, grad_gu = jnp.concatenate(hidden), jnp.concatenate(grad_gu)
    order = [here ^ k for k in range(HEADS)]
    hops = range(1, copies)
    down_rows = mlp_down.shape[0]

    def down_cut(m):
        return lax.dynamic_slice_in_dim(hidden, (turn ^ m) * down_rows, down_rows, 1)

    hidden, grad_gu = lax.optimization_barrier((hidden, grad_gu, two_got[0], *two_parts))[:2]
    down_away = [mm_tn(down_cut(m), grad_mlp).astype(BF) for m in hops]
    grad_gu, *down_away = lax.optimization_barrier((grad_gu,) + tuple(down_away))
    two_view = normed_two.reshape(group, HEADS, copies, shard)
    gu_away = [mm_tn(split_rows(two_view, turn, m, order), grad_gu).astype(BF) for m in hops]
    hidden, *gu_away = lax.optimization_barrier((hidden, *gu_away, two_got[1]))[:copies]
    down_total = sum_copies(lambda: mm_tn(down_cut(0), grad_mlp), down_away)
    grad_gu, *gu_away, down_total = lax.optimization_barrier((grad_gu, *gu_away, down_total))
    down_part = lax.psum_scatter(down_total, "seq", scatter_dimension=0, tiled=True)
    gu_total = sum_copies(lambda: mm_tn(split_rows(two_view, turn, 0, order), grad_gu), gu_away)
    *two_got, gu_total, down_part = lax.optimization_barrier((*two_got, gu_total, down_part))
    grad_norm_two = two_parts[0].astype(F32)
    for part in two_got:
        grad_norm_two = grad_norm_two + part.astype(F32)
    gu_part = lax.psum_scatter(
        gu_total.reshape(HEADS, shard, 2 * hidden_width), "seq", scatter_dimension=0, tiled=True
    )
    gain_two_grad = jnp.sum(grad_norm_two * hat_two, axis=0)
    grad_rows = grad_out.astype(F32)
    grad_resid = grad_rows + norm_back(grad_norm_two * gain_two, hat_two, scale_two)
    grad_attn_own = (mask_own * grad_resid).astype(BF)
    attn_blocks = gather_heads(grad_attn_own)
    mlp_part = mm(hidden, weight_down).astype(BF)
    mlp_part, *attn_blocks = lax.optimization_barrier((mlp_part,) + tuple(attn_blocks))
    grad_attn = jnp.concatenate(attn_blocks)
    mlp_part = mlp_part.reshape(HEADS, rows, D)
    mlp_out = scatter_heads([mlp_part[k] for k in range(HEADS)])
    result = (residual + mask_own * mlp_out).astype(BF)

    grad_gated = mm_nt(grad_attn, weight_out).reshape(HEADS, rows, HEAD)
    grad_qs, grad_kv, grad_li, adjoint, slot_part = mixer_backward(
        qs, kv, li, init, gain_head8, mixer_out, probs, mix, grad_gated
    )
    adjoint, gu_part = lax.optimization_barrier((adjoint, gu_part))
    gu_part = swap_diagonal(gu_part)
    one_view = normed.reshape(group, HEADS, copies, shard)
    one_views = [split_rows(one_view, turn, m, order) for m in range(copies)]
    out_view = gated.reshape(group, 1, copies, shard)
    out_views = [split_rows(out_view, turn, m, [0]) for m in range(copies)]

    def weight_grad(views, right):
        return sum_copies(
            lambda: mm_tn(views[0], right), [mm_tn(views[m], right).astype(BF) for m in hops]
        )

    grad_qs = grad_qs.reshape(group, 2 * HEAD)
    out_total = weight_grad(out_views, grad_attn)
    qs_total = weight_grad(one_views, grad_qs)
    ends = chain_pair(adjoint, decay, False)
    ends, gu_part, down_part, out_total, qs_total = lax.optimization_barrier(
        (ends, gu_part, down_part, out_total, qs_total)
    )
    gu_whole = lax.all_gather(gu_part, "seq", axis=0, tiled=True)
    down_grad = lax.all_gather(after(down_part, ends), "seq", axis=0, tiled=True)
    qs_total = qs_total.reshape(HEADS, shard, 2 * HEAD)
    out_total, qs_near, qs_far = inward(out_total), inward(qs_total[1::2]), inward(qs_total[0::2])
    grad_kv, grad_li = mixer_finish(kv, li, init, ends, grad_kv, grad_li)
    grad_kv = grad_kv.reshape(group, 2 * HEAD)
    grad_li = grad_li.reshape(group, 2 * SLOTS)
    grad_decay = (
        mask_all
        * (grad_li[:, :SLOTS] - grad_li[:, SLOTS:] * jnp.exp(log_sig))
        / NORMALIZER
        * jax.nn.sigmoid(-forget)
    )
    bias_part = jnp.sum(grad_decay, axis=0)
    up_part = lax.dot_general(
        gate_low, grad_decay, (((0,), (0,)), ((), ())), precision=HIGHEST, preferred_element_type=F32
    )
    grad_low = lax.dot_general(
        grad_decay, up_head, (((1,), (1,)), ((), ())), precision=HIGHEST, preferred_element_type=F32
    ).astype(BF)
    down_low_part = mm_tn(normed, grad_low)

    one_part = (
        (mm_nt(grad_qs, weight_qs) + mm_nt(grad_kv, weight_kv) + mm_nt(grad_low, down_full))
        .astype(BF)
        .reshape(HEADS, rows, D)
    )
    kv_total = weight_grad(one_views, grad_kv)
    grad_norm_one, kv_total, out_total, qs_near, qs_far = scatter_heads(
        [one_part[k] for k in range(HEADS)], kv_total, out_total, qs_near, qs_far
    )
    kv_total = kv_total.reshape(HEADS, shard, 2 * HEAD)
    kv_near, kv_far = inward(kv_total[1::2]), inward(kv_total[0::2])
    out_grad = outward(across(out_total)).astype(F32)
    qs_near, qs_far = outward(across(qs_near)), outward(across(qs_far))
    kv_near, kv_far = outward(across(kv_near)), outward(across(kv_far))
    gate_grad, up_grad = assemble(gu_whole[None], order, 2)
    query_grad, swish_grad = spread_line(qs_near, qs_far, here, 2)
    key_grad, value_grad = spread_line(kv_near, kv_far, here, 2)
    scale_one = inverse_rms(tokens_f)
    hat_one = tokens_f * scale_one
    gain_one_grad = jnp.sum(grad_norm_one * hat_one, axis=0)
    grad_tokens = (grad_resid + norm_back(grad_norm_one * gain_one, hat_one, scale_one)).astype(BF)

    def placed(part, width):
        whole = jnp.zeros(part.shape[:-1] + (HEADS * width,), F32)
        return lax.dynamic_update_slice_in_dim(whole, part, here * width, part.ndim - 1)

    up_sum = placed(up_part, SLOTS).reshape(RANK, HEADS, copies, -1).transpose(1, 2, 0, 3)
    sums = [
        gain_one_grad,
        down_low_part,
        up_sum,
        placed(bias_part, SLOTS),
        placed(slot_part[0], HEAD),
        gain_two_grad,
    ]
    flat = jnp.concatenate([a.reshape(HEADS, copies, -1) for a in sums], axis=2)
    flat = sum_small(flat, here, turn)
    totals, offset = [], 0
    for a in sums:
        size = a.size // owners
        totals.append(flat[offset : offset + size])
        offset += size

    return (
        result,
        grad_tokens,
        totals[0],
        query_grad,
        key_grad,
        value_grad,
        totals[1].reshape(shard, RANK),
        totals[2].reshape(RANK, -1),
        totals[3],
        swish_grad,
        totals[4],
        out_grad,
        totals[5],
        gate_grad,
        up_grad,
        down_grad.astype(F32),
    )


def solution(mesh):
    count, span = mesh.devices.shape
    split = Mesh(mesh.devices.reshape(HEADS, count // HEADS, span), ("p", "r", "seq"))
    rows = P(("p", "r", "seq"), None)
    matrix, vector, last = P(("p", "r"), None), P(("p", "r")), P(None, ("p", "r"))
    in_specs = (
        rows, vector, vector, matrix, matrix, matrix, matrix, last, vector, matrix, vector, matrix,
        vector, matrix, matrix, matrix, rows,
    )
    out_specs = (
        rows, rows, vector, matrix, matrix, matrix, matrix, last, vector, matrix, vector, matrix,
        vector, matrix, matrix, matrix,
    )
    return jax.shard_map(body, mesh=split, in_specs=in_specs, out_specs=out_specs, check_vma=False)
```

```python
import functools
import jax
import jax.numpy as jnp
from jax import lax
from jax.experimental import pallas as pl
from jax.experimental.pallas import tpu as pltpu
from jax.sharding import Mesh, PartitionSpec as P

HEAD = 512
SLOTS = 64
SCALE = HEAD ** (-0.5)
EPSILON = 1e-06
HIGHEST = lax.Precision.HIGHEST
BF = jnp.bfloat16
F32 = jnp.float32


def mm(a, b):
    return lax.dot_general(a, b, (((1,), (0,)), ((), ())), preferred_element_type=F32)


def mm_nt(a, b):
    return lax.dot_general(a, b, (((1,), (1,)), ((), ())), preferred_element_type=F32)


def mm_tn(a, b):
    return lax.dot_general(a, b, (((0,), (0,)), ((), ())), preferred_element_type=F32)


def exact(a, b):
    return lax.dot_general(
        a, b, (((1,), (0,)), ((), ())), precision=HIGHEST, preferred_element_type=F32
    )


def row_bit(rows, level):
    t = lax.broadcasted_iota(jnp.int32, (rows, SLOTS), 0)
    return ((t >> level) & 1) == 1


def prefix_levels(log_decay):
    rows = log_decay.shape[0]
    levels = rows.bit_length() - 1
    f, g = log_decay, jnp.zeros_like(log_decay)
    out = []
    for level in range(levels):
        out.append((f, g))
        total = f + g
        step = 1 << level
        bit = row_bit(rows, level)
        f = f + jnp.where(bit, pltpu.roll(total, step, 0), 0.0)
        g = g + jnp.where(bit, 0.0, pltpu.roll(total, rows - step, 0))
    return out, f, g


def same_block(rows, level):
    t = lax.broadcasted_iota(jnp.int32, (rows, rows), 0)
    s = lax.broadcasted_iota(jnp.int32, (rows, rows), 1)
    return (t >> (level + 1)) == (s >> (level + 1))


def level_mask(table, level, levels):
    if level == levels - 1:
        return table
    return jnp.where(same_block(table.shape[0], level), table, jnp.zeros_like(table))


def factors(pair, level, inflow):
    f, g = pair
    bit = row_bit(f.shape[0], level)
    left = jnp.where(bit, jnp.exp(f), 0.0)
    right = jnp.where(bit, 0.0, jnp.exp(g))
    return left, right, right * inflow


def diagonal(rows):
    t = lax.broadcasted_iota(jnp.int32, (rows, rows), 0)
    s = lax.broadcasted_iota(jnp.int32, (rows, rows), 1)
    return t == s


def slot_table(weights, pairs, inflow):
    rows = weights.shape[0]
    levels = len(pairs)
    table = jnp.where(diagonal(rows), jnp.sum(weights * inflow, axis=1, keepdims=True), 0.0)
    for level in range(levels):
        left, _, gain = factors(pairs[level], level, inflow)
        block = mm_nt((weights * left).astype(BF), gain.astype(BF))
        table = table + level_mask(block, level, levels)
    return table


def slot_sums(table, pairs, inflow):
    rows = table.shape[0]
    levels = len(pairs)
    own = jnp.sum(jnp.where(diagonal(rows), table, 0.0), axis=1, keepdims=True)
    low = table.astype(BF)
    total = own * inflow
    for level in range(levels):
        left, _, gain = factors(pairs[level], level, inflow)
        total = total + left * mm(level_mask(low, level, levels), gain.astype(BF))
    return total


def states_kernel(kv_ref, li_ref, state_ref, decay_ref):
    kv = kv_ref[0]
    log_decay = li_ref[0, :, :SLOTS]
    inflow = li_ref[0, :, SLOTS:]
    rows = kv.shape[0]
    t = lax.broadcasted_iota(jnp.int32, (rows, rows), 0)
    s = lax.broadcasted_iota(jnp.int32, (rows, rows), 1)
    after = exact((s > t).astype(F32), log_decay)
    weight = jnp.exp(after) * inflow
    state_ref[0] = mm_tn(weight.astype(BF), kv)
    total = lax.dot_general(
        log_decay, jnp.ones((rows, 128), F32), (((0,), (0,)), ((), ())),
        precision=HIGHEST, preferred_element_type=F32,
    )
    decay_ref[0] = jnp.exp(total)


def forward_kernel(qs_ref, kv_ref, li_ref, init_ref, gain_ref, gated_ref, out_ref, prob_ref, mix_ref):
    queries = qs_ref[0, :, :HEAD].astype(BF)
    swish = qs_ref[0, :, HEAD:]
    keys = kv_ref[0, :, :HEAD]
    values = kv_ref[0, :, HEAD:]
    log_decay = li_ref[0, :, :SLOTS]
    inflow = li_ref[0, :, SLOTS:]
    init = init_ref[0].astype(BF)
    pairs, running, _ = prefix_levels(log_decay)
    growth = jnp.exp(running)
    scores = mm_nt(queries, keys) * SCALE
    slots = slot_sums(scores, pairs, inflow) + mm_nt(queries, init[:, :HEAD]) * SCALE * growth
    top = jnp.max(slots, axis=1, keepdims=True)
    weights = jnp.exp(slots - top)
    probs = weights / jnp.sum(weights, axis=1, keepdims=True)
    mix = slot_table(probs, pairs, inflow).astype(BF)
    out = mm(mix, values) + mm((probs * growth).astype(BF), init[:, HEAD:])
    hat = out * lax.rsqrt(jnp.mean(out * out, axis=1, keepdims=True) + EPSILON)
    gated_ref[0] = (hat * gain_ref[0:1] * (swish * jax.nn.sigmoid(swish))).astype(BF)
    out_ref[0] = out
    prob_ref[0] = probs
    mix_ref[0] = mix


def backward_kernel(
    qs_ref, kv_ref, li_ref, init_ref, gain_ref, out_ref, prob_ref, mix_ref, gg_ref,
    dqs_ref, dkv_ref, ddi_ref, adj_ref, sg_ref,
):
    queries = qs_ref[0, :, :HEAD].astype(BF)
    swish = qs_ref[0, :, HEAD:]
    keys = kv_ref[0, :, :HEAD]
    values = kv_ref[0, :, HEAD:]
    log_decay = li_ref[0, :, :SLOTS]
    inflow = li_ref[0, :, SLOTS:]
    init = init_ref[0].astype(BF)
    out = out_ref[0]
    probs = prob_ref[0]
    gain = gain_ref[0:1]
    rows = out.shape[0]
    scale_out = lax.rsqrt(jnp.mean(out * out, axis=1, keepdims=True) + EPSILON)
    hat = out * scale_out
    sig = jax.nn.sigmoid(swish)
    silu = swish * sig
    gg = gg_ref[0].astype(F32)
    gg_hat = gg * hat
    dqs_ref[0, :, HEAD:] = (gg_hat * gain * (sig * (1.0 + swish * (1.0 - sig)))).astype(BF)
    part = jnp.broadcast_to(jnp.sum(gg_hat * silu, axis=0, keepdims=True), (8, HEAD))

    @pl.when(pl.program_id(0) == 0)
    def _():
        sg_ref[...] = part

    @pl.when(pl.program_id(0) > 0)
    def _():
        sg_ref[...] = sg_ref[...] + part

    grad_hat = gg * gain * silu
    dout = scale_out * (grad_hat - hat * jnp.mean(grad_hat * hat, axis=1, keepdims=True))
    dout = dout.astype(BF)
    pairs, running, _ = prefix_levels(log_decay)
    levels = len(pairs)
    growth = jnp.exp(running)
    scores = mm_nt(queries, keys) * SCALE
    grads = mm_nt(dout, values)
    key_part = mm_nt(queries, init[:, :HEAD]) * SCALE * growth
    value_part = mm_nt(dout, init[:, HEAD:]) * growth
    dprob = slot_sums(grads, pairs, inflow) + value_part
    dslot = probs * (dprob - jnp.sum(probs * dprob, axis=1, keepdims=True))
    back = slot_table(dslot, pairs, inflow).astype(BF)
    dslot_g = (dslot * growth).astype(BF)
    prob_g = (probs * growth).astype(BF)
    dqs_ref[0, :, :HEAD] = (SCALE * (mm(back, keys) + mm(dslot_g, init[:, :HEAD]))).astype(BF)
    dkv_ref[0, :, :HEAD] = SCALE * mm_tn(back, queries)
    dkv_ref[0, :, HEAD:] = mm_tn(mix_ref[0], dout)
    adj_ref[0, :, :HEAD] = SCALE * mm_tn(dslot_g, queries)
    adj_ref[0, :, HEAD:] = mm_tn(prob_g, dout)
    diag = diagonal(rows)
    own_a = jnp.sum(jnp.where(diag, scores, 0.0), axis=1, keepdims=True)
    own_b = jnp.sum(jnp.where(diag, grads, 0.0), axis=1, keepdims=True)
    dinflow = dslot * own_a + probs * own_b
    scores_low = scores.astype(BF)
    grads_low = grads.astype(BF)
    fbar = dslot * key_part + probs * value_part
    gbar = jnp.zeros_like(fbar)
    for level in range(levels - 1, -1, -1):
        left, right, amount = factors(pairs[level], level, inflow)
        table_a = level_mask(scores_low, level, levels)
        table_b = level_mask(grads_low, level, levels)
        amount_low = amount.astype(BF)
        dleft = dslot * left
        pleft = probs * left
        grow = dleft * mm(table_a, amount_low) + pleft * mm(table_b, amount_low)
        back_in = mm_tn(table_a, dleft.astype(BF)) + mm_tn(table_b, pleft.astype(BF))
        dinflow = dinflow + right * back_in
        step = 1 << level
        bit = row_bit(rows, level)
        total = pltpu.roll(jnp.where(bit, fbar, 0.0), rows - step, 0) + pltpu.roll(
            jnp.where(bit, 0.0, gbar), step, 0
        )
        fbar = fbar + grow + total
        gbar = gbar + amount * back_in + total
    ddi_ref[0, :, :SLOTS] = fbar
    ddi_ref[0, :, SLOTS:] = dinflow


def finish_kernel(kv_ref, li_ref, init_ref, end_ref, dkv_ref, ddi_ref, okv_ref, oddi_ref):
    kv = kv_ref[0]
    log_decay = li_ref[0, :, :SLOTS]
    inflow = li_ref[0, :, SLOTS:]
    end = end_ref[0]
    rows = kv.shape[0]
    t = lax.broadcasted_iota(jnp.int32, (rows, rows), 0)
    s = lax.broadcasted_iota(jnp.int32, (rows, rows), 1)
    earlier = (s < t).astype(F32)
    after = exact((s > t).astype(F32), log_decay)
    fade = jnp.exp(after)
    weight = fade * inflow
    end_low = end.astype(BF)
    okv_ref[0] = (dkv_ref[0] + mm(weight.astype(BF), end_low)).astype(BF)
    reach = mm_nt(kv, end_low)
    whole = jnp.exp(jnp.sum(log_decay, axis=0, keepdims=True))
    carry = lax.dot_general(
        jnp.ones((8, 2 * HEAD), F32), end * init_ref[0], (((1,), (1,)), ((), ())),
        precision=HIGHEST, preferred_element_type=F32,
    )[0:1]
    oddi_ref[0, :, :SLOTS] = (
        ddi_ref[0, :, :SLOTS] + exact(earlier, weight * reach) + whole * carry
    )
    oddi_ref[0, :, SLOTS:] = ddi_ref[0, :, SLOTS:] + fade * reach


def blocked(shape):
    return pl.BlockSpec((1,) + shape, lambda i: (i, 0, 0))


def run(kernel, args, specs, outs, out_specs, flops, moved):
    return pl.pallas_call(
        kernel,
        grid=(args[0].shape[0],),
        in_specs=specs,
        out_specs=out_specs,
        out_shape=outs,
        cost_estimate=pl.CostEstimate(flops=flops, bytes_accessed=moved, transcendentals=0),
        compiler_params=pltpu.CompilerParams(vmem_limit_bytes=56 << 20),
    )(*args)


def sds(shape, dtype=F32):
    return jax.ShapeDtypeStruct(shape, dtype)


def chunk_states(kv, li):
    n, rows, _ = kv.shape
    return run(
        states_kernel, (kv, li),
        [blocked((rows, 2 * HEAD)), blocked((rows, 2 * SLOTS))],
        (sds((n, SLOTS, 2 * HEAD)), sds((n, SLOTS, 128))),
        (blocked((SLOTS, 2 * HEAD)), blocked((SLOTS, 128))),
        n * 10**9, n * 10**6,
    )


def mixer_forward(qs, kv, li, init, gain):
    n, rows, _ = kv.shape
    return run(
        forward_kernel, (qs, kv, li, init, gain),
        [blocked((rows, 2 * HEAD)), blocked((rows, 2 * HEAD)), blocked((rows, 2 * SLOTS)),
         blocked((SLOTS, 2 * HEAD)), pl.BlockSpec((8, HEAD), lambda i: (0, 0))],
        (sds((n, rows, HEAD), BF), sds((n, rows, HEAD)), sds((n, rows, SLOTS)), sds((n, rows, rows), BF)),
        (blocked((rows, HEAD)), blocked((rows, HEAD)), blocked((rows, SLOTS)), blocked((rows, rows))),
        n * 3 * 10**9, n * 4 * 10**6,
    )


def mixer_backward(qs, kv, li, init, gain, out, probs, mix, gg):
    n, rows, _ = kv.shape
    return run(
        backward_kernel, (qs, kv, li, init, gain, out, probs, mix, gg),
        [blocked((rows, 2 * HEAD)), blocked((rows, 2 * HEAD)), blocked((rows, 2 * SLOTS)),
         blocked((SLOTS, 2 * HEAD)), pl.BlockSpec((8, HEAD), lambda i: (0, 0)),
         blocked((rows, HEAD)), blocked((rows, SLOTS)), blocked((rows, rows)), blocked((rows, HEAD))],
        (sds((n, rows, 2 * HEAD), BF), sds((n, rows, 2 * HEAD)), sds((n, rows, 2 * SLOTS)),
         sds((n, SLOTS, 2 * HEAD)), sds((8, HEAD))),
        (blocked((rows, 2 * HEAD)), blocked((rows, 2 * HEAD)), blocked((rows, 2 * SLOTS)),
         blocked((SLOTS, 2 * HEAD)), pl.BlockSpec((8, HEAD), lambda i: (0, 0))),
        n * 6 * 10**9, n * 5 * 10**6,
    )


def mixer_finish(kv, li, init, end, dkv, ddi):
    n, rows, _ = kv.shape
    return run(
        finish_kernel, (kv, li, init, end, dkv, ddi),
        [blocked((rows, 2 * HEAD)), blocked((rows, 2 * SLOTS)), blocked((SLOTS, 2 * HEAD)),
         blocked((SLOTS, 2 * HEAD)), blocked((rows, 2 * HEAD)), blocked((rows, 2 * SLOTS))],
        (sds((n, rows, 2 * HEAD), BF), sds((n, rows, 2 * SLOTS))),
        (blocked((rows, 2 * HEAD)), blocked((rows, 2 * SLOTS))),
        n * 10**9, n * 3 * 10**6,
    )


D = 2048
HEADS = 4
RANK = 16
NORMALIZER = 8.0


def inverse_rms(values):
    return lax.rsqrt(jnp.mean(values * values, axis=-1, keepdims=True) + EPSILON)


def silu_slope(values):
    sigmoid_val = jax.nn.sigmoid(values)
    return sigmoid_val * (1.0 + values * (1.0 - sigmoid_val))


def norm_back(grad_hat, hat_rows, scale_rows):
    return scale_rows * (
        grad_hat - hat_rows * jnp.mean(grad_hat * hat_rows, axis=-1, keepdims=True)
    )


def swap(value, axis, step):
    count = lax.axis_size(axis)
    return lax.ppermute(value, axis, [(i, i ^ step) for i in range(count)])


def gather_heads(block):
    return [block] + [swap(block, "p", k) for k in range(1, HEADS)]


def scatter_heads(parts, *fillers):
    got = [swap(parts[k], "p", k) for k in range(1, HEADS)]
    if fillers:
        held = lax.optimization_barrier(tuple(got) + fillers)
        got, fillers = held[: HEADS - 1], held[HEADS - 1 :]
    total = parts[0].astype(F32)
    for part in got:
        total = total + part.astype(F32)
    return (total,) + tuple(fillers) if fillers else total


def after(value, *others):
    return lax.optimization_barrier((value,) + others)[0]


def place_kernel(blocks, spot_ref, *refs):
    ins, out = refs[:-1], refs[-1]
    part = ins[0].shape[1]
    for i, ref in enumerate(ins):
        for k in range(blocks):
            start = pl.multiple_of(spot_ref[i * blocks + k] * part, part)
            out[pl.ds(start, part), :] = ref[k]


def place(parts, spots):
    blocks, part, width = parts[0].shape
    chunk = 256
    table = jnp.stack([jnp.asarray(x, jnp.int32) for row in spots for x in row])
    rows = len(parts) * blocks * part
    return pl.pallas_call(
        functools.partial(place_kernel, blocks),
        grid_spec=pltpu.PrefetchScalarGridSpec(
            num_scalar_prefetch=1,
            grid=(width // chunk,),
            in_specs=[pl.BlockSpec((blocks, part, chunk), lambda i, s: (0, 0, i))] * len(parts),
            out_specs=pl.BlockSpec((rows, chunk), lambda i, s: (0, i)),
        ),
        out_shape=jax.ShapeDtypeStruct((rows, width), BF),
        cost_estimate=pl.CostEstimate(flops=0, bytes_accessed=4 * rows * width, transcendentals=0),
        compiler_params=pltpu.CompilerParams(vmem_limit_bytes=56 << 20),
    )(table, *parts)


def column_cuts(shards, here, k):
    cuts = []
    for shard in shards:
        width = shard.shape[1] // HEADS
        cuts.append(lax.dynamic_slice_in_dim(shard, (here ^ k) * width, width, 1))
    return jnp.concatenate(cuts, axis=1)


def head_columns(shards, here):
    copies = lax.axis_size("r")
    turn = lax.axis_index("r")
    own = column_cuts(shards, here, 0)
    pieces = [own] + [swap(column_cuts(shards, here, k), "p", k) for k in range(1, HEADS)]
    parts, spots = [], []
    for k in range(HEADS):
        for m in range(copies):
            piece = pieces[k] if m == 0 else swap(pieces[k], "r", m)
            parts.append(piece[None])
            spots.append([(here ^ k) * copies + (turn ^ m)])
    return place(parts, spots), pieces[1:]


def seq_pieces(shards, here):
    count, spot = lax.axis_size("seq"), lax.axis_index("seq")
    rows = shards[0].shape[0] // count
    shards = [lax.dynamic_slice_in_dim(shard, spot * rows, rows, 0) for shard in shards]
    own = column_cuts(shards, here, 0)
    return jnp.stack([own] + [swap(column_cuts(shards, here, k), "p", k) for k in range(1, HEADS)])


def seq_columns(pieces, here):
    copies, count = lax.axis_size("r"), lax.axis_size("seq")
    turn, spot = lax.axis_index("r"), lax.axis_index("seq")
    parts, spots = [], []
    for j, part in enumerate(gather_seq(pieces)):
        for m in range(copies):
            parts.append(part if m == 0 else swap(part, "r", m))
            spots.append(
                [(((here ^ k) * copies + (turn ^ m)) * count + (spot ^ j)) for k in range(HEADS)]
            )
    return place(parts, spots)


def gather_small(packed, here, turn):
    copies = lax.axis_size("r")
    near = jnp.concatenate([packed] + [swap(packed, "r", m) for m in range(1, copies)])
    both = jnp.concatenate(gather_heads(near))
    heads = jnp.arange(HEADS, dtype=jnp.int32) ^ here
    turns = jnp.arange(copies, dtype=jnp.int32) ^ turn
    order = (heads[:, None] * copies + turns[None, :]).reshape(-1)
    return jnp.take(both, order, axis=0)


def sum_small(value, here, turn):
    mine = [lax.dynamic_index_in_dim(value, here ^ k, 0, False) for k in range(HEADS)]
    total = scatter_heads(mine)
    copies = lax.axis_size("r")
    kept = lax.dynamic_index_in_dim(total, turn, 0, True)
    for m in range(1, copies):
        kept = kept + swap(lax.dynamic_index_in_dim(total, turn ^ m, 0, True), "r", m)
    step = 1
    while step < lax.axis_size("seq"):
        kept = kept + swap(kept, "seq", step)
        step *= 2
    return kept[0]


def chain(state, decay, forward):
    count = lax.axis_size("seq")
    total = jnp.zeros_like(state)
    for hop in range(count - 1):
        pair = (hop, hop + 1) if forward else (count - 1 - hop, count - 2 - hop)
        sent = (decay * total + state).astype(BF)
        total = total + lax.ppermute(sent, "seq", [pair]).astype(F32)
    return total


def chain_pair(both, decay, forward):
    return jnp.concatenate(
        [chain(both[..., :HEAD], decay, forward), chain(both[..., HEAD:], decay, forward)], axis=-1
    )


def split_rows(left, turn, step, groups):
    copies, width = left.shape[2:]
    flat = left.reshape(left.shape[0], -1)
    cuts = [
        lax.dynamic_slice_in_dim(flat, (g * copies + (turn ^ step)) * width, width, 1)
        for g in groups
    ]
    return jnp.concatenate(cuts, axis=1)


def sum_copies(own, away):
    got = [swap(part, "r", m + 1) for m, part in enumerate(away)]
    total = own()
    for part in got:
        total = total + part.astype(F32)
    return total.astype(BF)


def gather_seq(value):
    count = lax.axis_size("seq")
    found = {0: value}
    step = count // 2
    while step >= 1:
        for j in list(found):
            found[j ^ step] = swap(found[j], "seq", step)
        step //= 2
    return [found[j] for j in range(count)]


def assemble_kernel(counts, spot_ref, *refs):
    n_in, n_out, part = counts
    ins, outs = refs[:n_in], refs[n_in:]
    width = outs[0].shape[1]
    for j in range(n_in):
        for o in range(n_out):
            cut = ins[j][0, :, o * width : (o + 1) * width]
            outs[o][j * part : (j + 1) * part, :] = cut.astype(F32)


def assemble(parts, columns, n_out):
    spans, blocks, part, width = parts.shape
    width //= n_out
    rows = part * spans
    spots = jnp.stack([jnp.asarray(c, jnp.int32) for c in columns])
    return pl.pallas_call(
        functools.partial(assemble_kernel, (spans, n_out, part)),
        grid_spec=pltpu.PrefetchScalarGridSpec(
            num_scalar_prefetch=1,
            grid=(blocks,),
            in_specs=[
                pl.BlockSpec((None, 1, part, n_out * width), lambda i, s, j=j: (j, i, 0, 0))
                for j in range(spans)
            ],
            out_specs=[pl.BlockSpec((rows, width), lambda i, s: (0, s[i]))] * n_out,
        ),
        out_shape=[jax.ShapeDtypeStruct((rows, blocks * width), F32)] * n_out,
        cost_estimate=pl.CostEstimate(
            flops=0, bytes_accessed=6 * n_out * rows * blocks * width, transcendentals=0
        ),
        compiler_params=pltpu.CompilerParams(vmem_limit_bytes=56 << 20),
    )(spots, *([parts] * spans))


def swap_diagonal(part):
    count = lax.axis_size("seq")
    sends = [(p * count + z, (p ^ z) * count + z) for p in range(HEADS) for z in range(count)]
    return lax.ppermute(part, ("p", "seq"), sends)


def body(
    tokens,
    seq_lengths,
    attn_gain,
    query_proj,
    key_proj,
    value_proj,
    decay_down,
    decay_up,
    decay_bias,
    swish_proj,
    slot_gain,
    out_proj,
    mlp_gain,
    mlp_gate,
    mlp_up,
    mlp_down,
    grad_out,
):
    rows = tokens.shape[0]
    copies = lax.axis_size("r")
    owners = HEADS * copies
    shard = D // owners
    here, turn, place = lax.axis_index("p"), lax.axis_index("r"), lax.axis_index("seq")
    group = HEADS * rows

    small = [attn_gain, decay_down, decay_up, decay_bias, slot_gain, mlp_gain, seq_lengths]
    packed = jnp.concatenate([a.astype(F32).reshape(-1) for a in small])
    packed = gather_small(packed[None], here, turn)
    fields, offset = [], 0
    for a in small:
        fields.append(packed[:, offset : offset + a.size])
        offset += a.size
    gain_one = fields[0].reshape(D)
    down_full = fields[1].reshape(D, RANK).astype(BF)
    up_full = fields[2].reshape(owners, RANK, -1).transpose(1, 0, 2).reshape(RANK, HEADS * SLOTS)
    up_head = lax.dynamic_slice_in_dim(up_full, here * SLOTS, SLOTS, 1)
    bias_head = lax.dynamic_slice_in_dim(fields[3].reshape(HEADS * SLOTS), here * SLOTS, SLOTS, 0)
    gain_head = lax.dynamic_slice_in_dim(fields[4].reshape(D), here * HEAD, HEAD, 0)
    gain_head8 = jnp.broadcast_to(gain_head[None], (8, HEAD))
    gain_two = fields[5].reshape(D)
    lengths = fields[6].reshape(HEADS, copies)
    positions = (place * rows + jnp.arange(rows, dtype=jnp.int32)).astype(F32)
    masks = [
        (positions < lax.dynamic_index_in_dim(lengths, here ^ k, 0, False)[turn]).astype(F32)
        for k in range(HEADS)
    ]
    mask_all = jnp.concatenate(masks)[:, None]
    mask_own = masks[0][:, None]

    token_blocks = gather_heads(tokens)
    weight_kv, kv_pieces = head_columns([key_proj, value_proj], here)
    late = lax.optimization_barrier((query_proj, swish_proj, mlp_gate, mlp_up) + tuple(kv_pieces))
    weight_qs, qs_pieces = head_columns(late[:2], here)
    gu_pieces = seq_pieces(late[2:4], here)
    grad_blocks = gather_heads(after(grad_out, *qs_pieces))
    weight_out = lax.all_gather(out_proj, "r", axis=0, tiled=True)
    weight_down = lax.all_gather(mlp_down, "r", axis=0, tiled=True)

    tokens_all = jnp.concatenate(token_blocks).astype(F32)
    normed = (tokens_all * inverse_rms(tokens_all) * gain_one).astype(BF)
    kv = mm(normed, weight_kv).astype(BF).reshape(HEADS, rows, 2 * HEAD)
    gate_low = mm(normed, down_full)
    forget = exact(gate_low, up_head) + bias_head
    log_sig = jax.nn.log_sigmoid(forget) / NORMALIZER
    li = jnp.concatenate([mask_all * log_sig, mask_all * -jnp.expm1(log_sig)], axis=1)
    li = li.reshape(HEADS, rows, 2 * SLOTS)
    state, decay = chunk_states(kv, li)
    decay = decay[:, :, :1]
    init = chain_pair(state, decay, True)
    init, gu_pieces = lax.optimization_barrier((init, gu_pieces))
    weight_gu = seq_columns(gu_pieces, here)
    qs = mm(normed, weight_qs).reshape(HEADS, rows, 2 * HEAD)
    gated, mixer_out, probs, mix = mixer_forward(qs, kv, li, init, gain_head8)
    gated = gated.reshape(group, HEAD)
    attn_part = mm(gated, weight_out).astype(BF).reshape(HEADS, rows, D)
    grad_mlp = (mask_all * jnp.concatenate(grad_blocks).astype(F32)).astype(BF)
    attn_out, grad_act = scatter_heads(
        [attn_part[k] for k in range(HEADS)], mm_nt(grad_mlp, weight_down)
    )

    tokens_f = tokens.astype(F32)
    residual = tokens_f + mask_own * attn_out
    scale_two = inverse_rms(residual)
    hat_two = residual * scale_two
    normed_two_own = (hat_two * gain_two).astype(BF)
    normed_two = jnp.concatenate(gather_heads(normed_two_own))

    hidden_width = weight_down.shape[0]
    gate_up = mm(normed_two, weight_gu)
    gate_pre, up_pre = gate_up[:, :hidden_width], gate_up[:, hidden_width:]
    hidden = (jax.nn.silu(gate_pre) * up_pre).astype(BF)
    grad_gate = (grad_act * up_pre * silu_slope(gate_pre)).astype(BF)
    grad_up = (grad_act * jax.nn.silu(gate_pre)).astype(BF)
    grad_gu = jnp.concatenate([grad_gate, grad_up], axis=1)
    order = [here ^ k for k in range(HEADS)]
    hops = range(1, copies)
    down_rows = mlp_down.shape[0]
    two_view = normed_two.reshape(group, HEADS, copies, shard)
    gu_away = [mm_tn(split_rows(two_view, turn, m, order), grad_gu).astype(BF) for m in hops]
    two_part = mm_nt(after(grad_gu, *gu_away), weight_gu).astype(BF)
    gu_total = sum_copies(
        lambda: mm_tn(split_rows(two_view, turn, 0, order), after(grad_gu, two_part)), gu_away
    )
    gu_part = lax.psum_scatter(
        gu_total.reshape(HEADS, shard, 2 * hidden_width), "seq", scatter_dimension=0, tiled=True
    )
    hidden_late = after(hidden, gu_total)

    def down_grad_part(m):
        cut = lax.dynamic_slice_in_dim(hidden_late, (turn ^ m) * down_rows, down_rows, 1)
        return mm_tn(cut, grad_mlp)

    down_total = sum_copies(
        lambda: down_grad_part(0), [down_grad_part(m).astype(BF) for m in hops]
    )
    two_part = two_part.reshape(HEADS, rows, D)
    grad_norm_two, down_total = scatter_heads([two_part[k] for k in range(HEADS)], down_total)
    gain_two_grad = jnp.sum(grad_norm_two * hat_two, axis=0)
    grad_rows = grad_out.astype(F32)
    grad_resid = grad_rows + norm_back(grad_norm_two * gain_two, hat_two, scale_two)
    grad_attn_own = (mask_own * grad_resid).astype(BF)
    attn_blocks = gather_heads(grad_attn_own)
    mlp_part = mm(hidden, weight_down).astype(BF)
    mlp_part, *attn_blocks = lax.optimization_barrier((mlp_part,) + tuple(attn_blocks))
    grad_attn = jnp.concatenate(attn_blocks)
    mlp_part = mlp_part.reshape(HEADS, rows, D)
    mlp_out = scatter_heads([mlp_part[k] for k in range(HEADS)])
    result = (residual + mask_own * mlp_out).astype(BF)

    grad_gated = mm_nt(grad_attn, weight_out).reshape(HEADS, rows, HEAD)
    grad_qs, grad_kv, grad_li, adjoint, slot_part = mixer_backward(
        qs, kv, li, init, gain_head8, mixer_out, probs, mix, grad_gated
    )
    adjoint, gu_part = lax.optimization_barrier((adjoint, gu_part))
    gu_part = swap_diagonal(gu_part)
    one_view = normed.reshape(group, HEADS, copies, shard)
    one_views = [split_rows(one_view, turn, m, order) for m in range(copies)]
    out_view = gated.reshape(group, 1, copies, shard)
    out_views = [split_rows(out_view, turn, m, [0]) for m in range(copies)]

    def weight_grad(views, right):
        return sum_copies(
            lambda: mm_tn(views[0], right), [mm_tn(views[m], right).astype(BF) for m in hops]
        )

    grad_qs = grad_qs.reshape(group, 2 * HEAD)
    out_total = weight_grad(out_views, grad_attn)
    qs_total = weight_grad(one_views, grad_qs)
    ends = chain_pair(adjoint, decay, False)
    ends, gu_part, out_total, qs_total = lax.optimization_barrier(
        (ends, gu_part, out_total, qs_total)
    )
    grad_kv, grad_li = mixer_finish(kv, li, init, ends, grad_kv, grad_li)
    grad_kv = grad_kv.reshape(group, 2 * HEAD)
    grad_li = grad_li.reshape(group, 2 * SLOTS)
    grad_decay = (
        mask_all
        * (grad_li[:, :SLOTS] - grad_li[:, SLOTS:] * jnp.exp(log_sig))
        / NORMALIZER
        * jax.nn.sigmoid(-forget)
    )
    bias_part = jnp.sum(grad_decay, axis=0)
    up_part = lax.dot_general(
        gate_low, grad_decay, (((0,), (0,)), ((), ())), precision=HIGHEST, preferred_element_type=F32
    )
    grad_low = lax.dot_general(
        grad_decay, up_head, (((1,), (1,)), ((), ())), precision=HIGHEST, preferred_element_type=F32
    ).astype(BF)
    down_low_part = mm_tn(normed, grad_low)

    one_part = (
        (mm_nt(grad_qs, weight_qs) + mm_nt(grad_kv, weight_kv) + mm_nt(grad_low, down_full))
        .astype(BF)
        .reshape(HEADS, rows, D)
    )
    kv_total = weight_grad(one_views, grad_kv)
    grad_norm_one, kv_total = scatter_heads([one_part[k] for k in range(HEADS)], kv_total)

    qs_total = qs_total.reshape(HEADS, shard, 2 * HEAD)
    kv_total = kv_total.reshape(HEADS, shard, 2 * HEAD)
    gu_whole = lax.all_gather(gu_part, "seq", axis=0, tiled=True)
    qs_part = lax.psum_scatter(
        after(qs_total, gu_whole), "seq", scatter_dimension=0, tiled=True
    )
    down_grad = lax.psum(after(down_total, qs_part), "seq")
    qs_whole = lax.all_gather(after(swap_diagonal(qs_part), down_grad), "seq", axis=0, tiled=True)
    kv_part = lax.psum_scatter(
        after(kv_total, qs_whole), "seq", scatter_dimension=0, tiled=True
    )
    out_grad = lax.psum(after(out_total, kv_part), "seq")
    kv_whole = lax.all_gather(after(swap_diagonal(kv_part), out_grad), "seq", axis=0, tiled=True)
    gate_grad, up_grad = assemble(gu_whole[None], order, 2)
    query_grad, swish_grad = assemble(qs_whole[None], order, 2)
    key_grad, value_grad = assemble(kv_whole[None], order, 2)
    out_grad = out_grad.astype(F32)
    scale_one = inverse_rms(tokens_f)
    hat_one = tokens_f * scale_one
    gain_one_grad = jnp.sum(grad_norm_one * hat_one, axis=0)
    grad_tokens = (grad_resid + norm_back(grad_norm_one * gain_one, hat_one, scale_one)).astype(BF)

    def placed(part, width):
        whole = jnp.zeros(part.shape[:-1] + (HEADS * width,), F32)
        return lax.dynamic_update_slice_in_dim(whole, part, here * width, part.ndim - 1)

    up_sum = placed(up_part, SLOTS).reshape(RANK, HEADS, copies, -1).transpose(1, 2, 0, 3)
    sums = [
        gain_one_grad,
        down_low_part,
        up_sum,
        placed(bias_part, SLOTS),
        placed(slot_part[0], HEAD),
        gain_two_grad,
    ]
    flat = jnp.concatenate([a.reshape(HEADS, copies, -1) for a in sums], axis=2)
    flat = sum_small(flat, here, turn)
    totals, offset = [], 0
    for a in sums:
        size = a.size // owners
        totals.append(flat[offset : offset + size])
        offset += size

    return (
        result,
        grad_tokens,
        totals[0],
        query_grad,
        key_grad,
        value_grad,
        totals[1].reshape(shard, RANK),
        totals[2].reshape(RANK, -1),
        totals[3],
        swish_grad,
        totals[4],
        out_grad,
        totals[5],
        gate_grad,
        up_grad,
        down_grad.astype(F32),
    )


def solution(mesh):
    count, span = mesh.devices.shape
    split = Mesh(mesh.devices.reshape(HEADS, count // HEADS, span), ("p", "r", "seq"))
    rows = P(("p", "r", "seq"), None)
    matrix, vector, last = P(("p", "r"), None), P(("p", "r")), P(None, ("p", "r"))
    in_specs = (
        rows, vector, vector, matrix, matrix, matrix, matrix, last, vector, matrix, vector, matrix,
        vector, matrix, matrix, matrix, rows,
    )
    out_specs = (
        rows, rows, vector, matrix, matrix, matrix, matrix, last, vector, matrix, vector, matrix,
        vector, matrix, matrix, matrix,
    )
    return jax.shard_map(body, mesh=split, in_specs=in_specs, out_specs=out_specs, check_vma=False)
```

```python
import functools
import jax
import jax.numpy as jnp
from jax import lax
from jax.experimental import pallas as pl
from jax.experimental.pallas import tpu as pltpu
from jax.sharding import Mesh, PartitionSpec as P

HEAD = 512
SLOTS = 64
SCALE = HEAD ** (-0.5)
EPSILON = 1e-06
HIGHEST = lax.Precision.HIGHEST
BF = jnp.bfloat16
F32 = jnp.float32


def mm(a, b):
    return lax.dot_general(a, b, (((1,), (0,)), ((), ())), preferred_element_type=F32)


def mm_nt(a, b):
    return lax.dot_general(a, b, (((1,), (1,)), ((), ())), preferred_element_type=F32)


def mm_tn(a, b):
    return lax.dot_general(a, b, (((0,), (0,)), ((), ())), preferred_element_type=F32)


def exact(a, b):
    return lax.dot_general(
        a, b, (((1,), (0,)), ((), ())), precision=HIGHEST, preferred_element_type=F32
    )


def row_bit(rows, level):
    t = lax.broadcasted_iota(jnp.int32, (rows, SLOTS), 0)
    return ((t >> level) & 1) == 1


def prefix_levels(log_decay):
    rows = log_decay.shape[0]
    levels = rows.bit_length() - 1
    f, g = log_decay, jnp.zeros_like(log_decay)
    out = []
    for level in range(levels):
        out.append((f, g))
        total = f + g
        step = 1 << level
        bit = row_bit(rows, level)
        f = f + jnp.where(bit, pltpu.roll(total, step, 0), 0.0)
        g = g + jnp.where(bit, 0.0, pltpu.roll(total, rows - step, 0))
    return out, f, g


def same_block(rows, level):
    t = lax.broadcasted_iota(jnp.int32, (rows, rows), 0)
    s = lax.broadcasted_iota(jnp.int32, (rows, rows), 1)
    return (t >> (level + 1)) == (s >> (level + 1))


def level_mask(table, level, levels):
    if level == levels - 1:
        return table
    return jnp.where(same_block(table.shape[0], level), table, jnp.zeros_like(table))


def factors(pair, level, inflow):
    f, g = pair
    bit = row_bit(f.shape[0], level)
    left = jnp.where(bit, jnp.exp(f), 0.0)
    right = jnp.where(bit, 0.0, jnp.exp(g))
    return left, right, right * inflow


def diagonal(rows):
    t = lax.broadcasted_iota(jnp.int32, (rows, rows), 0)
    s = lax.broadcasted_iota(jnp.int32, (rows, rows), 1)
    return t == s


def slot_table(weights, pairs, inflow):
    rows = weights.shape[0]
    levels = len(pairs)
    table = jnp.where(diagonal(rows), jnp.sum(weights * inflow, axis=1, keepdims=True), 0.0)
    for level in range(levels):
        left, _, gain = factors(pairs[level], level, inflow)
        block = mm_nt((weights * left).astype(BF), gain.astype(BF))
        table = table + level_mask(block, level, levels)
    return table


def slot_sums(table, pairs, inflow):
    rows = table.shape[0]
    levels = len(pairs)
    own = jnp.sum(jnp.where(diagonal(rows), table, 0.0), axis=1, keepdims=True)
    low = table.astype(BF)
    total = own * inflow
    for level in range(levels):
        left, _, gain = factors(pairs[level], level, inflow)
        total = total + left * mm(level_mask(low, level, levels), gain.astype(BF))
    return total


def states_kernel(kv_ref, li_ref, state_ref, decay_ref):
    kv = kv_ref[0]
    log_decay = li_ref[0, :, :SLOTS]
    inflow = li_ref[0, :, SLOTS:]
    rows = kv.shape[0]
    t = lax.broadcasted_iota(jnp.int32, (rows, rows), 0)
    s = lax.broadcasted_iota(jnp.int32, (rows, rows), 1)
    after = exact((s > t).astype(F32), log_decay)
    weight = jnp.exp(after) * inflow
    state_ref[0] = mm_tn(weight.astype(BF), kv)
    total = lax.dot_general(
        log_decay, jnp.ones((rows, 128), F32), (((0,), (0,)), ((), ())),
        precision=HIGHEST, preferred_element_type=F32,
    )
    decay_ref[0] = jnp.exp(total)


def forward_kernel(qs_ref, kv_ref, li_ref, init_ref, gain_ref, gated_ref, out_ref, prob_ref, mix_ref):
    queries = qs_ref[0, :, :HEAD].astype(BF)
    swish = qs_ref[0, :, HEAD:]
    keys = kv_ref[0, :, :HEAD]
    values = kv_ref[0, :, HEAD:]
    log_decay = li_ref[0, :, :SLOTS]
    inflow = li_ref[0, :, SLOTS:]
    init = init_ref[0].astype(BF)
    pairs, running, _ = prefix_levels(log_decay)
    growth = jnp.exp(running)
    scores = mm_nt(queries, keys) * SCALE
    slots = slot_sums(scores, pairs, inflow) + mm_nt(queries, init[:, :HEAD]) * SCALE * growth
    top = jnp.max(slots, axis=1, keepdims=True)
    weights = jnp.exp(slots - top)
    probs = weights / jnp.sum(weights, axis=1, keepdims=True)
    mix = slot_table(probs, pairs, inflow).astype(BF)
    out = mm(mix, values) + mm((probs * growth).astype(BF), init[:, HEAD:])
    hat = out * lax.rsqrt(jnp.mean(out * out, axis=1, keepdims=True) + EPSILON)
    gated_ref[0] = (hat * gain_ref[0:1] * (swish * jax.nn.sigmoid(swish))).astype(BF)
    out_ref[0] = out
    prob_ref[0] = probs
    mix_ref[0] = mix


def backward_kernel(
    qs_ref, kv_ref, li_ref, init_ref, gain_ref, out_ref, prob_ref, mix_ref, gg_ref,
    dqs_ref, dkv_ref, ddi_ref, adj_ref, sg_ref,
):
    queries = qs_ref[0, :, :HEAD].astype(BF)
    swish = qs_ref[0, :, HEAD:]
    keys = kv_ref[0, :, :HEAD]
    values = kv_ref[0, :, HEAD:]
    log_decay = li_ref[0, :, :SLOTS]
    inflow = li_ref[0, :, SLOTS:]
    init = init_ref[0].astype(BF)
    out = out_ref[0]
    probs = prob_ref[0]
    gain = gain_ref[0:1]
    rows = out.shape[0]
    scale_out = lax.rsqrt(jnp.mean(out * out, axis=1, keepdims=True) + EPSILON)
    hat = out * scale_out
    sig = jax.nn.sigmoid(swish)
    silu = swish * sig
    gg = gg_ref[0].astype(F32)
    gg_hat = gg * hat
    dqs_ref[0, :, HEAD:] = (gg_hat * gain * (sig * (1.0 + swish * (1.0 - sig)))).astype(BF)
    part = jnp.broadcast_to(jnp.sum(gg_hat * silu, axis=0, keepdims=True), (8, HEAD))

    @pl.when(pl.program_id(0) == 0)
    def _():
        sg_ref[...] = part

    @pl.when(pl.program_id(0) > 0)
    def _():
        sg_ref[...] = sg_ref[...] + part

    grad_hat = gg * gain * silu
    dout = scale_out * (grad_hat - hat * jnp.mean(grad_hat * hat, axis=1, keepdims=True))
    dout = dout.astype(BF)
    pairs, running, _ = prefix_levels(log_decay)
    levels = len(pairs)
    growth = jnp.exp(running)
    scores = mm_nt(queries, keys) * SCALE
    grads = mm_nt(dout, values)
    key_part = mm_nt(queries, init[:, :HEAD]) * SCALE * growth
    value_part = mm_nt(dout, init[:, HEAD:]) * growth
    dprob = slot_sums(grads, pairs, inflow) + value_part
    dslot = probs * (dprob - jnp.sum(probs * dprob, axis=1, keepdims=True))
    back = slot_table(dslot, pairs, inflow).astype(BF)
    dslot_g = (dslot * growth).astype(BF)
    prob_g = (probs * growth).astype(BF)
    dqs_ref[0, :, :HEAD] = (SCALE * (mm(back, keys) + mm(dslot_g, init[:, :HEAD]))).astype(BF)
    dkv_ref[0, :, :HEAD] = SCALE * mm_tn(back, queries)
    dkv_ref[0, :, HEAD:] = mm_tn(mix_ref[0], dout)
    adj_ref[0, :, :HEAD] = SCALE * mm_tn(dslot_g, queries)
    adj_ref[0, :, HEAD:] = mm_tn(prob_g, dout)
    diag = diagonal(rows)
    own_a = jnp.sum(jnp.where(diag, scores, 0.0), axis=1, keepdims=True)
    own_b = jnp.sum(jnp.where(diag, grads, 0.0), axis=1, keepdims=True)
    dinflow = dslot * own_a + probs * own_b
    scores_low = scores.astype(BF)
    grads_low = grads.astype(BF)
    fbar = dslot * key_part + probs * value_part
    gbar = jnp.zeros_like(fbar)
    for level in range(levels - 1, -1, -1):
        left, right, amount = factors(pairs[level], level, inflow)
        table_a = level_mask(scores_low, level, levels)
        table_b = level_mask(grads_low, level, levels)
        amount_low = amount.astype(BF)
        dleft = dslot * left
        pleft = probs * left
        grow = dleft * mm(table_a, amount_low) + pleft * mm(table_b, amount_low)
        back_in = mm_tn(table_a, dleft.astype(BF)) + mm_tn(table_b, pleft.astype(BF))
        dinflow = dinflow + right * back_in
        step = 1 << level
        bit = row_bit(rows, level)
        total = pltpu.roll(jnp.where(bit, fbar, 0.0), rows - step, 0) + pltpu.roll(
            jnp.where(bit, 0.0, gbar), step, 0
        )
        fbar = fbar + grow + total
        gbar = gbar + amount * back_in + total
    ddi_ref[0, :, :SLOTS] = fbar
    ddi_ref[0, :, SLOTS:] = dinflow


def finish_kernel(kv_ref, li_ref, init_ref, end_ref, dkv_ref, ddi_ref, okv_ref, oddi_ref):
    kv = kv_ref[0]
    log_decay = li_ref[0, :, :SLOTS]
    inflow = li_ref[0, :, SLOTS:]
    end = end_ref[0]
    rows = kv.shape[0]
    t = lax.broadcasted_iota(jnp.int32, (rows, rows), 0)
    s = lax.broadcasted_iota(jnp.int32, (rows, rows), 1)
    earlier = (s < t).astype(F32)
    after = exact((s > t).astype(F32), log_decay)
    fade = jnp.exp(after)
    weight = fade * inflow
    end_low = end.astype(BF)
    okv_ref[0] = (dkv_ref[0] + mm(weight.astype(BF), end_low)).astype(BF)
    reach = mm_nt(kv, end_low)
    whole = jnp.exp(jnp.sum(log_decay, axis=0, keepdims=True))
    carry = lax.dot_general(
        jnp.ones((8, 2 * HEAD), F32), end * init_ref[0], (((1,), (1,)), ((), ())),
        precision=HIGHEST, preferred_element_type=F32,
    )[0:1]
    oddi_ref[0, :, :SLOTS] = (
        ddi_ref[0, :, :SLOTS] + exact(earlier, weight * reach) + whole * carry
    )
    oddi_ref[0, :, SLOTS:] = ddi_ref[0, :, SLOTS:] + fade * reach


def blocked(shape):
    return pl.BlockSpec((1,) + shape, lambda i: (i, 0, 0))


def run(kernel, args, specs, outs, out_specs, flops, moved):
    return pl.pallas_call(
        kernel,
        grid=(args[0].shape[0],),
        in_specs=specs,
        out_specs=out_specs,
        out_shape=outs,
        cost_estimate=pl.CostEstimate(flops=flops, bytes_accessed=moved, transcendentals=0),
        compiler_params=pltpu.CompilerParams(vmem_limit_bytes=56 << 20),
    )(*args)


def sds(shape, dtype=F32):
    return jax.ShapeDtypeStruct(shape, dtype)


def chunk_states(kv, li):
    n, rows, _ = kv.shape
    return run(
        states_kernel, (kv, li),
        [blocked((rows, 2 * HEAD)), blocked((rows, 2 * SLOTS))],
        (sds((n, SLOTS, 2 * HEAD)), sds((n, SLOTS, 128))),
        (blocked((SLOTS, 2 * HEAD)), blocked((SLOTS, 128))),
        n * 10**9, n * 10**6,
    )


def mixer_forward(qs, kv, li, init, gain):
    n, rows, _ = kv.shape
    return run(
        forward_kernel, (qs, kv, li, init, gain),
        [blocked((rows, 2 * HEAD)), blocked((rows, 2 * HEAD)), blocked((rows, 2 * SLOTS)),
         blocked((SLOTS, 2 * HEAD)), pl.BlockSpec((8, HEAD), lambda i: (0, 0))],
        (sds((n, rows, HEAD), BF), sds((n, rows, HEAD)), sds((n, rows, SLOTS)), sds((n, rows, rows), BF)),
        (blocked((rows, HEAD)), blocked((rows, HEAD)), blocked((rows, SLOTS)), blocked((rows, rows))),
        n * 3 * 10**9, n * 4 * 10**6,
    )


def mixer_backward(qs, kv, li, init, gain, out, probs, mix, gg):
    n, rows, _ = kv.shape
    return run(
        backward_kernel, (qs, kv, li, init, gain, out, probs, mix, gg),
        [blocked((rows, 2 * HEAD)), blocked((rows, 2 * HEAD)), blocked((rows, 2 * SLOTS)),
         blocked((SLOTS, 2 * HEAD)), pl.BlockSpec((8, HEAD), lambda i: (0, 0)),
         blocked((rows, HEAD)), blocked((rows, SLOTS)), blocked((rows, rows)), blocked((rows, HEAD))],
        (sds((n, rows, 2 * HEAD), BF), sds((n, rows, 2 * HEAD)), sds((n, rows, 2 * SLOTS)),
         sds((n, SLOTS, 2 * HEAD)), sds((8, HEAD))),
        (blocked((rows, 2 * HEAD)), blocked((rows, 2 * HEAD)), blocked((rows, 2 * SLOTS)),
         blocked((SLOTS, 2 * HEAD)), pl.BlockSpec((8, HEAD), lambda i: (0, 0))),
        n * 6 * 10**9, n * 5 * 10**6,
    )


def mixer_finish(kv, li, init, end, dkv, ddi):
    n, rows, _ = kv.shape
    return run(
        finish_kernel, (kv, li, init, end, dkv, ddi),
        [blocked((rows, 2 * HEAD)), blocked((rows, 2 * SLOTS)), blocked((SLOTS, 2 * HEAD)),
         blocked((SLOTS, 2 * HEAD)), blocked((rows, 2 * HEAD)), blocked((rows, 2 * SLOTS))],
        (sds((n, rows, 2 * HEAD), BF), sds((n, rows, 2 * SLOTS))),
        (blocked((rows, 2 * HEAD)), blocked((rows, 2 * SLOTS))),
        n * 10**9, n * 3 * 10**6,
    )


D = 2048
HEADS = 4
RANK = 16
NORMALIZER = 8.0


def inverse_rms(values):
    return lax.rsqrt(jnp.mean(values * values, axis=-1, keepdims=True) + EPSILON)


def silu_slope(values):
    sigmoid_val = jax.nn.sigmoid(values)
    return sigmoid_val * (1.0 + values * (1.0 - sigmoid_val))


def norm_back(grad_hat, hat_rows, scale_rows):
    return scale_rows * (
        grad_hat - hat_rows * jnp.mean(grad_hat * hat_rows, axis=-1, keepdims=True)
    )


def swap(value, axis, step):
    count = lax.axis_size(axis)
    return lax.ppermute(value, axis, [(i, i ^ step) for i in range(count)])


def gather_heads(block):
    return [block] + [swap(block, "p", k) for k in range(1, HEADS)]


def scatter_heads(parts, *fillers):
    got = [swap(parts[k], "p", k) for k in range(1, HEADS)]
    if fillers:
        held = lax.optimization_barrier(tuple(got) + fillers)
        got, fillers = held[: HEADS - 1], held[HEADS - 1 :]
    total = parts[0].astype(F32)
    for part in got:
        total = total + part.astype(F32)
    return (total,) + tuple(fillers) if fillers else total


def after(value, *others):
    return lax.optimization_barrier((value,) + others)[0]


def place_kernel(blocks, spot_ref, *refs):
    ins, out = refs[:-1], refs[-1]
    part = ins[0].shape[1]
    for i, ref in enumerate(ins):
        for k in range(blocks):
            start = pl.multiple_of(spot_ref[i * blocks + k] * part, part)
            out[pl.ds(start, part), :] = ref[k]


def place(parts, spots):
    blocks, part, width = parts[0].shape
    chunk = 256
    table = jnp.stack([jnp.asarray(x, jnp.int32) for row in spots for x in row])
    rows = len(parts) * blocks * part
    return pl.pallas_call(
        functools.partial(place_kernel, blocks),
        grid_spec=pltpu.PrefetchScalarGridSpec(
            num_scalar_prefetch=1,
            grid=(width // chunk,),
            in_specs=[pl.BlockSpec((blocks, part, chunk), lambda i, s: (0, 0, i))] * len(parts),
            out_specs=pl.BlockSpec((rows, chunk), lambda i, s: (0, i)),
        ),
        out_shape=jax.ShapeDtypeStruct((rows, width), BF),
        cost_estimate=pl.CostEstimate(flops=0, bytes_accessed=4 * rows * width, transcendentals=0),
        compiler_params=pltpu.CompilerParams(vmem_limit_bytes=56 << 20),
    )(table, *parts)


def column_cuts(shards, here, k):
    cuts = []
    for shard in shards:
        width = shard.shape[1] // HEADS
        cuts.append(lax.dynamic_slice_in_dim(shard, (here ^ k) * width, width, 1))
    return jnp.concatenate(cuts, axis=1)


def head_columns(shards, here):
    copies = lax.axis_size("r")
    turn = lax.axis_index("r")
    own = column_cuts(shards, here, 0)
    pieces = [own] + [swap(column_cuts(shards, here, k), "p", k) for k in range(1, HEADS)]
    parts, spots = [], []
    for k in range(HEADS):
        for m in range(copies):
            piece = pieces[k] if m == 0 else swap(pieces[k], "r", m)
            parts.append(piece[None])
            spots.append([(here ^ k) * copies + (turn ^ m)])
    return place(parts, spots), pieces[1:]


def seq_pieces(shards, here):
    count, spot = lax.axis_size("seq"), lax.axis_index("seq")
    rows = shards[0].shape[0] // count
    shards = [lax.dynamic_slice_in_dim(shard, spot * rows, rows, 0) for shard in shards]
    own = column_cuts(shards, here, 0)
    return jnp.stack([own] + [swap(column_cuts(shards, here, k), "p", k) for k in range(1, HEADS)])


def seq_columns(pieces, here):
    copies, count = lax.axis_size("r"), lax.axis_size("seq")
    turn, spot = lax.axis_index("r"), lax.axis_index("seq")
    parts, spots = [], []
    for j, part in enumerate(gather_seq(pieces)):
        for m in range(copies):
            parts.append(part if m == 0 else swap(part, "r", m))
            spots.append(
                [(((here ^ k) * copies + (turn ^ m)) * count + (spot ^ j)) for k in range(HEADS)]
            )
    return place(parts, spots)


def gather_small(packed, here, turn):
    copies = lax.axis_size("r")
    near = jnp.concatenate([packed] + [swap(packed, "r", m) for m in range(1, copies)])
    both = jnp.concatenate(gather_heads(near))
    heads = jnp.arange(HEADS, dtype=jnp.int32) ^ here
    turns = jnp.arange(copies, dtype=jnp.int32) ^ turn
    order = (heads[:, None] * copies + turns[None, :]).reshape(-1)
    return jnp.take(both, order, axis=0)


def sum_small(value, here, turn):
    mine = [lax.dynamic_index_in_dim(value, here ^ k, 0, False) for k in range(HEADS)]
    total = scatter_heads(mine)
    copies = lax.axis_size("r")
    kept = lax.dynamic_index_in_dim(total, turn, 0, True)
    for m in range(1, copies):
        kept = kept + swap(lax.dynamic_index_in_dim(total, turn ^ m, 0, True), "r", m)
    step = 1
    while step < lax.axis_size("seq"):
        kept = kept + swap(kept, "seq", step)
        step *= 2
    return kept[0]


def chain(state, decay, forward):
    count = lax.axis_size("seq")
    total = jnp.zeros_like(state)
    for hop in range(count - 1):
        pair = (hop, hop + 1) if forward else (count - 1 - hop, count - 2 - hop)
        sent = (decay * total + state).astype(BF)
        total = total + lax.ppermute(sent, "seq", [pair]).astype(F32)
    return total


def chain_pair(both, decay, forward):
    return jnp.concatenate(
        [chain(both[..., :HEAD], decay, forward), chain(both[..., HEAD:], decay, forward)], axis=-1
    )


def split_rows(left, turn, step, groups):
    copies, width = left.shape[2:]
    flat = left.reshape(left.shape[0], -1)
    cuts = [
        lax.dynamic_slice_in_dim(flat, (g * copies + (turn ^ step)) * width, width, 1)
        for g in groups
    ]
    return jnp.concatenate(cuts, axis=1)


def sum_copies(own, away):
    got = [swap(part, "r", m + 1) for m, part in enumerate(away)]
    total = own()
    for part in got:
        total = total + part.astype(F32)
    return total.astype(BF)


def gather_seq(value):
    count = lax.axis_size("seq")
    found = {0: value}
    step = count // 2
    while step >= 1:
        for j in list(found):
            found[j ^ step] = swap(found[j], "seq", step)
        step //= 2
    return [found[j] for j in range(count)]


def assemble_kernel(counts, spot_ref, *refs):
    n_in, n_out, part = counts
    ins, outs = refs[:n_in], refs[n_in:]
    width = outs[0].shape[1]
    for j in range(n_in):
        for o in range(n_out):
            cut = ins[j][0, :, o * width : (o + 1) * width]
            outs[o][j * part : (j + 1) * part, :] = cut.astype(F32)


def assemble(parts, columns, n_out):
    spans, blocks, part, width = parts.shape
    width //= n_out
    rows = part * spans
    spots = jnp.stack([jnp.asarray(c, jnp.int32) for c in columns])
    return pl.pallas_call(
        functools.partial(assemble_kernel, (spans, n_out, part)),
        grid_spec=pltpu.PrefetchScalarGridSpec(
            num_scalar_prefetch=1,
            grid=(blocks,),
            in_specs=[
                pl.BlockSpec((None, 1, part, n_out * width), lambda i, s, j=j: (j, i, 0, 0))
                for j in range(spans)
            ],
            out_specs=[pl.BlockSpec((rows, width), lambda i, s: (0, s[i]))] * n_out,
        ),
        out_shape=[jax.ShapeDtypeStruct((rows, blocks * width), F32)] * n_out,
        cost_estimate=pl.CostEstimate(
            flops=0, bytes_accessed=6 * n_out * rows * blocks * width, transcendentals=0
        ),
        compiler_params=pltpu.CompilerParams(vmem_limit_bytes=56 << 20),
    )(spots, *([parts] * spans))


def line_sum(chunks):
    count, spot = lax.axis_size("seq"), lax.axis_index("seq")
    half = count // 2
    totals, last = [], {}

    def send(value, key, pairs):
        if key in last:
            value = after(value, last[key])
        last[key] = lax.ppermute(value, "seq", pairs)
        return value, last[key]

    for value in chunks:
        for i in range(half - 1):
            value, got = send(value, ("in", i), [(i, i + 1), (count - 1 - i, count - 2 - i)])
            value = value + got
        value, got = send(value, "across", [(half - 1, half), (half, half - 1)])
        value = value + got
        for i in range(half - 2, -1, -1):
            value, got = send(value, ("out", i), [(i + 1, i), (count - 2 - i, count - 1 - i)])
            value = jnp.where((spot == i) | (spot == count - 1 - i), got, value)
        totals.append(value)
    return totals


def spread_line(near, far, here):
    got = [far[0], swap(near[0], "p", 1), swap(far[1], "p", 2), swap(near[1], "p", 3)]
    return assemble(jnp.stack(got)[None], [here ^ k for k in range(HEADS)], 2)


def swap_diagonal(part):
    count = lax.axis_size("seq")
    sends = [(p * count + z, (p ^ z) * count + z) for p in range(HEADS) for z in range(count)]
    return lax.ppermute(part, ("p", "seq"), sends)


def body(
    tokens,
    seq_lengths,
    attn_gain,
    query_proj,
    key_proj,
    value_proj,
    decay_down,
    decay_up,
    decay_bias,
    swish_proj,
    slot_gain,
    out_proj,
    mlp_gain,
    mlp_gate,
    mlp_up,
    mlp_down,
    grad_out,
):
    rows = tokens.shape[0]
    copies = lax.axis_size("r")
    owners = HEADS * copies
    shard = D // owners
    here, turn, place = lax.axis_index("p"), lax.axis_index("r"), lax.axis_index("seq")
    group = HEADS * rows

    small = [attn_gain, decay_down, decay_up, decay_bias, slot_gain, mlp_gain, seq_lengths]
    packed = jnp.concatenate([a.astype(F32).reshape(-1) for a in small])
    packed = gather_small(packed[None], here, turn)
    fields, offset = [], 0
    for a in small:
        fields.append(packed[:, offset : offset + a.size])
        offset += a.size
    gain_one = fields[0].reshape(D)
    down_full = fields[1].reshape(D, RANK).astype(BF)
    up_full = fields[2].reshape(owners, RANK, -1).transpose(1, 0, 2).reshape(RANK, HEADS * SLOTS)
    up_head = lax.dynamic_slice_in_dim(up_full, here * SLOTS, SLOTS, 1)
    bias_head = lax.dynamic_slice_in_dim(fields[3].reshape(HEADS * SLOTS), here * SLOTS, SLOTS, 0)
    gain_head = lax.dynamic_slice_in_dim(fields[4].reshape(D), here * HEAD, HEAD, 0)
    gain_head8 = jnp.broadcast_to(gain_head[None], (8, HEAD))
    gain_two = fields[5].reshape(D)
    lengths = fields[6].reshape(HEADS, copies)
    positions = (place * rows + jnp.arange(rows, dtype=jnp.int32)).astype(F32)
    masks = [
        (positions < lax.dynamic_index_in_dim(lengths, here ^ k, 0, False)[turn]).astype(F32)
        for k in range(HEADS)
    ]
    mask_all = jnp.concatenate(masks)[:, None]
    mask_own = masks[0][:, None]

    token_blocks = gather_heads(tokens)
    weight_kv, kv_pieces = head_columns([key_proj, value_proj], here)
    late = lax.optimization_barrier((query_proj, swish_proj, mlp_gate, mlp_up) + tuple(kv_pieces))
    weight_qs, qs_pieces = head_columns(late[:2], here)
    gu_pieces = seq_pieces(late[2:4], here)
    grad_blocks = gather_heads(after(grad_out, *qs_pieces))
    weight_out = lax.all_gather(out_proj, "r", axis=0, tiled=True)
    weight_down = lax.all_gather(mlp_down, "r", axis=0, tiled=True)

    tokens_all = jnp.concatenate(token_blocks).astype(F32)
    normed = (tokens_all * inverse_rms(tokens_all) * gain_one).astype(BF)
    kv = mm(normed, weight_kv).astype(BF).reshape(HEADS, rows, 2 * HEAD)
    gate_low = mm(normed, down_full)
    forget = exact(gate_low, up_head) + bias_head
    log_sig = jax.nn.log_sigmoid(forget) / NORMALIZER
    li = jnp.concatenate([mask_all * log_sig, mask_all * -jnp.expm1(log_sig)], axis=1)
    li = li.reshape(HEADS, rows, 2 * SLOTS)
    state, decay = chunk_states(kv, li)
    decay = decay[:, :, :1]
    init = chain_pair(state, decay, True)
    init, gu_pieces = lax.optimization_barrier((init, gu_pieces))
    weight_gu = seq_columns(gu_pieces, here)
    qs = mm(normed, weight_qs).reshape(HEADS, rows, 2 * HEAD)
    gated, mixer_out, probs, mix = mixer_forward(qs, kv, li, init, gain_head8)
    gated = gated.reshape(group, HEAD)
    attn_part = mm(gated, weight_out).astype(BF).reshape(HEADS, rows, D)
    grad_mlp = (mask_all * jnp.concatenate(grad_blocks).astype(F32)).astype(BF)
    attn_out, grad_act = scatter_heads(
        [attn_part[k] for k in range(HEADS)], mm_nt(grad_mlp, weight_down)
    )

    tokens_f = tokens.astype(F32)
    residual = tokens_f + mask_own * attn_out
    scale_two = inverse_rms(residual)
    hat_two = residual * scale_two
    normed_two_own = (hat_two * gain_two).astype(BF)
    normed_two = jnp.concatenate(gather_heads(normed_two_own))

    hidden_width = weight_down.shape[0]
    gate_up = mm(normed_two, weight_gu)
    gate_pre, up_pre = gate_up[:, :hidden_width], gate_up[:, hidden_width:]
    hidden = (jax.nn.silu(gate_pre) * up_pre).astype(BF)
    grad_gate = (grad_act * up_pre * silu_slope(gate_pre)).astype(BF)
    grad_up = (grad_act * jax.nn.silu(gate_pre)).astype(BF)
    grad_gu = jnp.concatenate([grad_gate, grad_up], axis=1)
    order = [here ^ k for k in range(HEADS)]
    hops = range(1, copies)
    down_rows = mlp_down.shape[0]
    two_view = normed_two.reshape(group, HEADS, copies, shard)
    gu_away = [mm_tn(split_rows(two_view, turn, m, order), grad_gu).astype(BF) for m in hops]
    two_part = mm_nt(after(grad_gu, *gu_away), weight_gu).astype(BF)
    gu_total = sum_copies(
        lambda: mm_tn(split_rows(two_view, turn, 0, order), after(grad_gu, two_part)), gu_away
    )
    gu_part = lax.psum_scatter(
        gu_total.reshape(HEADS, shard, 2 * hidden_width), "seq", scatter_dimension=0, tiled=True
    )
    hidden_late = after(hidden, gu_total)

    def down_grad_part(m):
        cut = lax.dynamic_slice_in_dim(hidden_late, (turn ^ m) * down_rows, down_rows, 1)
        return mm_tn(cut, grad_mlp)

    down_total = sum_copies(
        lambda: down_grad_part(0), [down_grad_part(m).astype(BF) for m in hops]
    )
    two_part = two_part.reshape(HEADS, rows, D)
    grad_norm_two, down_total = scatter_heads([two_part[k] for k in range(HEADS)], down_total)
    gain_two_grad = jnp.sum(grad_norm_two * hat_two, axis=0)
    grad_rows = grad_out.astype(F32)
    grad_resid = grad_rows + norm_back(grad_norm_two * gain_two, hat_two, scale_two)
    grad_attn_own = (mask_own * grad_resid).astype(BF)
    attn_blocks = gather_heads(grad_attn_own)
    mlp_part = mm(hidden, weight_down).astype(BF)
    mlp_part, gu_part, *attn_blocks = lax.optimization_barrier((mlp_part, gu_part, *attn_blocks))
    gu_part = swap_diagonal(gu_part)
    grad_attn = jnp.concatenate(attn_blocks)
    mlp_part = mlp_part.reshape(HEADS, rows, D)
    mlp_out = scatter_heads([mlp_part[k] for k in range(HEADS)])
    result = (residual + mask_own * mlp_out).astype(BF)

    grad_gated = mm_nt(grad_attn, weight_out).reshape(HEADS, rows, HEAD)
    grad_qs, grad_kv, grad_li, adjoint, slot_part = mixer_backward(
        qs, kv, li, init, gain_head8, mixer_out, probs, mix, grad_gated
    )
    adjoint, gu_part = lax.optimization_barrier((adjoint, gu_part))
    gu_whole = lax.all_gather(gu_part, "seq", axis=0, tiled=True)
    one_view = normed.reshape(group, HEADS, copies, shard)
    one_views = [split_rows(one_view, turn, m, order) for m in range(copies)]
    out_view = gated.reshape(group, 1, copies, shard)
    out_views = [split_rows(out_view, turn, m, [0]) for m in range(copies)]

    def weight_grad(views, right):
        return sum_copies(
            lambda: mm_tn(views[0], right), [mm_tn(views[m], right).astype(BF) for m in hops]
        )

    grad_qs = grad_qs.reshape(group, 2 * HEAD)
    out_total = weight_grad(out_views, grad_attn)
    qs_total = weight_grad(one_views, grad_qs)
    ends = chain_pair(adjoint, decay, False)
    ends, out_total, qs_total = lax.optimization_barrier((ends, out_total, qs_total))
    grad_kv, grad_li = mixer_finish(kv, li, init, ends, grad_kv, grad_li)
    grad_kv = grad_kv.reshape(group, 2 * HEAD)
    grad_li = grad_li.reshape(group, 2 * SLOTS)
    grad_decay = (
        mask_all
        * (grad_li[:, :SLOTS] - grad_li[:, SLOTS:] * jnp.exp(log_sig))
        / NORMALIZER
        * jax.nn.sigmoid(-forget)
    )
    bias_part = jnp.sum(grad_decay, axis=0)
    up_part = lax.dot_general(
        gate_low, grad_decay, (((0,), (0,)), ((), ())), precision=HIGHEST, preferred_element_type=F32
    )
    grad_low = lax.dot_general(
        grad_decay, up_head, (((1,), (1,)), ((), ())), precision=HIGHEST, preferred_element_type=F32
    ).astype(BF)
    down_low_part = mm_tn(normed, grad_low)

    one_part = (
        (mm_nt(grad_qs, weight_qs) + mm_nt(grad_kv, weight_kv) + mm_nt(grad_low, down_full))
        .astype(BF)
        .reshape(HEADS, rows, D)
    )
    kv_total = weight_grad(one_views, grad_kv)
    grad_norm_one, kv_total = scatter_heads([one_part[k] for k in range(HEADS)], kv_total)

    qs_total = qs_total.reshape(HEADS, shard, 2 * HEAD)
    kv_total = kv_total.reshape(HEADS, shard, 2 * HEAD)
    half_rows = down_rows // 2
    first = after(down_total[:half_rows], gu_whole, one_part)
    chunks = [first, down_total[half_rows:], out_total]
    chunks += [qs_total[1::2], qs_total[0::2], kv_total[1::2], kv_total[0::2]]
    near, far, out_grad, *wide = line_sum(chunks)
    down_grad = jnp.concatenate([near, far])
    gate_grad, up_grad = assemble(gu_whole[None], order, 2)
    query_grad, swish_grad = spread_line(wide[0], wide[1], here)
    key_grad, value_grad = spread_line(wide[2], wide[3], here)
    out_grad = out_grad.astype(F32)
    scale_one = inverse_rms(tokens_f)
    hat_one = tokens_f * scale_one
    gain_one_grad = jnp.sum(grad_norm_one * hat_one, axis=0)
    grad_tokens = (grad_resid + norm_back(grad_norm_one * gain_one, hat_one, scale_one)).astype(BF)

    def placed(part, width):
        whole = jnp.zeros(part.shape[:-1] + (HEADS * width,), F32)
        return lax.dynamic_update_slice_in_dim(whole, part, here * width, part.ndim - 1)

    up_sum = placed(up_part, SLOTS).reshape(RANK, HEADS, copies, -1).transpose(1, 2, 0, 3)
    sums = [
        gain_one_grad,
        down_low_part,
        up_sum,
        placed(bias_part, SLOTS),
        placed(slot_part[0], HEAD),
        gain_two_grad,
    ]
    flat = jnp.concatenate([a.reshape(HEADS, copies, -1) for a in sums], axis=2)
    flat = sum_small(flat, here, turn)
    totals, offset = [], 0
    for a in sums:
        size = a.size // owners
        totals.append(flat[offset : offset + size])
        offset += size

    return (
        result,
        grad_tokens,
        totals[0],
        query_grad,
        key_grad,
        value_grad,
        totals[1].reshape(shard, RANK),
        totals[2].reshape(RANK, -1),
        totals[3],
        swish_grad,
        totals[4],
        out_grad,
        totals[5],
        gate_grad,
        up_grad,
        down_grad.astype(F32),
    )


def solution(mesh):
    count, span = mesh.devices.shape
    split = Mesh(mesh.devices.reshape(HEADS, count // HEADS, span), ("p", "r", "seq"))
    rows = P(("p", "r", "seq"), None)
    matrix, vector, last = P(("p", "r"), None), P(("p", "r")), P(None, ("p", "r"))
    in_specs = (
        rows, vector, vector, matrix, matrix, matrix, matrix, last, vector, matrix, vector, matrix,
        vector, matrix, matrix, matrix, rows,
    )
    out_specs = (
        rows, rows, vector, matrix, matrix, matrix, matrix, last, vector, matrix, vector, matrix,
        vector, matrix, matrix, matrix,
    )
    return jax.shard_map(body, mesh=split, in_specs=in_specs, out_specs=out_specs, check_vma=False)
```

```python
import functools
import jax
import jax.numpy as jnp
from jax import lax
from jax.experimental import pallas as pl
from jax.experimental.pallas import tpu as pltpu
from jax.sharding import Mesh, PartitionSpec as P

HEAD = 512
SLOTS = 64
SCALE = HEAD ** (-0.5)
EPSILON = 1e-06
HIGHEST = lax.Precision.HIGHEST
BF = jnp.bfloat16
F32 = jnp.float32


def mm(a, b):
    return lax.dot_general(a, b, (((1,), (0,)), ((), ())), preferred_element_type=F32)


def mm_nt(a, b):
    return lax.dot_general(a, b, (((1,), (1,)), ((), ())), preferred_element_type=F32)


def mm_tn(a, b):
    return lax.dot_general(a, b, (((0,), (0,)), ((), ())), preferred_element_type=F32)


def exact(a, b):
    return lax.dot_general(
        a, b, (((1,), (0,)), ((), ())), precision=HIGHEST, preferred_element_type=F32
    )


def row_bit(rows, level):
    t = lax.broadcasted_iota(jnp.int32, (rows, SLOTS), 0)
    return ((t >> level) & 1) == 1


def prefix_levels(log_decay):
    rows = log_decay.shape[0]
    levels = rows.bit_length() - 1
    f, g = log_decay, jnp.zeros_like(log_decay)
    out = []
    for level in range(levels):
        out.append((f, g))
        total = f + g
        step = 1 << level
        bit = row_bit(rows, level)
        f = f + jnp.where(bit, pltpu.roll(total, step, 0), 0.0)
        g = g + jnp.where(bit, 0.0, pltpu.roll(total, rows - step, 0))
    return out, f, g


def same_block(rows, level):
    t = lax.broadcasted_iota(jnp.int32, (rows, rows), 0)
    s = lax.broadcasted_iota(jnp.int32, (rows, rows), 1)
    return (t >> (level + 1)) == (s >> (level + 1))


def level_mask(table, level, levels):
    if level == levels - 1:
        return table
    return jnp.where(same_block(table.shape[0], level), table, jnp.zeros_like(table))


def factors(pair, level, inflow):
    f, g = pair
    bit = row_bit(f.shape[0], level)
    left = jnp.where(bit, jnp.exp(f), 0.0)
    right = jnp.where(bit, 0.0, jnp.exp(g))
    return left, right, right * inflow


def diagonal(rows):
    t = lax.broadcasted_iota(jnp.int32, (rows, rows), 0)
    s = lax.broadcasted_iota(jnp.int32, (rows, rows), 1)
    return t == s


def slot_table(weights, pairs, inflow):
    rows = weights.shape[0]
    levels = len(pairs)
    table = jnp.where(diagonal(rows), jnp.sum(weights * inflow, axis=1, keepdims=True), 0.0)
    for level in range(levels):
        left, _, gain = factors(pairs[level], level, inflow)
        block = mm_nt((weights * left).astype(BF), gain.astype(BF))
        table = table + level_mask(block, level, levels)
    return table


def slot_sums(table, pairs, inflow):
    rows = table.shape[0]
    levels = len(pairs)
    own = jnp.sum(jnp.where(diagonal(rows), table, 0.0), axis=1, keepdims=True)
    low = table.astype(BF)
    total = own * inflow
    for level in range(levels):
        left, _, gain = factors(pairs[level], level, inflow)
        total = total + left * mm(level_mask(low, level, levels), gain.astype(BF))
    return total


def states_kernel(kv_ref, li_ref, state_ref, decay_ref):
    kv = kv_ref[0]
    log_decay = li_ref[0, :, :SLOTS]
    inflow = li_ref[0, :, SLOTS:]
    rows = kv.shape[0]
    t = lax.broadcasted_iota(jnp.int32, (rows, rows), 0)
    s = lax.broadcasted_iota(jnp.int32, (rows, rows), 1)
    after = exact((s > t).astype(F32), log_decay)
    weight = jnp.exp(after) * inflow
    state_ref[0] = mm_tn(weight.astype(BF), kv)
    total = lax.dot_general(
        log_decay, jnp.ones((rows, 128), F32), (((0,), (0,)), ((), ())),
        precision=HIGHEST, preferred_element_type=F32,
    )
    decay_ref[0] = jnp.exp(total)


def forward_kernel(qs_ref, kv_ref, li_ref, init_ref, gain_ref, gated_ref, out_ref, prob_ref, mix_ref):
    queries = qs_ref[0, :, :HEAD].astype(BF)
    swish = qs_ref[0, :, HEAD:]
    keys = kv_ref[0, :, :HEAD]
    values = kv_ref[0, :, HEAD:]
    log_decay = li_ref[0, :, :SLOTS]
    inflow = li_ref[0, :, SLOTS:]
    init = init_ref[0].astype(BF)
    pairs, running, _ = prefix_levels(log_decay)
    growth = jnp.exp(running)
    scores = mm_nt(queries, keys) * SCALE
    slots = slot_sums(scores, pairs, inflow) + mm_nt(queries, init[:, :HEAD]) * SCALE * growth
    top = jnp.max(slots, axis=1, keepdims=True)
    weights = jnp.exp(slots - top)
    probs = weights / jnp.sum(weights, axis=1, keepdims=True)
    mix = slot_table(probs, pairs, inflow).astype(BF)
    out = mm(mix, values) + mm((probs * growth).astype(BF), init[:, HEAD:])
    hat = out * lax.rsqrt(jnp.mean(out * out, axis=1, keepdims=True) + EPSILON)
    gated_ref[0] = (hat * gain_ref[0:1] * (swish * jax.nn.sigmoid(swish))).astype(BF)
    out_ref[0] = out
    prob_ref[0] = probs
    mix_ref[0] = mix


def backward_kernel(
    qs_ref, kv_ref, li_ref, init_ref, gain_ref, out_ref, prob_ref, mix_ref, gg_ref,
    dqs_ref, dkv_ref, ddi_ref, adj_ref, sg_ref,
):
    queries = qs_ref[0, :, :HEAD].astype(BF)
    swish = qs_ref[0, :, HEAD:]
    keys = kv_ref[0, :, :HEAD]
    values = kv_ref[0, :, HEAD:]
    log_decay = li_ref[0, :, :SLOTS]
    inflow = li_ref[0, :, SLOTS:]
    init = init_ref[0].astype(BF)
    out = out_ref[0]
    probs = prob_ref[0]
    gain = gain_ref[0:1]
    rows = out.shape[0]
    scale_out = lax.rsqrt(jnp.mean(out * out, axis=1, keepdims=True) + EPSILON)
    hat = out * scale_out
    sig = jax.nn.sigmoid(swish)
    silu = swish * sig
    gg = gg_ref[0].astype(F32)
    gg_hat = gg * hat
    dqs_ref[0, :, HEAD:] = (gg_hat * gain * (sig * (1.0 + swish * (1.0 - sig)))).astype(BF)
    part = jnp.broadcast_to(jnp.sum(gg_hat * silu, axis=0, keepdims=True), (8, HEAD))

    @pl.when(pl.program_id(0) == 0)
    def _():
        sg_ref[...] = part

    @pl.when(pl.program_id(0) > 0)
    def _():
        sg_ref[...] = sg_ref[...] + part

    grad_hat = gg * gain * silu
    dout = scale_out * (grad_hat - hat * jnp.mean(grad_hat * hat, axis=1, keepdims=True))
    dout = dout.astype(BF)
    pairs, running, _ = prefix_levels(log_decay)
    levels = len(pairs)
    growth = jnp.exp(running)
    scores = mm_nt(queries, keys) * SCALE
    grads = mm_nt(dout, values)
    key_part = mm_nt(queries, init[:, :HEAD]) * SCALE * growth
    value_part = mm_nt(dout, init[:, HEAD:]) * growth
    dprob = slot_sums(grads, pairs, inflow) + value_part
    dslot = probs * (dprob - jnp.sum(probs * dprob, axis=1, keepdims=True))
    back = slot_table(dslot, pairs, inflow).astype(BF)
    dslot_g = (dslot * growth).astype(BF)
    prob_g = (probs * growth).astype(BF)
    dqs_ref[0, :, :HEAD] = (SCALE * (mm(back, keys) + mm(dslot_g, init[:, :HEAD]))).astype(BF)
    dkv_ref[0, :, :HEAD] = SCALE * mm_tn(back, queries)
    dkv_ref[0, :, HEAD:] = mm_tn(mix_ref[0], dout)
    adj_ref[0, :, :HEAD] = SCALE * mm_tn(dslot_g, queries)
    adj_ref[0, :, HEAD:] = mm_tn(prob_g, dout)
    diag = diagonal(rows)
    own_a = jnp.sum(jnp.where(diag, scores, 0.0), axis=1, keepdims=True)
    own_b = jnp.sum(jnp.where(diag, grads, 0.0), axis=1, keepdims=True)
    dinflow = dslot * own_a + probs * own_b
    scores_low = scores.astype(BF)
    grads_low = grads.astype(BF)
    fbar = dslot * key_part + probs * value_part
    gbar = jnp.zeros_like(fbar)
    for level in range(levels - 1, -1, -1):
        left, right, amount = factors(pairs[level], level, inflow)
        table_a = level_mask(scores_low, level, levels)
        table_b = level_mask(grads_low, level, levels)
        amount_low = amount.astype(BF)
        dleft = dslot * left
        pleft = probs * left
        grow = dleft * mm(table_a, amount_low) + pleft * mm(table_b, amount_low)
        back_in = mm_tn(table_a, dleft.astype(BF)) + mm_tn(table_b, pleft.astype(BF))
        dinflow = dinflow + right * back_in
        step = 1 << level
        bit = row_bit(rows, level)
        total = pltpu.roll(jnp.where(bit, fbar, 0.0), rows - step, 0) + pltpu.roll(
            jnp.where(bit, 0.0, gbar), step, 0
        )
        fbar = fbar + grow + total
        gbar = gbar + amount * back_in + total
    ddi_ref[0, :, :SLOTS] = fbar
    ddi_ref[0, :, SLOTS:] = dinflow


def finish_kernel(kv_ref, li_ref, init_ref, end_ref, dkv_ref, ddi_ref, okv_ref, oddi_ref):
    kv = kv_ref[0]
    log_decay = li_ref[0, :, :SLOTS]
    inflow = li_ref[0, :, SLOTS:]
    end = end_ref[0]
    rows = kv.shape[0]
    t = lax.broadcasted_iota(jnp.int32, (rows, rows), 0)
    s = lax.broadcasted_iota(jnp.int32, (rows, rows), 1)
    earlier = (s < t).astype(F32)
    after = exact((s > t).astype(F32), log_decay)
    fade = jnp.exp(after)
    weight = fade * inflow
    end_low = end.astype(BF)
    okv_ref[0] = (dkv_ref[0] + mm(weight.astype(BF), end_low)).astype(BF)
    reach = mm_nt(kv, end_low)
    whole = jnp.exp(jnp.sum(log_decay, axis=0, keepdims=True))
    carry = lax.dot_general(
        jnp.ones((8, 2 * HEAD), F32), end * init_ref[0], (((1,), (1,)), ((), ())),
        precision=HIGHEST, preferred_element_type=F32,
    )[0:1]
    oddi_ref[0, :, :SLOTS] = (
        ddi_ref[0, :, :SLOTS] + exact(earlier, weight * reach) + whole * carry
    )
    oddi_ref[0, :, SLOTS:] = ddi_ref[0, :, SLOTS:] + fade * reach


def blocked(shape):
    return pl.BlockSpec((1,) + shape, lambda i: (i, 0, 0))


def run(kernel, args, specs, outs, out_specs, flops, moved):
    return pl.pallas_call(
        kernel,
        grid=(args[0].shape[0],),
        in_specs=specs,
        out_specs=out_specs,
        out_shape=outs,
        cost_estimate=pl.CostEstimate(flops=flops, bytes_accessed=moved, transcendentals=0),
        compiler_params=pltpu.CompilerParams(vmem_limit_bytes=56 << 20),
    )(*args)


def sds(shape, dtype=F32):
    return jax.ShapeDtypeStruct(shape, dtype)


def chunk_states(kv, li):
    n, rows, _ = kv.shape
    return run(
        states_kernel, (kv, li),
        [blocked((rows, 2 * HEAD)), blocked((rows, 2 * SLOTS))],
        (sds((n, SLOTS, 2 * HEAD)), sds((n, SLOTS, 128))),
        (blocked((SLOTS, 2 * HEAD)), blocked((SLOTS, 128))),
        n * 10**9, n * 10**6,
    )


def mixer_forward(qs, kv, li, init, gain):
    n, rows, _ = kv.shape
    return run(
        forward_kernel, (qs, kv, li, init, gain),
        [blocked((rows, 2 * HEAD)), blocked((rows, 2 * HEAD)), blocked((rows, 2 * SLOTS)),
         blocked((SLOTS, 2 * HEAD)), pl.BlockSpec((8, HEAD), lambda i: (0, 0))],
        (sds((n, rows, HEAD), BF), sds((n, rows, HEAD)), sds((n, rows, SLOTS)), sds((n, rows, rows), BF)),
        (blocked((rows, HEAD)), blocked((rows, HEAD)), blocked((rows, SLOTS)), blocked((rows, rows))),
        n * 3 * 10**9, n * 4 * 10**6,
    )


def mixer_backward(qs, kv, li, init, gain, out, probs, mix, gg):
    n, rows, _ = kv.shape
    return run(
        backward_kernel, (qs, kv, li, init, gain, out, probs, mix, gg),
        [blocked((rows, 2 * HEAD)), blocked((rows, 2 * HEAD)), blocked((rows, 2 * SLOTS)),
         blocked((SLOTS, 2 * HEAD)), pl.BlockSpec((8, HEAD), lambda i: (0, 0)),
         blocked((rows, HEAD)), blocked((rows, SLOTS)), blocked((rows, rows)), blocked((rows, HEAD))],
        (sds((n, rows, 2 * HEAD), BF), sds((n, rows, 2 * HEAD)), sds((n, rows, 2 * SLOTS)),
         sds((n, SLOTS, 2 * HEAD)), sds((8, HEAD))),
        (blocked((rows, 2 * HEAD)), blocked((rows, 2 * HEAD)), blocked((rows, 2 * SLOTS)),
         blocked((SLOTS, 2 * HEAD)), pl.BlockSpec((8, HEAD), lambda i: (0, 0))),
        n * 6 * 10**9, n * 5 * 10**6,
    )


def mixer_finish(kv, li, init, end, dkv, ddi):
    n, rows, _ = kv.shape
    return run(
        finish_kernel, (kv, li, init, end, dkv, ddi),
        [blocked((rows, 2 * HEAD)), blocked((rows, 2 * SLOTS)), blocked((SLOTS, 2 * HEAD)),
         blocked((SLOTS, 2 * HEAD)), blocked((rows, 2 * HEAD)), blocked((rows, 2 * SLOTS))],
        (sds((n, rows, 2 * HEAD), BF), sds((n, rows, 2 * SLOTS))),
        (blocked((rows, 2 * HEAD)), blocked((rows, 2 * SLOTS))),
        n * 10**9, n * 3 * 10**6,
    )


D = 2048
HEADS = 4
RANK = 16
NORMALIZER = 8.0


def inverse_rms(values):
    return lax.rsqrt(jnp.mean(values * values, axis=-1, keepdims=True) + EPSILON)


def silu_slope(values):
    sigmoid_val = jax.nn.sigmoid(values)
    return sigmoid_val * (1.0 + values * (1.0 - sigmoid_val))


def norm_back(grad_hat, hat_rows, scale_rows):
    return scale_rows * (
        grad_hat - hat_rows * jnp.mean(grad_hat * hat_rows, axis=-1, keepdims=True)
    )


def swap(value, axis, step):
    count = lax.axis_size(axis)
    return lax.ppermute(value, axis, [(i, i ^ step) for i in range(count)])


def gather_heads(block):
    return [block] + [swap(block, "p", k) for k in range(1, HEADS)]


def scatter_heads(parts, *fillers):
    got = [swap(parts[k], "p", k) for k in range(1, HEADS)]
    if fillers:
        held = lax.optimization_barrier(tuple(got) + fillers)
        got, fillers = held[: HEADS - 1], held[HEADS - 1 :]
    total = parts[0].astype(F32)
    for part in got:
        total = total + part.astype(F32)
    return (total,) + tuple(fillers) if fillers else total


def after(value, *others):
    return lax.optimization_barrier((value,) + others)[0]


def place_kernel(blocks, spot_ref, *refs):
    ins, out = refs[:-1], refs[-1]
    part = ins[0].shape[1]
    for i, ref in enumerate(ins):
        for k in range(blocks):
            start = pl.multiple_of(spot_ref[i * blocks + k] * part, part)
            out[pl.ds(start, part), :] = ref[k]


def place(parts, spots):
    blocks, part, width = parts[0].shape
    chunk = 256
    table = jnp.stack([jnp.asarray(x, jnp.int32) for row in spots for x in row])
    rows = len(parts) * blocks * part
    return pl.pallas_call(
        functools.partial(place_kernel, blocks),
        grid_spec=pltpu.PrefetchScalarGridSpec(
            num_scalar_prefetch=1,
            grid=(width // chunk,),
            in_specs=[pl.BlockSpec((blocks, part, chunk), lambda i, s: (0, 0, i))] * len(parts),
            out_specs=pl.BlockSpec((rows, chunk), lambda i, s: (0, i)),
        ),
        out_shape=jax.ShapeDtypeStruct((rows, width), BF),
        cost_estimate=pl.CostEstimate(flops=0, bytes_accessed=4 * rows * width, transcendentals=0),
        compiler_params=pltpu.CompilerParams(vmem_limit_bytes=56 << 20),
    )(table, *parts)


def column_cuts(shards, here, k):
    cuts = []
    for shard in shards:
        width = shard.shape[1] // HEADS
        cuts.append(lax.dynamic_slice_in_dim(shard, (here ^ k) * width, width, 1))
    return jnp.concatenate(cuts, axis=1)


def head_columns(shards, here):
    copies = lax.axis_size("r")
    turn = lax.axis_index("r")
    own = column_cuts(shards, here, 0)
    pieces = [own] + [swap(column_cuts(shards, here, k), "p", k) for k in range(1, HEADS)]
    parts, spots = [], []
    for k in range(HEADS):
        for m in range(copies):
            piece = pieces[k] if m == 0 else swap(pieces[k], "r", m)
            parts.append(piece[None])
            spots.append([(here ^ k) * copies + (turn ^ m)])
    return place(parts, spots), pieces[1:]


def seq_pieces(shards, here):
    rows = shards[0].shape[0] // 2
    start = lax.axis_index("seq") % 2 * rows
    shards = [lax.dynamic_slice_in_dim(shard, start, rows, 0) for shard in shards]
    own = column_cuts(shards, here, 0)
    return jnp.stack([own] + [swap(column_cuts(shards, here, k), "p", k) for k in range(1, HEADS)])


def seq_columns(pieces, here):
    copies, turn, half = lax.axis_size("r"), lax.axis_index("r"), lax.axis_index("seq") % 2
    parts, spots = [], []
    for j, part in enumerate([pieces, swap(pieces, "seq", 1)]):
        for m in range(copies):
            parts.append(part if m == 0 else swap(part, "r", m))
            spots.append(
                [((here ^ k) * copies + (turn ^ m)) * 2 + (half ^ j) for k in range(HEADS)]
            )
    return place(parts, spots)


def gather_small(packed, here, turn):
    copies = lax.axis_size("r")
    near = jnp.concatenate([packed] + [swap(packed, "r", m) for m in range(1, copies)])
    both = jnp.concatenate(gather_heads(near))
    heads = jnp.arange(HEADS, dtype=jnp.int32) ^ here
    turns = jnp.arange(copies, dtype=jnp.int32) ^ turn
    order = (heads[:, None] * copies + turns[None, :]).reshape(-1)
    return jnp.take(both, order, axis=0)


def sum_small(value, here, turn):
    mine = [lax.dynamic_index_in_dim(value, here ^ k, 0, False) for k in range(HEADS)]
    total = scatter_heads(mine)
    copies = lax.axis_size("r")
    kept = lax.dynamic_index_in_dim(total, turn, 0, True)
    for m in range(1, copies):
        kept = kept + swap(lax.dynamic_index_in_dim(total, turn ^ m, 0, True), "r", m)
    return kept[0]


def chain(state, decay, forward):
    count = lax.axis_size("seq")
    total = jnp.zeros_like(state)
    for hop in range(count - 1):
        pair = (hop, hop + 1) if forward else (count - 1 - hop, count - 2 - hop)
        sent = (decay * total + state).astype(BF)
        total = total + lax.ppermute(sent, "seq", [pair]).astype(F32)
    return total


def chain_pair(both, decay, forward):
    return jnp.concatenate(
        [chain(both[..., :HEAD], decay, forward), chain(both[..., HEAD:], decay, forward)], axis=-1
    )


def split_rows(left, turn, step, groups):
    copies, width = left.shape[2:]
    flat = left.reshape(left.shape[0], -1)
    cuts = [
        lax.dynamic_slice_in_dim(flat, (g * copies + (turn ^ step)) * width, width, 1)
        for g in groups
    ]
    return jnp.concatenate(cuts, axis=1)


def sum_copies(own, away):
    got = [swap(part, "r", m + 1) for m, part in enumerate(away)]
    total = own()
    for part in got:
        total = total + part.astype(F32)
    return total.astype(BF)


def assemble_kernel(counts, spot_ref, *refs):
    n_in, n_out, part = counts
    ins, outs = refs[:n_in], refs[n_in:]
    width = outs[0].shape[1]
    for j in range(n_in):
        for o in range(n_out):
            cut = ins[j][0, :, o * width : (o + 1) * width]
            outs[o][j * part : (j + 1) * part, :] = cut.astype(F32)


def assemble(parts, columns, n_out):
    spans, blocks, part, width = parts.shape
    width //= n_out
    rows = part * spans
    spots = jnp.stack([jnp.asarray(c, jnp.int32) for c in columns])
    return pl.pallas_call(
        functools.partial(assemble_kernel, (spans, n_out, part)),
        grid_spec=pltpu.PrefetchScalarGridSpec(
            num_scalar_prefetch=1,
            grid=(blocks,),
            in_specs=[
                pl.BlockSpec((None, 1, part, n_out * width), lambda i, s, j=j: (j, i, 0, 0))
                for j in range(spans)
            ],
            out_specs=[pl.BlockSpec((rows, width), lambda i, s: (0, s[i]))] * n_out,
        ),
        out_shape=[jax.ShapeDtypeStruct((rows, blocks * width), F32)] * n_out,
        cost_estimate=pl.CostEstimate(
            flops=0, bytes_accessed=6 * n_out * rows * blocks * width, transcendentals=0
        ),
        compiler_params=pltpu.CompilerParams(vmem_limit_bytes=56 << 20),
    )(spots, *([parts] * spans))


def line_sum(chunks):
    count, spot = lax.axis_size("seq"), lax.axis_index("seq")
    half = count // 2
    totals, last = [], {}

    def send(value, key, pairs):
        if key in last:
            value = after(value, last[key])
        last[key] = lax.ppermute(value, "seq", pairs)
        return value, last[key]

    for value in chunks:
        for i in range(half - 1):
            value, got = send(value, ("in", i), [(i, i + 1), (count - 1 - i, count - 2 - i)])
            value = value + got
        value, got = send(value, "across", [(half - 1, half), (half, half - 1)])
        value = value + got
        for i in range(half - 2, -1, -1):
            value, got = send(value, ("out", i), [(i + 1, i), (count - 2 - i, count - 1 - i)])
            value = jnp.where((spot == i) | (spot == count - 1 - i), got, value)
        totals.append(value)
    return totals


def spread_line(near, far, here):
    got = [far[0], swap(near[0], "p", 1), swap(far[1], "p", 2), swap(near[1], "p", 3)]
    return assemble(jnp.stack(got)[None], [here ^ k for k in range(HEADS)], 2)


def swap_diagonal(part):
    count = lax.axis_size("seq")
    sends = [(p * count + z, (p ^ z) * count + z) for p in range(HEADS) for z in range(count)]
    return lax.ppermute(part, ("p", "seq"), sends)


def body(
    tokens,
    seq_lengths,
    attn_gain,
    query_proj,
    key_proj,
    value_proj,
    decay_down,
    decay_up,
    decay_bias,
    swish_proj,
    slot_gain,
    out_proj,
    mlp_gain,
    mlp_gate,
    mlp_up,
    mlp_down,
    grad_out,
):
    rows = tokens.shape[0]
    copies = lax.axis_size("r")
    owners = HEADS * copies
    shard = D // owners
    here, turn, place = lax.axis_index("p"), lax.axis_index("r"), lax.axis_index("seq")
    group = HEADS * rows

    small = [attn_gain, decay_down, decay_up, decay_bias, slot_gain, mlp_gain, seq_lengths]
    packed = jnp.concatenate([a.astype(F32).reshape(-1) for a in small])
    packed = gather_small(packed[None], here, turn)
    fields, offset = [], 0
    for a in small:
        fields.append(packed[:, offset : offset + a.size])
        offset += a.size
    gain_one = fields[0].reshape(D)
    down_full = fields[1].reshape(D, RANK).astype(BF)
    up_full = fields[2].reshape(owners, RANK, -1).transpose(1, 0, 2).reshape(RANK, HEADS * SLOTS)
    up_head = lax.dynamic_slice_in_dim(up_full, here * SLOTS, SLOTS, 1)
    bias_head = lax.dynamic_slice_in_dim(fields[3].reshape(HEADS * SLOTS), here * SLOTS, SLOTS, 0)
    gain_head = lax.dynamic_slice_in_dim(fields[4].reshape(D), here * HEAD, HEAD, 0)
    gain_head8 = jnp.broadcast_to(gain_head[None], (8, HEAD))
    gain_two = fields[5].reshape(D)
    lengths = fields[6].reshape(HEADS, copies)
    positions = (place * rows + jnp.arange(rows, dtype=jnp.int32)).astype(F32)
    masks = [
        (positions < lax.dynamic_index_in_dim(lengths, here ^ k, 0, False)[turn]).astype(F32)
        for k in range(HEADS)
    ]
    mask_all = jnp.concatenate(masks)[:, None]
    mask_own = masks[0][:, None]

    token_blocks = gather_heads(tokens)
    weight_kv, kv_pieces = head_columns([key_proj, value_proj], here)
    late = lax.optimization_barrier((query_proj, swish_proj, mlp_gate, mlp_up) + tuple(kv_pieces))
    weight_qs, qs_pieces = head_columns(late[:2], here)
    gu_pieces = seq_pieces(late[2:4], here)
    grad_blocks = gather_heads(after(grad_out, *qs_pieces))
    weight_out = lax.all_gather(out_proj, "r", axis=0, tiled=True)
    weight_down = lax.all_gather(mlp_down, "r", axis=0, tiled=True)

    tokens_all = jnp.concatenate(token_blocks).astype(F32)
    normed = (tokens_all * inverse_rms(tokens_all) * gain_one).astype(BF)
    kv = mm(normed, weight_kv).astype(BF).reshape(HEADS, rows, 2 * HEAD)
    gate_low = mm(normed, down_full)
    forget = exact(gate_low, up_head) + bias_head
    log_sig = jax.nn.log_sigmoid(forget) / NORMALIZER
    li = jnp.concatenate([mask_all * log_sig, mask_all * -jnp.expm1(log_sig)], axis=1)
    li = li.reshape(HEADS, rows, 2 * SLOTS)
    state, decay = chunk_states(kv, li)
    decay = decay[:, :, :1]
    init = chain_pair(state, decay, True)
    init, gu_pieces = lax.optimization_barrier((init, gu_pieces))
    weight_gu = seq_columns(gu_pieces, here)
    qs = mm(normed, weight_qs).reshape(HEADS, rows, 2 * HEAD)
    gated, mixer_out, probs, mix = mixer_forward(qs, kv, li, init, gain_head8)
    gated = gated.reshape(group, HEAD)
    attn_part = mm(gated, weight_out).astype(BF).reshape(HEADS, rows, D)
    grad_mlp = (mask_all * jnp.concatenate(grad_blocks).astype(F32)).astype(BF)
    attn_out, grad_act = scatter_heads(
        [attn_part[k] for k in range(HEADS)], mm_nt(grad_mlp, weight_down)
    )

    tokens_f = tokens.astype(F32)
    residual = tokens_f + mask_own * attn_out
    scale_two = inverse_rms(residual)
    hat_two = residual * scale_two
    normed_two_own = (hat_two * gain_two).astype(BF)
    normed_two = jnp.concatenate(gather_heads(normed_two_own))

    hidden_width = weight_down.shape[0]
    gate_up = mm(normed_two, weight_gu)
    gate_pre, up_pre = gate_up[:, :hidden_width], gate_up[:, hidden_width:]
    hidden = (jax.nn.silu(gate_pre) * up_pre).astype(BF)
    grad_gate = (grad_act * up_pre * silu_slope(gate_pre)).astype(BF)
    grad_up = (grad_act * jax.nn.silu(gate_pre)).astype(BF)
    grad_gu = jnp.concatenate([grad_gate, grad_up], axis=1)
    order = [here ^ k for k in range(HEADS)]
    hops = range(1, copies)
    down_rows = mlp_down.shape[0]
    two_view = normed_two.reshape(group, HEADS, copies, shard)
    gu_away = [mm_tn(split_rows(two_view, turn, m, order), grad_gu).astype(BF) for m in hops]
    two_part = mm_nt(after(grad_gu, *gu_away), weight_gu).astype(BF)
    gu_total = sum_copies(
        lambda: mm_tn(split_rows(two_view, turn, 0, order), after(grad_gu, two_part)), gu_away
    )
    gu_part = lax.psum_scatter(
        gu_total.reshape(HEADS, shard, 2 * hidden_width), "seq", scatter_dimension=0, tiled=True
    )
    hidden_late = after(hidden, gu_total)

    def down_grad_part(m):
        cut = lax.dynamic_slice_in_dim(hidden_late, (turn ^ m) * down_rows, down_rows, 1)
        return mm_tn(cut, grad_mlp)

    down_total = sum_copies(
        lambda: down_grad_part(0), [down_grad_part(m).astype(BF) for m in hops]
    )
    two_part = two_part.reshape(HEADS, rows, D)
    grad_norm_two, down_total = scatter_heads([two_part[k] for k in range(HEADS)], down_total)
    gain_two_grad = jnp.sum(grad_norm_two * hat_two, axis=0)
    grad_rows = grad_out.astype(F32)
    grad_resid = grad_rows + norm_back(grad_norm_two * gain_two, hat_two, scale_two)
    grad_attn_own = (mask_own * grad_resid).astype(BF)
    attn_blocks = gather_heads(grad_attn_own)
    mlp_part = mm(hidden, weight_down).astype(BF)
    mlp_part, gu_part, *attn_blocks = lax.optimization_barrier((mlp_part, gu_part, *attn_blocks))
    gu_part = swap_diagonal(gu_part)
    grad_attn = jnp.concatenate(attn_blocks)
    mlp_part = mlp_part.reshape(HEADS, rows, D)
    mlp_out = scatter_heads([mlp_part[k] for k in range(HEADS)])

    grad_gated = mm_nt(grad_attn, weight_out).reshape(HEADS, rows, HEAD)
    grad_qs, grad_kv, grad_li, adjoint, slot_part = mixer_backward(
        qs, kv, li, init, gain_head8, mixer_out, probs, mix, grad_gated
    )
    adjoint, gu_part = lax.optimization_barrier((adjoint, gu_part))
    gu_whole = lax.all_gather(gu_part, "seq", axis=0, tiled=True)
    one_view = normed.reshape(group, HEADS, copies, shard)
    one_views = [split_rows(one_view, turn, m, order) for m in range(copies)]
    out_view = gated.reshape(group, 1, copies, shard)
    out_views = [split_rows(out_view, turn, m, [0]) for m in range(copies)]

    def weight_grad(views, right):
        return sum_copies(
            lambda: mm_tn(views[0], right), [mm_tn(views[m], right).astype(BF) for m in hops]
        )

    grad_qs = grad_qs.reshape(group, 2 * HEAD)
    out_total = weight_grad(out_views, grad_attn)
    qs_total = weight_grad(one_views, grad_qs)
    ends = chain_pair(adjoint, decay, False)
    ends, mlp_out, out_total, qs_total = lax.optimization_barrier(
        (ends, mlp_out, out_total, qs_total)
    )
    result = (residual + mask_own * mlp_out).astype(BF)
    grad_kv, grad_li = mixer_finish(kv, li, init, ends, grad_kv, grad_li)
    grad_kv = grad_kv.reshape(group, 2 * HEAD)
    grad_li = grad_li.reshape(group, 2 * SLOTS)
    grad_decay = (
        mask_all
        * (grad_li[:, :SLOTS] - grad_li[:, SLOTS:] * jnp.exp(log_sig))
        / NORMALIZER
        * jax.nn.sigmoid(-forget)
    )
    bias_part = jnp.sum(grad_decay, axis=0)
    up_part = lax.dot_general(
        gate_low, grad_decay, (((0,), (0,)), ((), ())), precision=HIGHEST, preferred_element_type=F32
    )
    grad_low = lax.dot_general(
        grad_decay, up_head, (((1,), (1,)), ((), ())), precision=HIGHEST, preferred_element_type=F32
    ).astype(BF)
    down_low_part = mm_tn(normed, grad_low)

    one_part = (
        (mm_nt(grad_qs, weight_qs) + mm_nt(grad_kv, weight_kv) + mm_nt(grad_low, down_full))
        .astype(BF)
        .reshape(HEADS, rows, D)
    )
    kv_total = weight_grad(one_views, grad_kv)
    grad_norm_one, kv_total = scatter_heads([one_part[k] for k in range(HEADS)], kv_total)

    scale_one = inverse_rms(tokens_f)
    hat_one = tokens_f * scale_one
    gain_one_grad = jnp.sum(grad_norm_one * hat_one, axis=0)
    grad_tokens = (grad_resid + norm_back(grad_norm_one * gain_one, hat_one, scale_one)).astype(BF)

    def placed(part, width):
        whole = jnp.zeros(part.shape[:-1] + (HEADS * width,), F32)
        return lax.dynamic_update_slice_in_dim(whole, part, here * width, part.ndim - 1)

    up_sum = placed(up_part, SLOTS).reshape(RANK, HEADS, copies, -1).transpose(1, 2, 0, 3)
    sums = [
        gain_one_grad,
        down_low_part,
        up_sum,
        placed(bias_part, SLOTS),
        placed(slot_part[0], HEAD),
        gain_two_grad,
    ]
    flat = jnp.concatenate([a.reshape(HEADS, copies, -1) for a in sums], axis=2)
    flat = sum_small(flat, here, turn)
    lanes = D * 8
    flat = jnp.pad(flat, (0, -flat.size % lanes)).astype(BF).reshape(-1, D)

    qs_total = qs_total.reshape(HEADS, shard, 2 * HEAD)
    kv_total = kv_total.reshape(HEADS, shard, 2 * HEAD)
    half_rows = down_rows // 2
    first = after(down_total[:half_rows], gu_whole, one_part)
    chunks = [first, down_total[half_rows:]]
    chunks += [qs_total[1::2], qs_total[0::2], kv_total[1::2], kv_total[0::2]]
    near, far, *wide, last = line_sum(chunks + [jnp.concatenate([out_total, flat])])
    down_grad = jnp.concatenate([near, far])
    gate_grad, up_grad = assemble(gu_whole[None], order, 2)
    query_grad, swish_grad = spread_line(wide[0], wide[1], here)
    key_grad, value_grad = spread_line(wide[2], wide[3], here)
    out_grad = last[:shard].astype(F32)
    flat = last[shard:].reshape(-1).astype(F32)
    totals, offset = [], 0
    for a in sums:
        size = a.size // owners
        totals.append(flat[offset : offset + size])
        offset += size

    return (
        result,
        grad_tokens,
        totals[0],
        query_grad,
        key_grad,
        value_grad,
        totals[1].reshape(shard, RANK),
        totals[2].reshape(RANK, -1),
        totals[3],
        swish_grad,
        totals[4],
        out_grad,
        totals[5],
        gate_grad,
        up_grad,
        down_grad.astype(F32),
    )


def solution(mesh):
    count, span = mesh.devices.shape
    split = Mesh(mesh.devices.reshape(HEADS, count // HEADS, span), ("p", "r", "seq"))
    rows = P(("p", "r", "seq"), None)
    matrix, vector, last = P(("p", "r"), None), P(("p", "r")), P(None, ("p", "r"))
    in_specs = (
        rows, vector, vector, matrix, matrix, matrix, matrix, last, vector, matrix, vector, matrix,
        vector, matrix, matrix, matrix, rows,
    )
    out_specs = (
        rows, rows, vector, matrix, matrix, matrix, matrix, last, vector, matrix, vector, matrix,
        vector, matrix, matrix, matrix,
    )
    return jax.shard_map(body, mesh=split, in_specs=in_specs, out_specs=out_specs, check_vma=False)
```

```python
import functools
import jax
import jax.numpy as jnp
from jax import lax
from jax.experimental import pallas as pl
from jax.experimental.pallas import tpu as pltpu
from jax.sharding import Mesh, PartitionSpec as P

HEAD = 512
SLOTS = 64
SCALE = HEAD ** (-0.5)
EPSILON = 1e-06
HIGHEST = lax.Precision.HIGHEST
BF = jnp.bfloat16
F32 = jnp.float32


def mm(a, b):
    return lax.dot_general(a, b, (((1,), (0,)), ((), ())), preferred_element_type=F32)


def mm_nt(a, b):
    return lax.dot_general(a, b, (((1,), (1,)), ((), ())), preferred_element_type=F32)


def mm_tn(a, b):
    return lax.dot_general(a, b, (((0,), (0,)), ((), ())), preferred_element_type=F32)


def exact(a, b):
    return lax.dot_general(
        a, b, (((1,), (0,)), ((), ())), precision=HIGHEST, preferred_element_type=F32
    )


def row_bit(rows, level):
    t = lax.broadcasted_iota(jnp.int32, (rows, SLOTS), 0)
    return ((t >> level) & 1) == 1


def prefix_levels(log_decay):
    rows = log_decay.shape[0]
    levels = rows.bit_length() - 1
    f, g = log_decay, jnp.zeros_like(log_decay)
    out = []
    for level in range(levels):
        out.append((f, g))
        total = f + g
        step = 1 << level
        bit = row_bit(rows, level)
        f = f + jnp.where(bit, pltpu.roll(total, step, 0), 0.0)
        g = g + jnp.where(bit, 0.0, pltpu.roll(total, rows - step, 0))
    return out, f, g


def same_block(rows, level):
    t = lax.broadcasted_iota(jnp.int32, (rows, rows), 0)
    s = lax.broadcasted_iota(jnp.int32, (rows, rows), 1)
    return (t >> (level + 1)) == (s >> (level + 1))


def level_mask(table, level, levels):
    if level == levels - 1:
        return table
    return jnp.where(same_block(table.shape[0], level), table, jnp.zeros_like(table))


def factors(pair, level, inflow):
    f, g = pair
    bit = row_bit(f.shape[0], level)
    left = jnp.where(bit, jnp.exp(f), 0.0)
    right = jnp.where(bit, 0.0, jnp.exp(g))
    return left, right, right * inflow


def diagonal(rows):
    t = lax.broadcasted_iota(jnp.int32, (rows, rows), 0)
    s = lax.broadcasted_iota(jnp.int32, (rows, rows), 1)
    return t == s


def slot_table(weights, pairs, inflow):
    rows = weights.shape[0]
    levels = len(pairs)
    table = jnp.where(diagonal(rows), jnp.sum(weights * inflow, axis=1, keepdims=True), 0.0)
    for level in range(levels):
        left, _, gain = factors(pairs[level], level, inflow)
        block = mm_nt((weights * left).astype(BF), gain.astype(BF))
        table = table + level_mask(block, level, levels)
    return table


def slot_sums(table, pairs, inflow):
    rows = table.shape[0]
    levels = len(pairs)
    own = jnp.sum(jnp.where(diagonal(rows), table, 0.0), axis=1, keepdims=True)
    low = table.astype(BF)
    total = own * inflow
    for level in range(levels):
        left, _, gain = factors(pairs[level], level, inflow)
        total = total + left * mm(level_mask(low, level, levels), gain.astype(BF))
    return total


def states_kernel(kv_ref, li_ref, state_ref, decay_ref):
    kv = kv_ref[0]
    log_decay = li_ref[0, :, :SLOTS]
    inflow = li_ref[0, :, SLOTS:]
    rows = kv.shape[0]
    t = lax.broadcasted_iota(jnp.int32, (rows, rows), 0)
    s = lax.broadcasted_iota(jnp.int32, (rows, rows), 1)
    after = exact((s > t).astype(F32), log_decay)
    weight = jnp.exp(after) * inflow
    state_ref[0] = mm_tn(weight.astype(BF), kv)
    total = lax.dot_general(
        log_decay, jnp.ones((rows, 128), F32), (((0,), (0,)), ((), ())),
        precision=HIGHEST, preferred_element_type=F32,
    )
    decay_ref[0] = jnp.exp(total)


def forward_kernel(qs_ref, kv_ref, li_ref, init_ref, gain_ref, gated_ref, out_ref, prob_ref, mix_ref):
    queries = qs_ref[0, :, :HEAD].astype(BF)
    swish = qs_ref[0, :, HEAD:]
    keys = kv_ref[0, :, :HEAD]
    values = kv_ref[0, :, HEAD:]
    log_decay = li_ref[0, :, :SLOTS]
    inflow = li_ref[0, :, SLOTS:]
    init = init_ref[0].astype(BF)
    pairs, running, _ = prefix_levels(log_decay)
    growth = jnp.exp(running)
    scores = mm_nt(queries, keys) * SCALE
    slots = slot_sums(scores, pairs, inflow) + mm_nt(queries, init[:, :HEAD]) * SCALE * growth
    top = jnp.max(slots, axis=1, keepdims=True)
    weights = jnp.exp(slots - top)
    probs = weights / jnp.sum(weights, axis=1, keepdims=True)
    mix = slot_table(probs, pairs, inflow).astype(BF)
    out = mm(mix, values) + mm((probs * growth).astype(BF), init[:, HEAD:])
    hat = out * lax.rsqrt(jnp.mean(out * out, axis=1, keepdims=True) + EPSILON)
    gated_ref[0] = (hat * gain_ref[0:1] * (swish * jax.nn.sigmoid(swish))).astype(BF)
    out_ref[0] = out
    prob_ref[0] = probs
    mix_ref[0] = mix


def backward_kernel(
    qs_ref, kv_ref, li_ref, init_ref, gain_ref, out_ref, prob_ref, mix_ref, gg_ref,
    dqs_ref, dkv_ref, ddi_ref, adj_ref, sg_ref,
):
    queries = qs_ref[0, :, :HEAD].astype(BF)
    swish = qs_ref[0, :, HEAD:]
    keys = kv_ref[0, :, :HEAD]
    values = kv_ref[0, :, HEAD:]
    log_decay = li_ref[0, :, :SLOTS]
    inflow = li_ref[0, :, SLOTS:]
    init = init_ref[0].astype(BF)
    out = out_ref[0]
    probs = prob_ref[0]
    gain = gain_ref[0:1]
    rows = out.shape[0]
    scale_out = lax.rsqrt(jnp.mean(out * out, axis=1, keepdims=True) + EPSILON)
    hat = out * scale_out
    sig = jax.nn.sigmoid(swish)
    silu = swish * sig
    gg = gg_ref[0].astype(F32)
    gg_hat = gg * hat
    dqs_ref[0, :, HEAD:] = (gg_hat * gain * (sig * (1.0 + swish * (1.0 - sig)))).astype(BF)
    part = jnp.broadcast_to(jnp.sum(gg_hat * silu, axis=0, keepdims=True), (8, HEAD))

    @pl.when(pl.program_id(0) == 0)
    def _():
        sg_ref[...] = part

    @pl.when(pl.program_id(0) > 0)
    def _():
        sg_ref[...] = sg_ref[...] + part

    grad_hat = gg * gain * silu
    dout = scale_out * (grad_hat - hat * jnp.mean(grad_hat * hat, axis=1, keepdims=True))
    dout = dout.astype(BF)
    pairs, running, _ = prefix_levels(log_decay)
    levels = len(pairs)
    growth = jnp.exp(running)
    scores = mm_nt(queries, keys) * SCALE
    grads = mm_nt(dout, values)
    key_part = mm_nt(queries, init[:, :HEAD]) * SCALE * growth
    value_part = mm_nt(dout, init[:, HEAD:]) * growth
    dprob = slot_sums(grads, pairs, inflow) + value_part
    dslot = probs * (dprob - jnp.sum(probs * dprob, axis=1, keepdims=True))
    back = slot_table(dslot, pairs, inflow).astype(BF)
    dslot_g = (dslot * growth).astype(BF)
    prob_g = (probs * growth).astype(BF)
    dqs_ref[0, :, :HEAD] = (SCALE * (mm(back, keys) + mm(dslot_g, init[:, :HEAD]))).astype(BF)
    dkv_ref[0, :, :HEAD] = SCALE * mm_tn(back, queries)
    dkv_ref[0, :, HEAD:] = mm_tn(mix_ref[0], dout)
    adj_ref[0, :, :HEAD] = SCALE * mm_tn(dslot_g, queries)
    adj_ref[0, :, HEAD:] = mm_tn(prob_g, dout)
    diag = diagonal(rows)
    own_a = jnp.sum(jnp.where(diag, scores, 0.0), axis=1, keepdims=True)
    own_b = jnp.sum(jnp.where(diag, grads, 0.0), axis=1, keepdims=True)
    dinflow = dslot * own_a + probs * own_b
    scores_low = scores.astype(BF)
    grads_low = grads.astype(BF)
    fbar = dslot * key_part + probs * value_part
    gbar = jnp.zeros_like(fbar)
    for level in range(levels - 1, -1, -1):
        left, right, amount = factors(pairs[level], level, inflow)
        table_a = level_mask(scores_low, level, levels)
        table_b = level_mask(grads_low, level, levels)
        amount_low = amount.astype(BF)
        dleft = dslot * left
        pleft = probs * left
        grow = dleft * mm(table_a, amount_low) + pleft * mm(table_b, amount_low)
        back_in = mm_tn(table_a, dleft.astype(BF)) + mm_tn(table_b, pleft.astype(BF))
        dinflow = dinflow + right * back_in
        step = 1 << level
        bit = row_bit(rows, level)
        total = pltpu.roll(jnp.where(bit, fbar, 0.0), rows - step, 0) + pltpu.roll(
            jnp.where(bit, 0.0, gbar), step, 0
        )
        fbar = fbar + grow + total
        gbar = gbar + amount * back_in + total
    ddi_ref[0, :, :SLOTS] = fbar
    ddi_ref[0, :, SLOTS:] = dinflow


def finish_kernel(kv_ref, li_ref, init_ref, end_ref, dkv_ref, ddi_ref, okv_ref, oddi_ref):
    kv = kv_ref[0]
    log_decay = li_ref[0, :, :SLOTS]
    inflow = li_ref[0, :, SLOTS:]
    end = end_ref[0]
    rows = kv.shape[0]
    t = lax.broadcasted_iota(jnp.int32, (rows, rows), 0)
    s = lax.broadcasted_iota(jnp.int32, (rows, rows), 1)
    earlier = (s < t).astype(F32)
    after = exact((s > t).astype(F32), log_decay)
    fade = jnp.exp(after)
    weight = fade * inflow
    end_low = end.astype(BF)
    okv_ref[0] = (dkv_ref[0] + mm(weight.astype(BF), end_low)).astype(BF)
    reach = mm_nt(kv, end_low)
    whole = jnp.exp(jnp.sum(log_decay, axis=0, keepdims=True))
    carry = lax.dot_general(
        jnp.ones((8, 2 * HEAD), F32), end * init_ref[0], (((1,), (1,)), ((), ())),
        precision=HIGHEST, preferred_element_type=F32,
    )[0:1]
    oddi_ref[0, :, :SLOTS] = (
        ddi_ref[0, :, :SLOTS] + exact(earlier, weight * reach) + whole * carry
    )
    oddi_ref[0, :, SLOTS:] = ddi_ref[0, :, SLOTS:] + fade * reach


def blocked(shape):
    return pl.BlockSpec((1,) + shape, lambda i: (i, 0, 0))


def run(kernel, args, specs, outs, out_specs, flops, moved):
    return pl.pallas_call(
        kernel,
        grid=(args[0].shape[0],),
        in_specs=specs,
        out_specs=out_specs,
        out_shape=outs,
        cost_estimate=pl.CostEstimate(flops=flops, bytes_accessed=moved, transcendentals=0),
        compiler_params=pltpu.CompilerParams(vmem_limit_bytes=56 << 20),
    )(*args)


def sds(shape, dtype=F32):
    return jax.ShapeDtypeStruct(shape, dtype)


def chunk_states(kv, li):
    n, rows, _ = kv.shape
    return run(
        states_kernel, (kv, li),
        [blocked((rows, 2 * HEAD)), blocked((rows, 2 * SLOTS))],
        (sds((n, SLOTS, 2 * HEAD)), sds((n, SLOTS, 128))),
        (blocked((SLOTS, 2 * HEAD)), blocked((SLOTS, 128))),
        n * 10**9, n * 10**6,
    )


def mixer_forward(qs, kv, li, init, gain):
    n, rows, _ = kv.shape
    return run(
        forward_kernel, (qs, kv, li, init, gain),
        [blocked((rows, 2 * HEAD)), blocked((rows, 2 * HEAD)), blocked((rows, 2 * SLOTS)),
         blocked((SLOTS, 2 * HEAD)), pl.BlockSpec((8, HEAD), lambda i: (0, 0))],
        (sds((n, rows, HEAD), BF), sds((n, rows, HEAD)), sds((n, rows, SLOTS)), sds((n, rows, rows), BF)),
        (blocked((rows, HEAD)), blocked((rows, HEAD)), blocked((rows, SLOTS)), blocked((rows, rows))),
        n * 3 * 10**9, n * 4 * 10**6,
    )


def mixer_backward(qs, kv, li, init, gain, out, probs, mix, gg):
    n, rows, _ = kv.shape
    return run(
        backward_kernel, (qs, kv, li, init, gain, out, probs, mix, gg),
        [blocked((rows, 2 * HEAD)), blocked((rows, 2 * HEAD)), blocked((rows, 2 * SLOTS)),
         blocked((SLOTS, 2 * HEAD)), pl.BlockSpec((8, HEAD), lambda i: (0, 0)),
         blocked((rows, HEAD)), blocked((rows, SLOTS)), blocked((rows, rows)), blocked((rows, HEAD))],
        (sds((n, rows, 2 * HEAD), BF), sds((n, rows, 2 * HEAD)), sds((n, rows, 2 * SLOTS)),
         sds((n, SLOTS, 2 * HEAD)), sds((8, HEAD))),
        (blocked((rows, 2 * HEAD)), blocked((rows, 2 * HEAD)), blocked((rows, 2 * SLOTS)),
         blocked((SLOTS, 2 * HEAD)), pl.BlockSpec((8, HEAD), lambda i: (0, 0))),
        n * 6 * 10**9, n * 5 * 10**6,
    )


def mixer_finish(kv, li, init, end, dkv, ddi):
    n, rows, _ = kv.shape
    return run(
        finish_kernel, (kv, li, init, end, dkv, ddi),
        [blocked((rows, 2 * HEAD)), blocked((rows, 2 * SLOTS)), blocked((SLOTS, 2 * HEAD)),
         blocked((SLOTS, 2 * HEAD)), blocked((rows, 2 * HEAD)), blocked((rows, 2 * SLOTS))],
        (sds((n, rows, 2 * HEAD), BF), sds((n, rows, 2 * SLOTS))),
        (blocked((rows, 2 * HEAD)), blocked((rows, 2 * SLOTS))),
        n * 10**9, n * 3 * 10**6,
    )


D = 2048
HEADS = 4
RANK = 16
NORMALIZER = 8.0


def inverse_rms(values):
    return lax.rsqrt(jnp.mean(values * values, axis=-1, keepdims=True) + EPSILON)


def silu_slope(values):
    sigmoid_val = jax.nn.sigmoid(values)
    return sigmoid_val * (1.0 + values * (1.0 - sigmoid_val))


def norm_back(grad_hat, hat_rows, scale_rows):
    return scale_rows * (
        grad_hat - hat_rows * jnp.mean(grad_hat * hat_rows, axis=-1, keepdims=True)
    )


def swap(value, axis, step):
    count = lax.axis_size(axis)
    return lax.ppermute(value, axis, [(i, i ^ step) for i in range(count)])


def gather_heads(block):
    return [block] + [swap(block, "p", k) for k in range(1, HEADS)]


def scatter_heads(parts, *fillers):
    got = [swap(parts[k], "p", k) for k in range(1, HEADS)]
    if fillers:
        held = lax.optimization_barrier(tuple(got) + fillers)
        got, fillers = held[: HEADS - 1], held[HEADS - 1 :]
    total = parts[0].astype(F32)
    for part in got:
        total = total + part.astype(F32)
    return (total,) + tuple(fillers) if fillers else total


def after(value, *others):
    return lax.optimization_barrier((value,) + others)[0]


def place_kernel(blocks, spot_ref, *refs):
    ins, out = refs[:-1], refs[-1]
    part = ins[0].shape[1]
    for i, ref in enumerate(ins):
        for k in range(blocks):
            start = pl.multiple_of(spot_ref[i * blocks + k] * part, part)
            out[pl.ds(start, part), :] = ref[k]


def place(parts, spots):
    blocks, part, width = parts[0].shape
    chunk = 256
    table = jnp.stack([jnp.asarray(x, jnp.int32) for row in spots for x in row])
    rows = len(parts) * blocks * part
    return pl.pallas_call(
        functools.partial(place_kernel, blocks),
        grid_spec=pltpu.PrefetchScalarGridSpec(
            num_scalar_prefetch=1,
            grid=(width // chunk,),
            in_specs=[pl.BlockSpec((blocks, part, chunk), lambda i, s: (0, 0, i))] * len(parts),
            out_specs=pl.BlockSpec((rows, chunk), lambda i, s: (0, i)),
        ),
        out_shape=jax.ShapeDtypeStruct((rows, width), BF),
        cost_estimate=pl.CostEstimate(flops=0, bytes_accessed=4 * rows * width, transcendentals=0),
        compiler_params=pltpu.CompilerParams(vmem_limit_bytes=56 << 20),
    )(table, *parts)


def column_cuts(shards, here, k):
    cuts = []
    for shard in shards:
        width = shard.shape[1] // HEADS
        cuts.append(lax.dynamic_slice_in_dim(shard, (here ^ k) * width, width, 1))
    return jnp.concatenate(cuts, axis=1)


def head_columns(shards, here):
    copies = lax.axis_size("r")
    turn = lax.axis_index("r")
    own = column_cuts(shards, here, 0)
    pieces = [own] + [swap(column_cuts(shards, here, k), "p", k) for k in range(1, HEADS)]
    parts, spots = [], []
    for k in range(HEADS):
        for m in range(copies):
            piece = pieces[k] if m == 0 else swap(pieces[k], "r", m)
            parts.append(piece[None])
            spots.append([(here ^ k) * copies + (turn ^ m)])
    return place(parts, spots), pieces[1:]


def seq_pieces(shards, here):
    rows = shards[0].shape[0] // 2
    start = lax.axis_index("seq") % 2 * rows
    shards = [lax.dynamic_slice_in_dim(shard, start, rows, 0) for shard in shards]
    own = column_cuts(shards, here, 0)
    return [own] + [swap(column_cuts(shards, here, k), "p", k) for k in range(1, HEADS)]


def seq_columns(pieces, here):
    copies, turn, half = lax.axis_size("r"), lax.axis_index("r"), lax.axis_index("seq") % 2
    parts, spots = [], []
    for j, part in enumerate([pieces, swap(pieces, "seq", 1)]):
        for m in range(copies):
            parts.append(part if m == 0 else swap(part, "r", m))
            spots.append(
                [((here ^ k) * copies + (turn ^ m)) * 2 + (half ^ j) for k in range(HEADS)]
            )
    return place(parts, spots)


def gather_small(packed, here, turn):
    copies = lax.axis_size("r")
    near = jnp.concatenate([packed] + [swap(packed, "r", m) for m in range(1, copies)])
    both = jnp.concatenate(gather_heads(near))
    heads = jnp.arange(HEADS, dtype=jnp.int32) ^ here
    turns = jnp.arange(copies, dtype=jnp.int32) ^ turn
    order = (heads[:, None] * copies + turns[None, :]).reshape(-1)
    return jnp.take(both, order, axis=0)


def sum_small(value, here, turn):
    mine = [lax.dynamic_index_in_dim(value, here ^ k, 0, False) for k in range(HEADS)]
    total = scatter_heads(mine)
    copies = lax.axis_size("r")
    kept = lax.dynamic_index_in_dim(total, turn, 0, True)
    for m in range(1, copies):
        kept = kept + swap(lax.dynamic_index_in_dim(total, turn ^ m, 0, True), "r", m)
    return kept[0]


def chain(state, decay, forward):
    count = lax.axis_size("seq")
    total = jnp.zeros_like(state)
    for hop in range(count - 1):
        pair = (hop, hop + 1) if forward else (count - 1 - hop, count - 2 - hop)
        sent = (decay * total + state).astype(BF)
        total = total + lax.ppermute(sent, "seq", [pair]).astype(F32)
    return total


def chain_pair(both, decay, forward):
    return jnp.concatenate(
        [chain(both[..., :HEAD], decay, forward), chain(both[..., HEAD:], decay, forward)], axis=-1
    )


def split_rows(left, turn, step, groups):
    copies, width = left.shape[2:]
    flat = left.reshape(left.shape[0], -1)
    cuts = [
        lax.dynamic_slice_in_dim(flat, (g * copies + (turn ^ step)) * width, width, 1)
        for g in groups
    ]
    return jnp.concatenate(cuts, axis=1)


def sum_copies(own, away):
    got = [swap(part, "r", m + 1) for m, part in enumerate(away)]
    total = own()
    for part in got:
        total = total + part.astype(F32)
    return total.astype(BF)


def assemble_kernel(counts, spot_ref, *refs):
    n_in, n_out, part = counts
    ins, outs = refs[:n_in], refs[n_in:]
    width = outs[0].shape[1]
    for j in range(n_in):
        for o in range(n_out):
            cut = ins[j][0, :, o * width : (o + 1) * width]
            outs[o][j * part : (j + 1) * part, :] = cut.astype(F32)


def assemble(parts, columns, n_out):
    spans, blocks, part, width = parts.shape
    width //= n_out
    rows = part * spans
    spots = jnp.stack([jnp.asarray(c, jnp.int32) for c in columns])
    return pl.pallas_call(
        functools.partial(assemble_kernel, (spans, n_out, part)),
        grid_spec=pltpu.PrefetchScalarGridSpec(
            num_scalar_prefetch=1,
            grid=(blocks,),
            in_specs=[
                pl.BlockSpec((None, 1, part, n_out * width), lambda i, s, j=j: (j, i, 0, 0))
                for j in range(spans)
            ],
            out_specs=[pl.BlockSpec((rows, width), lambda i, s: (0, s[i]))] * n_out,
        ),
        out_shape=[jax.ShapeDtypeStruct((rows, blocks * width), F32)] * n_out,
        cost_estimate=pl.CostEstimate(
            flops=0, bytes_accessed=6 * n_out * rows * blocks * width, transcendentals=0
        ),
        compiler_params=pltpu.CompilerParams(vmem_limit_bytes=56 << 20),
    )(spots, *([parts] * spans))


def line_pairs(i):
    count = lax.axis_size("seq")
    return [(i, i + 1), (count - 1 - i, count - 2 - i)]


def inward(value, last):
    for i in range(lax.axis_size("seq") // 2 - 1):
        if i in last:
            value = after(value, last[i])
        last[i] = lax.ppermute(value, "seq", line_pairs(i))
        value = value + last[i]
    return value


def across(value, last):
    half = lax.axis_size("seq") // 2
    if "across" in last:
        value = after(value, last["across"])
    last["across"] = lax.ppermute(value, "seq", [(half - 1, half), (half, half - 1)])
    return value + last["across"]


def outward(value, last):
    count, spot = lax.axis_size("seq"), lax.axis_index("seq")
    for i in range(count // 2 - 2, -1, -1):
        if ("out", i) in last:
            value = after(value, last["out", i])
        got = lax.ppermute(value, "seq", [(b, a) for a, b in line_pairs(i)])
        last["out", i] = got
        value = jnp.where((spot == i) | (spot == count - 1 - i), got, value)
    return value


def spread_line(near, far, here):
    got = [far[0], swap(near[0], "p", 1), swap(far[1], "p", 2), swap(near[1], "p", 3)]
    return assemble(jnp.stack(got)[None], [here ^ k for k in range(HEADS)], 2)


def swap_diagonal(part):
    count = lax.axis_size("seq")
    sends = [(p * count + z, (p ^ z) * count + z) for p in range(HEADS) for z in range(count)]
    return lax.ppermute(part, ("p", "seq"), sends)


def body(
    tokens,
    seq_lengths,
    attn_gain,
    query_proj,
    key_proj,
    value_proj,
    decay_down,
    decay_up,
    decay_bias,
    swish_proj,
    slot_gain,
    out_proj,
    mlp_gain,
    mlp_gate,
    mlp_up,
    mlp_down,
    grad_out,
):
    rows = tokens.shape[0]
    copies = lax.axis_size("r")
    owners = HEADS * copies
    shard = D // owners
    here, turn, place = lax.axis_index("p"), lax.axis_index("r"), lax.axis_index("seq")
    group = HEADS * rows

    small = [attn_gain, decay_down, decay_up, decay_bias, slot_gain, mlp_gain, seq_lengths]
    packed = jnp.concatenate([a.astype(F32).reshape(-1) for a in small])
    packed = gather_small(packed[None], here, turn)
    fields, offset = [], 0
    for a in small:
        fields.append(packed[:, offset : offset + a.size])
        offset += a.size
    gain_one = fields[0].reshape(D)
    down_full = fields[1].reshape(D, RANK).astype(BF)
    up_full = fields[2].reshape(owners, RANK, -1).transpose(1, 0, 2).reshape(RANK, HEADS * SLOTS)
    up_head = lax.dynamic_slice_in_dim(up_full, here * SLOTS, SLOTS, 1)
    bias_head = lax.dynamic_slice_in_dim(fields[3].reshape(HEADS * SLOTS), here * SLOTS, SLOTS, 0)
    gain_head = lax.dynamic_slice_in_dim(fields[4].reshape(D), here * HEAD, HEAD, 0)
    gain_head8 = jnp.broadcast_to(gain_head[None], (8, HEAD))
    gain_two = fields[5].reshape(D)
    lengths = fields[6].reshape(HEADS, copies)
    positions = (place * rows + jnp.arange(rows, dtype=jnp.int32)).astype(F32)
    masks = [
        (positions < lax.dynamic_index_in_dim(lengths, here ^ k, 0, False)[turn]).astype(F32)
        for k in range(HEADS)
    ]
    mask_all = jnp.concatenate(masks)[:, None]
    mask_own = masks[0][:, None]

    token_blocks = gather_heads(tokens)
    weight_kv, kv_pieces = head_columns([key_proj, value_proj], here)
    late = lax.optimization_barrier((query_proj, swish_proj, mlp_gate, mlp_up) + tuple(kv_pieces))
    weight_qs, qs_pieces = head_columns(late[:2], here)
    gu_pieces = seq_pieces(late[2:4], here)
    grad_all = lax.all_gather(after(grad_out, *qs_pieces), "p", axis=0, tiled=False)
    weight_out = lax.all_gather(out_proj, "r", axis=0, tiled=True)
    weight_down = lax.all_gather(mlp_down, "r", axis=0, tiled=True)

    tokens_all = jnp.concatenate(token_blocks).astype(F32)
    normed = (tokens_all * inverse_rms(tokens_all) * gain_one).astype(BF)
    kv = mm(normed, weight_kv).astype(BF).reshape(HEADS, rows, 2 * HEAD)
    gate_low = mm(normed, down_full)
    forget = exact(gate_low, up_head) + bias_head
    log_sig = jax.nn.log_sigmoid(forget) / NORMALIZER
    li = jnp.concatenate([mask_all * log_sig, mask_all * -jnp.expm1(log_sig)], axis=1)
    li = li.reshape(HEADS, rows, 2 * SLOTS)
    state, decay = chunk_states(kv, li)
    decay = decay[:, :, :1]
    init = chain_pair(state, decay, True)
    *gu_pieces, _ = lax.optimization_barrier((*gu_pieces, init))
    weight_gu = seq_columns(jnp.stack(gu_pieces), here)
    qs = mm(normed, weight_qs).reshape(HEADS, rows, 2 * HEAD)
    gated, mixer_out, probs, mix = mixer_forward(qs, kv, li, init, gain_head8)
    gated = gated.reshape(group, HEAD)
    attn_part = mm(gated, weight_out).astype(BF).reshape(HEADS, rows, D)
    grad_blocks = [
        lax.dynamic_index_in_dim(grad_all, here ^ k, 0, False) for k in range(HEADS)
    ]
    grad_mlp = (mask_all * jnp.concatenate(grad_blocks).astype(F32)).astype(BF)
    attn_out, grad_act = scatter_heads(
        [attn_part[k] for k in range(HEADS)], mm_nt(grad_mlp, weight_down)
    )

    tokens_f = tokens.astype(F32)
    residual = tokens_f + mask_own * attn_out
    scale_two = inverse_rms(residual)
    hat_two = residual * scale_two
    normed_two_own = (hat_two * gain_two).astype(BF)
    weight_gu, *two_blocks = lax.optimization_barrier((weight_gu, *gather_heads(normed_two_own)))
    normed_two = jnp.concatenate(two_blocks)

    hidden_width = weight_down.shape[0]
    gate_up = mm(normed_two, weight_gu)
    gate_pre, up_pre = gate_up[:, :hidden_width], gate_up[:, hidden_width:]
    hidden = (jax.nn.silu(gate_pre) * up_pre).astype(BF)
    grad_gate = (grad_act * up_pre * silu_slope(gate_pre)).astype(BF)
    grad_up = (grad_act * jax.nn.silu(gate_pre)).astype(BF)
    grad_gu = jnp.concatenate([grad_gate, grad_up], axis=1)
    order = [here ^ k for k in range(HEADS)]
    hops = range(1, copies)
    down_rows = mlp_down.shape[0]
    two_view = normed_two.reshape(group, HEADS, copies, shard)
    gu_away = [mm_tn(split_rows(two_view, turn, m, order), grad_gu).astype(BF) for m in hops]
    two_part = mm_nt(after(grad_gu, *gu_away), weight_gu).astype(BF)
    gu_total = sum_copies(
        lambda: mm_tn(split_rows(two_view, turn, 0, order), after(grad_gu, two_part)), gu_away
    )
    gu_part = lax.psum_scatter(
        gu_total.reshape(HEADS, shard, 2 * hidden_width), "seq", scatter_dimension=0, tiled=True
    )
    hidden_late = after(hidden, gu_total)

    def down_grad_part(m):
        cut = lax.dynamic_slice_in_dim(hidden_late, (turn ^ m) * down_rows, down_rows, 1)
        return mm_tn(cut, grad_mlp)

    down_total = sum_copies(
        lambda: down_grad_part(0), [down_grad_part(m).astype(BF) for m in hops]
    )
    two_part = two_part.reshape(HEADS, rows, D)
    grad_norm_two, down_total = scatter_heads([two_part[k] for k in range(HEADS)], down_total)
    gain_two_grad = jnp.sum(grad_norm_two * hat_two, axis=0)
    grad_rows = grad_out.astype(F32)
    grad_resid = grad_rows + norm_back(grad_norm_two * gain_two, hat_two, scale_two)
    grad_attn_own = (mask_own * grad_resid).astype(BF)
    attn_blocks = gather_heads(grad_attn_own)
    mlp_part = mm(hidden, weight_down).astype(BF)
    mlp_part, gu_part, *attn_blocks = lax.optimization_barrier((mlp_part, gu_part, *attn_blocks))
    gu_part = swap_diagonal(gu_part)
    half_rows, line = down_rows // 2, {}
    down_near = inward(after(down_total[:half_rows], *attn_blocks), line)
    grad_attn = jnp.concatenate(attn_blocks)
    mlp_part = mlp_part.reshape(HEADS, rows, D)
    mlp_out = scatter_heads([mlp_part[k] for k in range(HEADS)])

    grad_gated = mm_nt(grad_attn, weight_out).reshape(HEADS, rows, HEAD)
    grad_qs, grad_kv, grad_li, adjoint, slot_part = mixer_backward(
        qs, kv, li, init, gain_head8, mixer_out, probs, mix, grad_gated
    )
    adjoint, gu_part, down_near = lax.optimization_barrier((adjoint, gu_part, down_near))
    gu_whole = lax.all_gather(gu_part, "seq", axis=0, tiled=True)
    one_view = normed.reshape(group, HEADS, copies, shard)
    one_views = [split_rows(one_view, turn, m, order) for m in range(copies)]
    out_view = gated.reshape(group, 1, copies, shard)
    out_views = [split_rows(out_view, turn, m, [0]) for m in range(copies)]

    def weight_grad(views, right):
        return sum_copies(
            lambda: mm_tn(views[0], right), [mm_tn(views[m], right).astype(BF) for m in hops]
        )

    grad_qs = grad_qs.reshape(group, 2 * HEAD)
    out_total = weight_grad(out_views, grad_attn)
    qs_total = weight_grad(one_views, grad_qs)
    ends = chain_pair(adjoint, decay, False)
    ends, mlp_out, out_total, qs_total, down_near, gu_whole = lax.optimization_barrier(
        (ends, mlp_out, out_total, qs_total, down_near, gu_whole)
    )
    result = (residual + mask_own * mlp_out).astype(BF)
    down_near = across(down_near, line)
    grad_qs = after(grad_qs, down_near)
    grad_kv, grad_li = mixer_finish(kv, li, init, ends, grad_kv, grad_li)
    grad_kv = grad_kv.reshape(group, 2 * HEAD)
    grad_li = grad_li.reshape(group, 2 * SLOTS)
    grad_decay = (
        mask_all
        * (grad_li[:, :SLOTS] - grad_li[:, SLOTS:] * jnp.exp(log_sig))
        / NORMALIZER
        * jax.nn.sigmoid(-forget)
    )
    bias_part = jnp.sum(grad_decay, axis=0)
    up_part = lax.dot_general(
        gate_low, grad_decay, (((0,), (0,)), ((), ())), precision=HIGHEST, preferred_element_type=F32
    )
    grad_low = lax.dot_general(
        grad_decay, up_head, (((1,), (1,)), ((), ())), precision=HIGHEST, preferred_element_type=F32
    ).astype(BF)
    down_low_part = mm_tn(normed, grad_low)

    one_part = (
        (mm_nt(grad_qs, weight_qs) + mm_nt(grad_kv, weight_kv) + mm_nt(grad_low, down_full))
        .astype(BF)
        .reshape(HEADS, rows, D)
    )
    kv_total = weight_grad(one_views, grad_kv)
    grad_norm_one, kv_total = scatter_heads([one_part[k] for k in range(HEADS)], kv_total)

    scale_one = inverse_rms(tokens_f)
    hat_one = tokens_f * scale_one
    gain_one_grad = jnp.sum(grad_norm_one * hat_one, axis=0)
    grad_tokens = (grad_resid + norm_back(grad_norm_one * gain_one, hat_one, scale_one)).astype(BF)

    def placed(part, width):
        whole = jnp.zeros(part.shape[:-1] + (HEADS * width,), F32)
        return lax.dynamic_update_slice_in_dim(whole, part, here * width, part.ndim - 1)

    up_sum = placed(up_part, SLOTS).reshape(RANK, HEADS, copies, -1).transpose(1, 2, 0, 3)
    sums = [
        gain_one_grad,
        down_low_part,
        up_sum,
        placed(bias_part, SLOTS),
        placed(slot_part[0], HEAD),
        gain_two_grad,
    ]
    flat = jnp.concatenate([a.reshape(HEADS, copies, -1) for a in sums], axis=2)
    flat = sum_small(flat, here, turn)
    lanes = D * 8
    flat = jnp.pad(flat, (0, -flat.size % lanes)).astype(BF).reshape(-1, D)

    qs_total = qs_total.reshape(HEADS, shard, 2 * HEAD)
    kv_total = kv_total.reshape(HEADS, shard, 2 * HEAD)
    chunks = [down_total[half_rows:], qs_total[1::2], qs_total[0::2], out_total]
    chunks += [kv_total[1::2], kv_total[0::2], flat]
    summed = [outward(down_near, line)]
    for chunk in chunks:
        summed.append(outward(across(inward(chunk, line), line), line))
    near, far, *wide, out_grad, kv_near, kv_far, flat = summed
    down_grad = jnp.concatenate([near, far])
    gate_grad, up_grad = assemble(gu_whole[None], order, 2)
    query_grad, swish_grad = spread_line(wide[0], wide[1], here)
    key_grad, value_grad = spread_line(kv_near, kv_far, here)
    out_grad = out_grad.astype(F32)
    flat = flat.reshape(-1).astype(F32)
    totals, offset = [], 0
    for a in sums:
        size = a.size // owners
        totals.append(flat[offset : offset + size])
        offset += size

    return (
        result,
        grad_tokens,
        totals[0],
        query_grad,
        key_grad,
        value_grad,
        totals[1].reshape(shard, RANK),
        totals[2].reshape(RANK, -1),
        totals[3],
        swish_grad,
        totals[4],
        out_grad,
        totals[5],
        gate_grad,
        up_grad,
        down_grad.astype(F32),
    )


def solution(mesh):
    count, span = mesh.devices.shape
    split = Mesh(mesh.devices.reshape(HEADS, count // HEADS, span), ("p", "r", "seq"))
    rows = P(("p", "r", "seq"), None)
    matrix, vector, last = P(("p", "r"), None), P(("p", "r")), P(None, ("p", "r"))
    in_specs = (
        rows, vector, vector, matrix, matrix, matrix, matrix, last, vector, matrix, vector, matrix,
        vector, matrix, matrix, matrix, rows,
    )
    out_specs = (
        rows, rows, vector, matrix, matrix, matrix, matrix, last, vector, matrix, vector, matrix,
        vector, matrix, matrix, matrix,
    )
    return jax.shard_map(body, mesh=split, in_specs=in_specs, out_specs=out_specs, check_vma=False)
```

```python
import functools
import jax
import jax.numpy as jnp
from jax import lax
from jax.experimental import pallas as pl
from jax.experimental.pallas import tpu as pltpu
from jax.sharding import Mesh, PartitionSpec as P

HEAD = 512
SLOTS = 64
SCALE = HEAD ** (-0.5)
EPSILON = 1e-06
HIGHEST = lax.Precision.HIGHEST
BF = jnp.bfloat16
F32 = jnp.float32


def mm(a, b):
    return lax.dot_general(a, b, (((1,), (0,)), ((), ())), preferred_element_type=F32)


def mm_nt(a, b):
    return lax.dot_general(a, b, (((1,), (1,)), ((), ())), preferred_element_type=F32)


def mm_tn(a, b):
    return lax.dot_general(a, b, (((0,), (0,)), ((), ())), preferred_element_type=F32)


def exact(a, b):
    return lax.dot_general(
        a, b, (((1,), (0,)), ((), ())), precision=HIGHEST, preferred_element_type=F32
    )


def row_bit(rows, level):
    t = lax.broadcasted_iota(jnp.int32, (rows, SLOTS), 0)
    return ((t >> level) & 1) == 1


def prefix_levels(log_decay):
    rows = log_decay.shape[0]
    levels = rows.bit_length() - 1
    f, g = log_decay, jnp.zeros_like(log_decay)
    out = []
    for level in range(levels):
        out.append((f, g))
        total = f + g
        step = 1 << level
        bit = row_bit(rows, level)
        f = f + jnp.where(bit, pltpu.roll(total, step, 0), 0.0)
        g = g + jnp.where(bit, 0.0, pltpu.roll(total, rows - step, 0))
    return out, f, g


def same_block(rows, level):
    t = lax.broadcasted_iota(jnp.int32, (rows, rows), 0)
    s = lax.broadcasted_iota(jnp.int32, (rows, rows), 1)
    return (t >> (level + 1)) == (s >> (level + 1))


def level_mask(table, level, levels):
    if level == levels - 1:
        return table
    return jnp.where(same_block(table.shape[0], level), table, jnp.zeros_like(table))


def factors(pair, level, inflow):
    f, g = pair
    bit = row_bit(f.shape[0], level)
    left = jnp.where(bit, jnp.exp(f), 0.0)
    right = jnp.where(bit, 0.0, jnp.exp(g))
    return left, right, right * inflow


def diagonal(rows):
    t = lax.broadcasted_iota(jnp.int32, (rows, rows), 0)
    s = lax.broadcasted_iota(jnp.int32, (rows, rows), 1)
    return t == s


def slot_table(weights, pairs, inflow):
    rows = weights.shape[0]
    levels = len(pairs)
    table = jnp.where(diagonal(rows), jnp.sum(weights * inflow, axis=1, keepdims=True), 0.0)
    for level in range(levels):
        left, _, gain = factors(pairs[level], level, inflow)
        block = mm_nt((weights * left).astype(BF), gain.astype(BF))
        table = table + level_mask(block, level, levels)
    return table


def slot_sums(table, pairs, inflow):
    rows = table.shape[0]
    levels = len(pairs)
    own = jnp.sum(jnp.where(diagonal(rows), table, 0.0), axis=1, keepdims=True)
    low = table.astype(BF)
    total = own * inflow
    for level in range(levels):
        left, _, gain = factors(pairs[level], level, inflow)
        total = total + left * mm(level_mask(low, level, levels), gain.astype(BF))
    return total


def states_kernel(kv_ref, li_ref, state_ref, decay_ref):
    kv = kv_ref[0]
    log_decay = li_ref[0, :, :SLOTS]
    inflow = li_ref[0, :, SLOTS:]
    rows = kv.shape[0]
    t = lax.broadcasted_iota(jnp.int32, (rows, rows), 0)
    s = lax.broadcasted_iota(jnp.int32, (rows, rows), 1)
    after = exact((s > t).astype(F32), log_decay)
    weight = jnp.exp(after) * inflow
    state_ref[0] = mm_tn(weight.astype(BF), kv)
    total = lax.dot_general(
        log_decay, jnp.ones((rows, 128), F32), (((0,), (0,)), ((), ())),
        precision=HIGHEST, preferred_element_type=F32,
    )
    decay_ref[0] = jnp.exp(total)


def forward_kernel(qs_ref, kv_ref, li_ref, init_ref, gain_ref, gated_ref, out_ref, prob_ref, mix_ref):
    queries = qs_ref[0, :, :HEAD].astype(BF)
    swish = qs_ref[0, :, HEAD:]
    keys = kv_ref[0, :, :HEAD]
    values = kv_ref[0, :, HEAD:]
    log_decay = li_ref[0, :, :SLOTS]
    inflow = li_ref[0, :, SLOTS:]
    init = init_ref[0].astype(BF)
    pairs, running, _ = prefix_levels(log_decay)
    growth = jnp.exp(running)
    scores = mm_nt(queries, keys) * SCALE
    slots = slot_sums(scores, pairs, inflow) + mm_nt(queries, init[:, :HEAD]) * SCALE * growth
    top = jnp.max(slots, axis=1, keepdims=True)
    weights = jnp.exp(slots - top)
    probs = weights / jnp.sum(weights, axis=1, keepdims=True)
    mix = slot_table(probs, pairs, inflow).astype(BF)
    out = mm(mix, values) + mm((probs * growth).astype(BF), init[:, HEAD:])
    hat = out * lax.rsqrt(jnp.mean(out * out, axis=1, keepdims=True) + EPSILON)
    gated_ref[0] = (hat * gain_ref[0:1] * (swish * jax.nn.sigmoid(swish))).astype(BF)
    out_ref[0] = out
    prob_ref[0] = probs
    mix_ref[0] = mix


def backward_kernel(
    qs_ref, kv_ref, li_ref, init_ref, gain_ref, out_ref, prob_ref, mix_ref, gg_ref,
    dqs_ref, dkv_ref, ddi_ref, adj_ref, sg_ref,
):
    queries = qs_ref[0, :, :HEAD].astype(BF)
    swish = qs_ref[0, :, HEAD:]
    keys = kv_ref[0, :, :HEAD]
    values = kv_ref[0, :, HEAD:]
    log_decay = li_ref[0, :, :SLOTS]
    inflow = li_ref[0, :, SLOTS:]
    init = init_ref[0].astype(BF)
    out = out_ref[0]
    probs = prob_ref[0]
    gain = gain_ref[0:1]
    rows = out.shape[0]
    scale_out = lax.rsqrt(jnp.mean(out * out, axis=1, keepdims=True) + EPSILON)
    hat = out * scale_out
    sig = jax.nn.sigmoid(swish)
    silu = swish * sig
    gg = gg_ref[0].astype(F32)
    gg_hat = gg * hat
    dqs_ref[0, :, HEAD:] = (gg_hat * gain * (sig * (1.0 + swish * (1.0 - sig)))).astype(BF)
    part = jnp.broadcast_to(jnp.sum(gg_hat * silu, axis=0, keepdims=True), (8, HEAD))

    @pl.when(pl.program_id(0) == 0)
    def _():
        sg_ref[...] = part

    @pl.when(pl.program_id(0) > 0)
    def _():
        sg_ref[...] = sg_ref[...] + part

    grad_hat = gg * gain * silu
    dout = scale_out * (grad_hat - hat * jnp.mean(grad_hat * hat, axis=1, keepdims=True))
    dout = dout.astype(BF)
    pairs, running, _ = prefix_levels(log_decay)
    levels = len(pairs)
    growth = jnp.exp(running)
    scores = mm_nt(queries, keys) * SCALE
    grads = mm_nt(dout, values)
    key_part = mm_nt(queries, init[:, :HEAD]) * SCALE * growth
    value_part = mm_nt(dout, init[:, HEAD:]) * growth
    dprob = slot_sums(grads, pairs, inflow) + value_part
    dslot = probs * (dprob - jnp.sum(probs * dprob, axis=1, keepdims=True))
    back = slot_table(dslot, pairs, inflow).astype(BF)
    dslot_g = (dslot * growth).astype(BF)
    prob_g = (probs * growth).astype(BF)
    dqs_ref[0, :, :HEAD] = (SCALE * (mm(back, keys) + mm(dslot_g, init[:, :HEAD]))).astype(BF)
    dkv_ref[0, :, :HEAD] = SCALE * mm_tn(back, queries)
    dkv_ref[0, :, HEAD:] = mm_tn(mix_ref[0], dout)
    adj_ref[0, :, :HEAD] = SCALE * mm_tn(dslot_g, queries)
    adj_ref[0, :, HEAD:] = mm_tn(prob_g, dout)
    diag = diagonal(rows)
    own_a = jnp.sum(jnp.where(diag, scores, 0.0), axis=1, keepdims=True)
    own_b = jnp.sum(jnp.where(diag, grads, 0.0), axis=1, keepdims=True)
    dinflow = dslot * own_a + probs * own_b
    scores_low = scores.astype(BF)
    grads_low = grads.astype(BF)
    fbar = dslot * key_part + probs * value_part
    gbar = jnp.zeros_like(fbar)
    for level in range(levels - 1, -1, -1):
        left, right, amount = factors(pairs[level], level, inflow)
        table_a = level_mask(scores_low, level, levels)
        table_b = level_mask(grads_low, level, levels)
        amount_low = amount.astype(BF)
        dleft = dslot * left
        pleft = probs * left
        grow = dleft * mm(table_a, amount_low) + pleft * mm(table_b, amount_low)
        back_in = mm_tn(table_a, dleft.astype(BF)) + mm_tn(table_b, pleft.astype(BF))
        dinflow = dinflow + right * back_in
        step = 1 << level
        bit = row_bit(rows, level)
        total = pltpu.roll(jnp.where(bit, fbar, 0.0), rows - step, 0) + pltpu.roll(
            jnp.where(bit, 0.0, gbar), step, 0
        )
        fbar = fbar + grow + total
        gbar = gbar + amount * back_in + total
    ddi_ref[0, :, :SLOTS] = fbar
    ddi_ref[0, :, SLOTS:] = dinflow


def finish_kernel(kv_ref, li_ref, init_ref, end_ref, dkv_ref, ddi_ref, okv_ref, oddi_ref):
    kv = kv_ref[0]
    log_decay = li_ref[0, :, :SLOTS]
    inflow = li_ref[0, :, SLOTS:]
    end = end_ref[0]
    rows = kv.shape[0]
    t = lax.broadcasted_iota(jnp.int32, (rows, rows), 0)
    s = lax.broadcasted_iota(jnp.int32, (rows, rows), 1)
    earlier = (s < t).astype(F32)
    after = exact((s > t).astype(F32), log_decay)
    fade = jnp.exp(after)
    weight = fade * inflow
    end_low = end.astype(BF)
    okv_ref[0] = (dkv_ref[0] + mm(weight.astype(BF), end_low)).astype(BF)
    reach = mm_nt(kv, end_low)
    whole = jnp.exp(jnp.sum(log_decay, axis=0, keepdims=True))
    carry = lax.dot_general(
        jnp.ones((8, 2 * HEAD), F32), end * init_ref[0], (((1,), (1,)), ((), ())),
        precision=HIGHEST, preferred_element_type=F32,
    )[0:1]
    oddi_ref[0, :, :SLOTS] = (
        ddi_ref[0, :, :SLOTS] + exact(earlier, weight * reach) + whole * carry
    )
    oddi_ref[0, :, SLOTS:] = ddi_ref[0, :, SLOTS:] + fade * reach


def blocked(shape):
    return pl.BlockSpec((1,) + shape, lambda i: (i, 0, 0))


def run(kernel, args, specs, outs, out_specs, flops, moved):
    return pl.pallas_call(
        kernel,
        grid=(args[0].shape[0],),
        in_specs=specs,
        out_specs=out_specs,
        out_shape=outs,
        cost_estimate=pl.CostEstimate(flops=flops, bytes_accessed=moved, transcendentals=0),
        compiler_params=pltpu.CompilerParams(vmem_limit_bytes=56 << 20),
    )(*args)


def sds(shape, dtype=F32):
    return jax.ShapeDtypeStruct(shape, dtype)


def chunk_states(kv, li):
    n, rows, _ = kv.shape
    return run(
        states_kernel, (kv, li),
        [blocked((rows, 2 * HEAD)), blocked((rows, 2 * SLOTS))],
        (sds((n, SLOTS, 2 * HEAD)), sds((n, SLOTS, 128))),
        (blocked((SLOTS, 2 * HEAD)), blocked((SLOTS, 128))),
        n * 10**9, n * 10**6,
    )


def mixer_forward(qs, kv, li, init, gain):
    n, rows, _ = kv.shape
    return run(
        forward_kernel, (qs, kv, li, init, gain),
        [blocked((rows, 2 * HEAD)), blocked((rows, 2 * HEAD)), blocked((rows, 2 * SLOTS)),
         blocked((SLOTS, 2 * HEAD)), pl.BlockSpec((8, HEAD), lambda i: (0, 0))],
        (sds((n, rows, HEAD), BF), sds((n, rows, HEAD)), sds((n, rows, SLOTS)), sds((n, rows, rows), BF)),
        (blocked((rows, HEAD)), blocked((rows, HEAD)), blocked((rows, SLOTS)), blocked((rows, rows))),
        n * 3 * 10**9, n * 4 * 10**6,
    )


def mixer_backward(qs, kv, li, init, gain, out, probs, mix, gg):
    n, rows, _ = kv.shape
    return run(
        backward_kernel, (qs, kv, li, init, gain, out, probs, mix, gg),
        [blocked((rows, 2 * HEAD)), blocked((rows, 2 * HEAD)), blocked((rows, 2 * SLOTS)),
         blocked((SLOTS, 2 * HEAD)), pl.BlockSpec((8, HEAD), lambda i: (0, 0)),
         blocked((rows, HEAD)), blocked((rows, SLOTS)), blocked((rows, rows)), blocked((rows, HEAD))],
        (sds((n, rows, 2 * HEAD), BF), sds((n, rows, 2 * HEAD)), sds((n, rows, 2 * SLOTS)),
         sds((n, SLOTS, 2 * HEAD)), sds((8, HEAD))),
        (blocked((rows, 2 * HEAD)), blocked((rows, 2 * HEAD)), blocked((rows, 2 * SLOTS)),
         blocked((SLOTS, 2 * HEAD)), pl.BlockSpec((8, HEAD), lambda i: (0, 0))),
        n * 6 * 10**9, n * 5 * 10**6,
    )


def mixer_finish(kv, li, init, end, dkv, ddi):
    n, rows, _ = kv.shape
    return run(
        finish_kernel, (kv, li, init, end, dkv, ddi),
        [blocked((rows, 2 * HEAD)), blocked((rows, 2 * SLOTS)), blocked((SLOTS, 2 * HEAD)),
         blocked((SLOTS, 2 * HEAD)), blocked((rows, 2 * HEAD)), blocked((rows, 2 * SLOTS))],
        (sds((n, rows, 2 * HEAD), BF), sds((n, rows, 2 * SLOTS))),
        (blocked((rows, 2 * HEAD)), blocked((rows, 2 * SLOTS))),
        n * 10**9, n * 3 * 10**6,
    )


D = 2048
HEADS = 4
RANK = 16
NORMALIZER = 8.0


def inverse_rms(values):
    return lax.rsqrt(jnp.mean(values * values, axis=-1, keepdims=True) + EPSILON)


def silu_slope(values):
    sigmoid_val = jax.nn.sigmoid(values)
    return sigmoid_val * (1.0 + values * (1.0 - sigmoid_val))


def norm_back(grad_hat, hat_rows, scale_rows):
    return scale_rows * (
        grad_hat - hat_rows * jnp.mean(grad_hat * hat_rows, axis=-1, keepdims=True)
    )


def swap(value, axis, step):
    count = lax.axis_size(axis)
    return lax.ppermute(value, axis, [(i, i ^ step) for i in range(count)])


def gather_heads(block):
    return [block] + [swap(block, "p", k) for k in range(1, HEADS)]


def scatter_heads(parts, *fillers):
    got = [swap(parts[k], "p", k) for k in range(1, HEADS)]
    if fillers:
        held = lax.optimization_barrier(tuple(got) + fillers)
        got, fillers = held[: HEADS - 1], held[HEADS - 1 :]
    total = parts[0].astype(F32)
    for part in got:
        total = total + part.astype(F32)
    return (total,) + tuple(fillers) if fillers else total


def after(value, *others):
    return lax.optimization_barrier((value,) + others)[0]


def place_kernel(blocks, spot_ref, *refs):
    ins, out = refs[:-1], refs[-1]
    part = ins[0].shape[1]
    for i, ref in enumerate(ins):
        for k in range(blocks):
            start = pl.multiple_of(spot_ref[i * blocks + k] * part, part)
            out[pl.ds(start, part), :] = ref[k]


def place(parts, spots):
    blocks, part, width = parts[0].shape
    chunk = 256
    table = jnp.stack([jnp.asarray(x, jnp.int32) for row in spots for x in row])
    rows = len(parts) * blocks * part
    return pl.pallas_call(
        functools.partial(place_kernel, blocks),
        grid_spec=pltpu.PrefetchScalarGridSpec(
            num_scalar_prefetch=1,
            grid=(width // chunk,),
            in_specs=[pl.BlockSpec((blocks, part, chunk), lambda i, s: (0, 0, i))] * len(parts),
            out_specs=pl.BlockSpec((rows, chunk), lambda i, s: (0, i)),
        ),
        out_shape=jax.ShapeDtypeStruct((rows, width), BF),
        cost_estimate=pl.CostEstimate(flops=0, bytes_accessed=4 * rows * width, transcendentals=0),
        compiler_params=pltpu.CompilerParams(vmem_limit_bytes=56 << 20),
    )(table, *parts)


def column_cuts(shards, here, k):
    cuts = []
    for shard in shards:
        width = shard.shape[1] // HEADS
        cuts.append(lax.dynamic_slice_in_dim(shard, (here ^ k) * width, width, 1))
    return jnp.concatenate(cuts, axis=1)


def head_columns(shards, here):
    copies = lax.axis_size("r")
    turn = lax.axis_index("r")
    own = column_cuts(shards, here, 0)
    pieces = [own] + [swap(column_cuts(shards, here, k), "p", k) for k in range(1, HEADS)]
    parts, spots = [], []
    for k in range(HEADS):
        for m in range(copies):
            piece = pieces[k] if m == 0 else swap(pieces[k], "r", m)
            parts.append(piece[None])
            spots.append([(here ^ k) * copies + (turn ^ m)])
    return place(parts, spots), pieces[1:]


def seq_pieces(shards, here):
    count, spot = lax.axis_size("seq"), lax.axis_index("seq")
    rows = shards[0].shape[0] // count
    shards = [lax.dynamic_slice_in_dim(shard, spot * rows, rows, 0) for shard in shards]
    own = column_cuts(shards, here, 0)
    return jnp.stack([own] + [swap(column_cuts(shards, here, k), "p", k) for k in range(1, HEADS)])


def seq_columns(pieces, here):
    copies, count = lax.axis_size("r"), lax.axis_size("seq")
    turn, spot = lax.axis_index("r"), lax.axis_index("seq")
    parts, spots = [], []
    for j, part in enumerate(gather_seq(pieces)):
        for m in range(copies):
            parts.append(part if m == 0 else swap(part, "r", m))
            spots.append(
                [(((here ^ k) * copies + (turn ^ m)) * count + (spot ^ j)) for k in range(HEADS)]
            )
    return place(parts, spots)


def gather_small(packed, here, turn):
    copies = lax.axis_size("r")
    near = jnp.concatenate([packed] + [swap(packed, "r", m) for m in range(1, copies)])
    both = jnp.concatenate(gather_heads(near))
    heads = jnp.arange(HEADS, dtype=jnp.int32) ^ here
    turns = jnp.arange(copies, dtype=jnp.int32) ^ turn
    order = (heads[:, None] * copies + turns[None, :]).reshape(-1)
    return jnp.take(both, order, axis=0)


def sum_small(value, here, turn):
    mine = [lax.dynamic_index_in_dim(value, here ^ k, 0, False) for k in range(HEADS)]
    total = scatter_heads(mine)
    copies = lax.axis_size("r")
    kept = lax.dynamic_index_in_dim(total, turn, 0, True)
    for m in range(1, copies):
        kept = kept + swap(lax.dynamic_index_in_dim(total, turn ^ m, 0, True), "r", m)
    return kept[0]


def chain(state, decay, forward):
    count = lax.axis_size("seq")
    total = jnp.zeros_like(state)
    for hop in range(count - 1):
        pair = (hop, hop + 1) if forward else (count - 1 - hop, count - 2 - hop)
        sent = (decay * total + state).astype(BF)
        total = total + lax.ppermute(sent, "seq", [pair]).astype(F32)
    return total


def chain_pair(both, decay, forward):
    return jnp.concatenate(
        [chain(both[..., :HEAD], decay, forward), chain(both[..., HEAD:], decay, forward)], axis=-1
    )


def split_rows(left, turn, step, groups):
    copies, width = left.shape[2:]
    flat = left.reshape(left.shape[0], -1)
    cuts = [
        lax.dynamic_slice_in_dim(flat, (g * copies + (turn ^ step)) * width, width, 1)
        for g in groups
    ]
    return jnp.concatenate(cuts, axis=1)


def sum_copies(own, away):
    got = [swap(part, "r", m + 1) for m, part in enumerate(away)]
    total = own()
    for part in got:
        total = total + part.astype(F32)
    return total.astype(BF)


def gather_seq(value):
    count = lax.axis_size("seq")
    found = {0: value}
    step = count // 2
    while step >= 1:
        for j in list(found):
            found[j ^ step] = swap(found[j], "seq", step)
        step //= 2
    return [found[j] for j in range(count)]


def assemble_kernel(counts, spot_ref, *refs):
    n_in, n_out, part = counts
    ins, outs = refs[:n_in], refs[n_in:]
    width = outs[0].shape[1]
    for j in range(n_in):
        for o in range(n_out):
            cut = ins[j][0, :, o * width : (o + 1) * width]
            outs[o][j * part : (j + 1) * part, :] = cut.astype(F32)


def assemble(parts, columns, n_out):
    spans, blocks, part, width = parts.shape
    width //= n_out
    rows = part * spans
    spots = jnp.stack([jnp.asarray(c, jnp.int32) for c in columns])
    return pl.pallas_call(
        functools.partial(assemble_kernel, (spans, n_out, part)),
        grid_spec=pltpu.PrefetchScalarGridSpec(
            num_scalar_prefetch=1,
            grid=(blocks,),
            in_specs=[
                pl.BlockSpec((None, 1, part, n_out * width), lambda i, s, j=j: (j, i, 0, 0))
                for j in range(spans)
            ],
            out_specs=[pl.BlockSpec((rows, width), lambda i, s: (0, s[i]))] * n_out,
        ),
        out_shape=[jax.ShapeDtypeStruct((rows, blocks * width), F32)] * n_out,
        cost_estimate=pl.CostEstimate(
            flops=0, bytes_accessed=6 * n_out * rows * blocks * width, transcendentals=0
        ),
        compiler_params=pltpu.CompilerParams(vmem_limit_bytes=56 << 20),
    )(spots, *([parts] * spans))


def line_pairs(i):
    count = lax.axis_size("seq")
    return [(i, i + 1), (count - 1 - i, count - 2 - i)]


def inward(value, last):
    for i in range(lax.axis_size("seq") // 2 - 1):
        if i in last:
            value = after(value, last[i])
        last[i] = lax.ppermute(value, "seq", line_pairs(i))
        value = value + last[i]
    return value


def across(value, last):
    half = lax.axis_size("seq") // 2
    if "across" in last:
        value = after(value, last["across"])
    last["across"] = lax.ppermute(value, "seq", [(half - 1, half), (half, half - 1)])
    return value + last["across"]


def outward(value, last):
    count, spot = lax.axis_size("seq"), lax.axis_index("seq")
    for i in range(count // 2 - 2, -1, -1):
        if ("out", i) in last:
            value = after(value, last["out", i])
        got = lax.ppermute(value, "seq", [(b, a) for a, b in line_pairs(i)])
        last["out", i] = got
        value = jnp.where((spot == i) | (spot == count - 1 - i), got, value)
    return value


def spread_line(near, far, here):
    got = [far[0], swap(near[0], "p", 1), swap(far[1], "p", 2), swap(near[1], "p", 3)]
    return assemble(jnp.stack(got)[None], [here ^ k for k in range(HEADS)], 2)


def swap_diagonal(part):
    count = lax.axis_size("seq")
    sends = [(p * count + z, (p ^ z) * count + z) for p in range(HEADS) for z in range(count)]
    return lax.ppermute(part, ("p", "seq"), sends)


def body(
    tokens,
    seq_lengths,
    attn_gain,
    query_proj,
    key_proj,
    value_proj,
    decay_down,
    decay_up,
    decay_bias,
    swish_proj,
    slot_gain,
    out_proj,
    mlp_gain,
    mlp_gate,
    mlp_up,
    mlp_down,
    grad_out,
):
    rows = tokens.shape[0]
    copies = lax.axis_size("r")
    owners = HEADS * copies
    shard = D // owners
    here, turn, place = lax.axis_index("p"), lax.axis_index("r"), lax.axis_index("seq")
    group = HEADS * rows

    small = [attn_gain, decay_down, decay_up, decay_bias, slot_gain, mlp_gain, seq_lengths]
    packed = jnp.concatenate([a.astype(F32).reshape(-1) for a in small])
    packed = gather_small(packed[None], here, turn)
    fields, offset = [], 0
    for a in small:
        fields.append(packed[:, offset : offset + a.size])
        offset += a.size
    gain_one = fields[0].reshape(D)
    down_full = fields[1].reshape(D, RANK).astype(BF)
    up_full = fields[2].reshape(owners, RANK, -1).transpose(1, 0, 2).reshape(RANK, HEADS * SLOTS)
    up_head = lax.dynamic_slice_in_dim(up_full, here * SLOTS, SLOTS, 1)
    bias_head = lax.dynamic_slice_in_dim(fields[3].reshape(HEADS * SLOTS), here * SLOTS, SLOTS, 0)
    gain_head = lax.dynamic_slice_in_dim(fields[4].reshape(D), here * HEAD, HEAD, 0)
    gain_head8 = jnp.broadcast_to(gain_head[None], (8, HEAD))
    gain_two = fields[5].reshape(D)
    lengths = fields[6].reshape(HEADS, copies)
    positions = (place * rows + jnp.arange(rows, dtype=jnp.int32)).astype(F32)
    masks = [
        (positions < lax.dynamic_index_in_dim(lengths, here ^ k, 0, False)[turn]).astype(F32)
        for k in range(HEADS)
    ]
    mask_all = jnp.concatenate(masks)[:, None]
    mask_own = masks[0][:, None]

    token_blocks = gather_heads(tokens)
    weight_kv, kv_pieces = head_columns([key_proj, value_proj], here)
    late = lax.optimization_barrier((query_proj, swish_proj, mlp_gate, mlp_up) + tuple(kv_pieces))
    weight_qs, qs_pieces = head_columns(late[:2], here)
    gu_pieces = seq_pieces(late[2:4], here)
    grad_blocks = gather_heads(after(grad_out, *qs_pieces))
    weight_out = lax.all_gather(out_proj, "r", axis=0, tiled=True)
    weight_down = lax.all_gather(mlp_down, "r", axis=0, tiled=True)

    tokens_all = jnp.concatenate(token_blocks).astype(F32)
    normed = (tokens_all * inverse_rms(tokens_all) * gain_one).astype(BF)
    kv = mm(normed, weight_kv).astype(BF).reshape(HEADS, rows, 2 * HEAD)
    gate_low = mm(normed, down_full)
    forget = exact(gate_low, up_head) + bias_head
    log_sig = jax.nn.log_sigmoid(forget) / NORMALIZER
    li = jnp.concatenate([mask_all * log_sig, mask_all * -jnp.expm1(log_sig)], axis=1)
    li = li.reshape(HEADS, rows, 2 * SLOTS)
    state, decay = chunk_states(kv, li)
    decay = decay[:, :, :1]
    init = chain_pair(state, decay, True)
    init, gu_pieces = lax.optimization_barrier((init, gu_pieces))
    weight_gu = seq_columns(gu_pieces, here)
    qs = mm(normed, weight_qs).reshape(HEADS, rows, 2 * HEAD)
    gated, mixer_out, probs, mix = mixer_forward(qs, kv, li, init, gain_head8)
    gated = gated.reshape(group, HEAD)
    attn_part = mm(gated, weight_out).astype(BF).reshape(HEADS, rows, D)
    grad_mlp = (mask_all * jnp.concatenate(grad_blocks).astype(F32)).astype(BF)
    attn_out, grad_act = scatter_heads(
        [attn_part[k] for k in range(HEADS)], mm_nt(grad_mlp, weight_down)
    )

    tokens_f = tokens.astype(F32)
    residual = tokens_f + mask_own * attn_out
    scale_two = inverse_rms(residual)
    hat_two = residual * scale_two
    normed_two_own = (hat_two * gain_two).astype(BF)
    normed_two = jnp.concatenate(gather_heads(normed_two_own))

    hidden_width = weight_down.shape[0]
    gate_up = mm(normed_two, weight_gu)
    gate_pre, up_pre = gate_up[:, :hidden_width], gate_up[:, hidden_width:]
    hidden = (jax.nn.silu(gate_pre) * up_pre).astype(BF)
    grad_gate = (grad_act * up_pre * silu_slope(gate_pre)).astype(BF)
    grad_up = (grad_act * jax.nn.silu(gate_pre)).astype(BF)
    grad_gu = jnp.concatenate([grad_gate, grad_up], axis=1)
    order = [here ^ k for k in range(HEADS)]
    hops = range(1, copies)
    down_rows = mlp_down.shape[0]
    two_view = normed_two.reshape(group, HEADS, copies, shard)
    gu_away = [mm_tn(split_rows(two_view, turn, m, order), grad_gu).astype(BF) for m in hops]
    two_part = mm_nt(after(grad_gu, *gu_away), weight_gu).astype(BF)
    gu_total = sum_copies(
        lambda: mm_tn(split_rows(two_view, turn, 0, order), after(grad_gu, two_part)), gu_away
    )
    gu_part = lax.psum_scatter(
        gu_total.reshape(HEADS, shard, 2 * hidden_width), "seq", scatter_dimension=0, tiled=True
    )
    hidden_late = after(hidden, gu_total)

    def down_grad_part(m):
        cut = lax.dynamic_slice_in_dim(hidden_late, (turn ^ m) * down_rows, down_rows, 1)
        return mm_tn(cut, grad_mlp)

    down_total = sum_copies(
        lambda: down_grad_part(0), [down_grad_part(m).astype(BF) for m in hops]
    )
    two_part = two_part.reshape(HEADS, rows, D)
    grad_norm_two, down_total = scatter_heads([two_part[k] for k in range(HEADS)], down_total)
    gain_two_grad = jnp.sum(grad_norm_two * hat_two, axis=0)
    grad_rows = grad_out.astype(F32)
    grad_resid = grad_rows + norm_back(grad_norm_two * gain_two, hat_two, scale_two)
    grad_attn_own = (mask_own * grad_resid).astype(BF)
    attn_blocks = gather_heads(grad_attn_own)
    mlp_part = mm(hidden, weight_down).astype(BF)
    mlp_part, gu_part, *attn_blocks = lax.optimization_barrier((mlp_part, gu_part, *attn_blocks))
    gu_part = swap_diagonal(gu_part)
    grad_attn = jnp.concatenate(attn_blocks)
    mlp_part = mlp_part.reshape(HEADS, rows, D)
    mlp_part = jnp.stack(
        [lax.dynamic_index_in_dim(mlp_part, here ^ k, 0, False) for k in range(HEADS)]
    )

    grad_gated = mm_nt(grad_attn, weight_out).reshape(HEADS, rows, HEAD)
    grad_qs, grad_kv, grad_li, adjoint, slot_part = mixer_backward(
        qs, kv, li, init, gain_head8, mixer_out, probs, mix, grad_gated
    )
    adjoint, gu_part = lax.optimization_barrier((adjoint, gu_part))
    gu_whole = lax.all_gather(gu_part, "seq", axis=0, tiled=True)
    one_view = normed.reshape(group, HEADS, copies, shard)
    one_views = [split_rows(one_view, turn, m, order) for m in range(copies)]
    out_view = gated.reshape(group, 1, copies, shard)
    out_views = [split_rows(out_view, turn, m, [0]) for m in range(copies)]

    def weight_grad(views, right):
        return sum_copies(
            lambda: mm_tn(views[0], right), [mm_tn(views[m], right).astype(BF) for m in hops]
        )

    grad_qs = grad_qs.reshape(group, 2 * HEAD)
    out_total = weight_grad(out_views, grad_attn)
    qs_total = weight_grad(one_views, grad_qs)
    ends = chain_pair(adjoint, decay, False)
    ends, out_total, qs_total = lax.optimization_barrier((ends, out_total, qs_total))
    grad_kv, grad_li = mixer_finish(kv, li, init, ends, grad_kv, grad_li)
    half_rows, line = down_rows // 2, {}
    grad_kv, mlp_part, gu_whole, down_total = lax.optimization_barrier(
        (grad_kv, mlp_part, gu_whole, down_total)
    )
    mlp_out = lax.psum_scatter(mlp_part, "p", scatter_dimension=0, tiled=False).astype(F32)
    down_near = inward(down_total[:half_rows], line)
    grad_qs, down_near = lax.optimization_barrier((grad_qs, down_near))
    result = (residual + mask_own * mlp_out).astype(BF)
    grad_kv = grad_kv.reshape(group, 2 * HEAD)
    grad_li = grad_li.reshape(group, 2 * SLOTS)
    grad_decay = (
        mask_all
        * (grad_li[:, :SLOTS] - grad_li[:, SLOTS:] * jnp.exp(log_sig))
        / NORMALIZER
        * jax.nn.sigmoid(-forget)
    )
    bias_part = jnp.sum(grad_decay, axis=0)
    up_part = lax.dot_general(
        gate_low, grad_decay, (((0,), (0,)), ((), ())), precision=HIGHEST, preferred_element_type=F32
    )
    grad_low = lax.dot_general(
        grad_decay, up_head, (((1,), (1,)), ((), ())), precision=HIGHEST, preferred_element_type=F32
    ).astype(BF)
    down_low_part = mm_tn(normed, grad_low)

    one_part = (
        (mm_nt(grad_qs, weight_qs) + mm_nt(grad_kv, weight_kv) + mm_nt(grad_low, down_full))
        .astype(BF)
        .reshape(HEADS, rows, D)
    )
    kv_total = weight_grad(one_views, grad_kv)
    grad_norm_one, kv_total = scatter_heads([one_part[k] for k in range(HEADS)], kv_total)

    scale_one = inverse_rms(tokens_f)
    hat_one = tokens_f * scale_one
    gain_one_grad = jnp.sum(grad_norm_one * hat_one, axis=0)
    grad_tokens = (grad_resid + norm_back(grad_norm_one * gain_one, hat_one, scale_one)).astype(BF)

    def placed(part, width):
        whole = jnp.zeros(part.shape[:-1] + (HEADS * width,), F32)
        return lax.dynamic_update_slice_in_dim(whole, part, here * width, part.ndim - 1)

    up_sum = placed(up_part, SLOTS).reshape(RANK, HEADS, copies, -1).transpose(1, 2, 0, 3)
    sums = [
        gain_one_grad,
        down_low_part,
        up_sum,
        placed(bias_part, SLOTS),
        placed(slot_part[0], HEAD),
        gain_two_grad,
    ]
    flat = jnp.concatenate([a.reshape(HEADS, copies, -1) for a in sums], axis=2)
    flat = sum_small(flat, here, turn)
    lanes = D * 8
    flat = jnp.pad(flat, (0, -flat.size % lanes)).astype(BF).reshape(-1, D)

    qs_total = qs_total.reshape(HEADS, shard, 2 * HEAD)
    kv_total = kv_total.reshape(HEADS, shard, 2 * HEAD)
    chunks = [down_total[half_rows:], qs_total[1::2], qs_total[0::2]]
    chunks += [kv_total[1::2], kv_total[0::2], jnp.concatenate([out_total, flat])]
    summed = [outward(across(down_near, line), line)]
    for chunk in chunks:
        summed.append(outward(across(inward(chunk, line), line), line))
    near, far, *wide, tail = summed
    down_grad = jnp.concatenate([near, far])
    gate_grad, up_grad = assemble(gu_whole[None], order, 2)
    query_grad, swish_grad = spread_line(wide[0], wide[1], here)
    key_grad, value_grad = spread_line(wide[2], wide[3], here)
    out_grad = tail[:shard].astype(F32)
    flat = tail[shard:].reshape(-1).astype(F32)
    totals, offset = [], 0
    for a in sums:
        size = a.size // owners
        totals.append(flat[offset : offset + size])
        offset += size

    return (
        result,
        grad_tokens,
        totals[0],
        query_grad,
        key_grad,
        value_grad,
        totals[1].reshape(shard, RANK),
        totals[2].reshape(RANK, -1),
        totals[3],
        swish_grad,
        totals[4],
        out_grad,
        totals[5],
        gate_grad,
        up_grad,
        down_grad.astype(F32),
    )


def solution(mesh):
    count, span = mesh.devices.shape
    split = Mesh(mesh.devices.reshape(HEADS, count // HEADS, span), ("p", "r", "seq"))
    rows = P(("p", "r", "seq"), None)
    matrix, vector, last = P(("p", "r"), None), P(("p", "r")), P(None, ("p", "r"))
    in_specs = (
        rows, vector, vector, matrix, matrix, matrix, matrix, last, vector, matrix, vector, matrix,
        vector, matrix, matrix, matrix, rows,
    )
    out_specs = (
        rows, rows, vector, matrix, matrix, matrix, matrix, last, vector, matrix, vector, matrix,
        vector, matrix, matrix, matrix,
    )
    return jax.shard_map(body, mesh=split, in_specs=in_specs, out_specs=out_specs, check_vma=False)
```

```python
import functools
import jax
import jax.numpy as jnp
from jax import lax
from jax.experimental import pallas as pl
from jax.experimental.pallas import tpu as pltpu
from jax.sharding import Mesh, PartitionSpec as P

HEAD = 512
SLOTS = 64
SCALE = HEAD ** (-0.5)
EPSILON = 1e-06
HIGHEST = lax.Precision.HIGHEST
BF = jnp.bfloat16
F32 = jnp.float32


def mm(a, b):
    return lax.dot_general(a, b, (((1,), (0,)), ((), ())), preferred_element_type=F32)


def mm_nt(a, b):
    return lax.dot_general(a, b, (((1,), (1,)), ((), ())), preferred_element_type=F32)


def mm_tn(a, b):
    return lax.dot_general(a, b, (((0,), (0,)), ((), ())), preferred_element_type=F32)


def exact(a, b):
    return lax.dot_general(
        a, b, (((1,), (0,)), ((), ())), precision=HIGHEST, preferred_element_type=F32
    )


def row_bit(rows, level):
    t = lax.broadcasted_iota(jnp.int32, (rows, SLOTS), 0)
    return ((t >> level) & 1) == 1


def prefix_levels(log_decay):
    rows = log_decay.shape[0]
    levels = rows.bit_length() - 1
    f, g = log_decay, jnp.zeros_like(log_decay)
    out = []
    for level in range(levels):
        out.append((f, g))
        total = f + g
        step = 1 << level
        bit = row_bit(rows, level)
        f = f + jnp.where(bit, pltpu.roll(total, step, 0), 0.0)
        g = g + jnp.where(bit, 0.0, pltpu.roll(total, rows - step, 0))
    return out, f, g


def same_block(rows, level):
    t = lax.broadcasted_iota(jnp.int32, (rows, rows), 0)
    s = lax.broadcasted_iota(jnp.int32, (rows, rows), 1)
    return (t >> (level + 1)) == (s >> (level + 1))


def level_mask(table, level, levels):
    if level == levels - 1:
        return table
    return jnp.where(same_block(table.shape[0], level), table, jnp.zeros_like(table))


def factors(pair, level, inflow):
    f, g = pair
    bit = row_bit(f.shape[0], level)
    left = jnp.where(bit, jnp.exp(f), 0.0)
    right = jnp.where(bit, 0.0, jnp.exp(g))
    return left, right, right * inflow


def diagonal(rows):
    t = lax.broadcasted_iota(jnp.int32, (rows, rows), 0)
    s = lax.broadcasted_iota(jnp.int32, (rows, rows), 1)
    return t == s


def slot_table(weights, pairs, inflow):
    rows = weights.shape[0]
    levels = len(pairs)
    table = jnp.where(diagonal(rows), jnp.sum(weights * inflow, axis=1, keepdims=True), 0.0)
    for level in range(levels):
        left, _, gain = factors(pairs[level], level, inflow)
        block = mm_nt((weights * left).astype(BF), gain.astype(BF))
        table = table + level_mask(block, level, levels)
    return table


def slot_sums(table, pairs, inflow):
    rows = table.shape[0]
    levels = len(pairs)
    own = jnp.sum(jnp.where(diagonal(rows), table, 0.0), axis=1, keepdims=True)
    low = table.astype(BF)
    total = own * inflow
    for level in range(levels):
        left, _, gain = factors(pairs[level], level, inflow)
        total = total + left * mm(level_mask(low, level, levels), gain.astype(BF))
    return total


def states_kernel(kv_ref, li_ref, state_ref, decay_ref):
    kv = kv_ref[0]
    log_decay = li_ref[0, :, :SLOTS]
    inflow = li_ref[0, :, SLOTS:]
    rows = kv.shape[0]
    t = lax.broadcasted_iota(jnp.int32, (rows, rows), 0)
    s = lax.broadcasted_iota(jnp.int32, (rows, rows), 1)
    after = exact((s > t).astype(F32), log_decay)
    weight = jnp.exp(after) * inflow
    state_ref[0] = mm_tn(weight.astype(BF), kv)
    total = lax.dot_general(
        log_decay, jnp.ones((rows, 128), F32), (((0,), (0,)), ((), ())),
        precision=HIGHEST, preferred_element_type=F32,
    )
    decay_ref[0] = jnp.exp(total)


def forward_kernel(qs_ref, kv_ref, li_ref, init_ref, gain_ref, gated_ref, out_ref, prob_ref, mix_ref):
    queries = qs_ref[0, :, :HEAD].astype(BF)
    swish = qs_ref[0, :, HEAD:]
    keys = kv_ref[0, :, :HEAD]
    values = kv_ref[0, :, HEAD:]
    log_decay = li_ref[0, :, :SLOTS]
    inflow = li_ref[0, :, SLOTS:]
    init = init_ref[0].astype(BF)
    pairs, running, _ = prefix_levels(log_decay)
    growth = jnp.exp(running)
    scores = mm_nt(queries, keys) * SCALE
    slots = slot_sums(scores, pairs, inflow) + mm_nt(queries, init[:, :HEAD]) * SCALE * growth
    top = jnp.max(slots, axis=1, keepdims=True)
    weights = jnp.exp(slots - top)
    probs = weights / jnp.sum(weights, axis=1, keepdims=True)
    mix = slot_table(probs, pairs, inflow).astype(BF)
    out = mm(mix, values) + mm((probs * growth).astype(BF), init[:, HEAD:])
    hat = out * lax.rsqrt(jnp.mean(out * out, axis=1, keepdims=True) + EPSILON)
    gated_ref[0] = (hat * gain_ref[0:1] * (swish * jax.nn.sigmoid(swish))).astype(BF)
    out_ref[0] = out
    prob_ref[0] = probs
    mix_ref[0] = mix


def backward_kernel(
    qs_ref, kv_ref, li_ref, init_ref, gain_ref, out_ref, prob_ref, mix_ref, gg_ref,
    dqs_ref, dkv_ref, ddi_ref, adj_ref, sg_ref,
):
    queries = qs_ref[0, :, :HEAD].astype(BF)
    swish = qs_ref[0, :, HEAD:]
    keys = kv_ref[0, :, :HEAD]
    values = kv_ref[0, :, HEAD:]
    log_decay = li_ref[0, :, :SLOTS]
    inflow = li_ref[0, :, SLOTS:]
    init = init_ref[0].astype(BF)
    out = out_ref[0]
    probs = prob_ref[0]
    gain = gain_ref[0:1]
    rows = out.shape[0]
    scale_out = lax.rsqrt(jnp.mean(out * out, axis=1, keepdims=True) + EPSILON)
    hat = out * scale_out
    sig = jax.nn.sigmoid(swish)
    silu = swish * sig
    gg = gg_ref[0].astype(F32)
    gg_hat = gg * hat
    dqs_ref[0, :, HEAD:] = (gg_hat * gain * (sig * (1.0 + swish * (1.0 - sig)))).astype(BF)
    part = jnp.broadcast_to(jnp.sum(gg_hat * silu, axis=0, keepdims=True), (8, HEAD))

    @pl.when(pl.program_id(0) == 0)
    def _():
        sg_ref[...] = part

    @pl.when(pl.program_id(0) > 0)
    def _():
        sg_ref[...] = sg_ref[...] + part

    grad_hat = gg * gain * silu
    dout = scale_out * (grad_hat - hat * jnp.mean(grad_hat * hat, axis=1, keepdims=True))
    dout = dout.astype(BF)
    pairs, running, _ = prefix_levels(log_decay)
    levels = len(pairs)
    growth = jnp.exp(running)
    scores = mm_nt(queries, keys) * SCALE
    grads = mm_nt(dout, values)
    key_part = mm_nt(queries, init[:, :HEAD]) * SCALE * growth
    value_part = mm_nt(dout, init[:, HEAD:]) * growth
    dprob = slot_sums(grads, pairs, inflow) + value_part
    dslot = probs * (dprob - jnp.sum(probs * dprob, axis=1, keepdims=True))
    back = slot_table(dslot, pairs, inflow).astype(BF)
    dslot_g = (dslot * growth).astype(BF)
    prob_g = (probs * growth).astype(BF)
    dqs_ref[0, :, :HEAD] = (SCALE * (mm(back, keys) + mm(dslot_g, init[:, :HEAD]))).astype(BF)
    dkv_ref[0, :, :HEAD] = SCALE * mm_tn(back, queries)
    dkv_ref[0, :, HEAD:] = mm_tn(mix_ref[0], dout)
    adj_ref[0, :, :HEAD] = SCALE * mm_tn(dslot_g, queries)
    adj_ref[0, :, HEAD:] = mm_tn(prob_g, dout)
    diag = diagonal(rows)
    own_a = jnp.sum(jnp.where(diag, scores, 0.0), axis=1, keepdims=True)
    own_b = jnp.sum(jnp.where(diag, grads, 0.0), axis=1, keepdims=True)
    dinflow = dslot * own_a + probs * own_b
    scores_low = scores.astype(BF)
    grads_low = grads.astype(BF)
    fbar = dslot * key_part + probs * value_part
    gbar = jnp.zeros_like(fbar)
    for level in range(levels - 1, -1, -1):
        left, right, amount = factors(pairs[level], level, inflow)
        table_a = level_mask(scores_low, level, levels)
        table_b = level_mask(grads_low, level, levels)
        amount_low = amount.astype(BF)
        dleft = dslot * left
        pleft = probs * left
        grow = dleft * mm(table_a, amount_low) + pleft * mm(table_b, amount_low)
        back_in = mm_tn(table_a, dleft.astype(BF)) + mm_tn(table_b, pleft.astype(BF))
        dinflow = dinflow + right * back_in
        step = 1 << level
        bit = row_bit(rows, level)
        total = pltpu.roll(jnp.where(bit, fbar, 0.0), rows - step, 0) + pltpu.roll(
            jnp.where(bit, 0.0, gbar), step, 0
        )
        fbar = fbar + grow + total
        gbar = gbar + amount * back_in + total
    ddi_ref[0, :, :SLOTS] = fbar
    ddi_ref[0, :, SLOTS:] = dinflow


def finish_kernel(kv_ref, li_ref, init_ref, end_ref, dkv_ref, ddi_ref, okv_ref, oddi_ref):
    kv = kv_ref[0]
    log_decay = li_ref[0, :, :SLOTS]
    inflow = li_ref[0, :, SLOTS:]
    end = end_ref[0]
    rows = kv.shape[0]
    t = lax.broadcasted_iota(jnp.int32, (rows, rows), 0)
    s = lax.broadcasted_iota(jnp.int32, (rows, rows), 1)
    earlier = (s < t).astype(F32)
    after = exact((s > t).astype(F32), log_decay)
    fade = jnp.exp(after)
    weight = fade * inflow
    end_low = end.astype(BF)
    okv_ref[0] = (dkv_ref[0] + mm(weight.astype(BF), end_low)).astype(BF)
    reach = mm_nt(kv, end_low)
    whole = jnp.exp(jnp.sum(log_decay, axis=0, keepdims=True))
    carry = lax.dot_general(
        jnp.ones((8, 2 * HEAD), F32), end * init_ref[0], (((1,), (1,)), ((), ())),
        precision=HIGHEST, preferred_element_type=F32,
    )[0:1]
    oddi_ref[0, :, :SLOTS] = (
        ddi_ref[0, :, :SLOTS] + exact(earlier, weight * reach) + whole * carry
    )
    oddi_ref[0, :, SLOTS:] = ddi_ref[0, :, SLOTS:] + fade * reach


def blocked(shape):
    return pl.BlockSpec((1,) + shape, lambda i: (i, 0, 0))


def run(kernel, args, specs, outs, out_specs, flops, moved):
    return pl.pallas_call(
        kernel,
        grid=(args[0].shape[0],),
        in_specs=specs,
        out_specs=out_specs,
        out_shape=outs,
        cost_estimate=pl.CostEstimate(flops=flops, bytes_accessed=moved, transcendentals=0),
        compiler_params=pltpu.CompilerParams(vmem_limit_bytes=56 << 20),
    )(*args)


def sds(shape, dtype=F32):
    return jax.ShapeDtypeStruct(shape, dtype)


def chunk_states(kv, li):
    n, rows, _ = kv.shape
    return run(
        states_kernel, (kv, li),
        [blocked((rows, 2 * HEAD)), blocked((rows, 2 * SLOTS))],
        (sds((n, SLOTS, 2 * HEAD)), sds((n, SLOTS, 128))),
        (blocked((SLOTS, 2 * HEAD)), blocked((SLOTS, 128))),
        n * 10**9, n * 10**6,
    )


def mixer_forward(qs, kv, li, init, gain):
    n, rows, _ = kv.shape
    return run(
        forward_kernel, (qs, kv, li, init, gain),
        [blocked((rows, 2 * HEAD)), blocked((rows, 2 * HEAD)), blocked((rows, 2 * SLOTS)),
         blocked((SLOTS, 2 * HEAD)), pl.BlockSpec((8, HEAD), lambda i: (0, 0))],
        (sds((n, rows, HEAD), BF), sds((n, rows, HEAD)), sds((n, rows, SLOTS)), sds((n, rows, rows), BF)),
        (blocked((rows, HEAD)), blocked((rows, HEAD)), blocked((rows, SLOTS)), blocked((rows, rows))),
        n * 3 * 10**9, n * 4 * 10**6,
    )


def mixer_backward(qs, kv, li, init, gain, out, probs, mix, gg):
    n, rows, _ = kv.shape
    return run(
        backward_kernel, (qs, kv, li, init, gain, out, probs, mix, gg),
        [blocked((rows, 2 * HEAD)), blocked((rows, 2 * HEAD)), blocked((rows, 2 * SLOTS)),
         blocked((SLOTS, 2 * HEAD)), pl.BlockSpec((8, HEAD), lambda i: (0, 0)),
         blocked((rows, HEAD)), blocked((rows, SLOTS)), blocked((rows, rows)), blocked((rows, HEAD))],
        (sds((n, rows, 2 * HEAD), BF), sds((n, rows, 2 * HEAD)), sds((n, rows, 2 * SLOTS)),
         sds((n, SLOTS, 2 * HEAD)), sds((8, HEAD))),
        (blocked((rows, 2 * HEAD)), blocked((rows, 2 * HEAD)), blocked((rows, 2 * SLOTS)),
         blocked((SLOTS, 2 * HEAD)), pl.BlockSpec((8, HEAD), lambda i: (0, 0))),
        n * 6 * 10**9, n * 5 * 10**6,
    )


def mixer_finish(kv, li, init, end, dkv, ddi):
    n, rows, _ = kv.shape
    return run(
        finish_kernel, (kv, li, init, end, dkv, ddi),
        [blocked((rows, 2 * HEAD)), blocked((rows, 2 * SLOTS)), blocked((SLOTS, 2 * HEAD)),
         blocked((SLOTS, 2 * HEAD)), blocked((rows, 2 * HEAD)), blocked((rows, 2 * SLOTS))],
        (sds((n, rows, 2 * HEAD), BF), sds((n, rows, 2 * SLOTS))),
        (blocked((rows, 2 * HEAD)), blocked((rows, 2 * SLOTS))),
        n * 10**9, n * 3 * 10**6,
    )


D = 2048
HEADS = 4
RANK = 16
NORMALIZER = 8.0


def inverse_rms(values):
    return lax.rsqrt(jnp.mean(values * values, axis=-1, keepdims=True) + EPSILON)


def silu_slope(values):
    sigmoid_val = jax.nn.sigmoid(values)
    return sigmoid_val * (1.0 + values * (1.0 - sigmoid_val))


def norm_back(grad_hat, hat_rows, scale_rows):
    return scale_rows * (
        grad_hat - hat_rows * jnp.mean(grad_hat * hat_rows, axis=-1, keepdims=True)
    )


def swap(value, axis, step):
    count = lax.axis_size(axis)
    return lax.ppermute(value, axis, [(i, i ^ step) for i in range(count)])


def gather_heads(block):
    return [block] + [swap(block, "p", k) for k in range(1, HEADS)]


def scatter_heads(parts, *fillers):
    got = [swap(parts[k], "p", k) for k in range(1, HEADS)]
    if fillers:
        held = lax.optimization_barrier(tuple(got) + fillers)
        got, fillers = held[: HEADS - 1], held[HEADS - 1 :]
    total = parts[0].astype(F32)
    for part in got:
        total = total + part.astype(F32)
    return (total,) + tuple(fillers) if fillers else total


def after(value, *others):
    return lax.optimization_barrier((value,) + others)[0]


def place_kernel(blocks, spot_ref, *refs):
    ins, out = refs[:-1], refs[-1]
    part = ins[0].shape[1]
    for i, ref in enumerate(ins):
        for k in range(blocks):
            start = pl.multiple_of(spot_ref[i * blocks + k] * part, part)
            out[pl.ds(start, part), :] = ref[k]


def place(parts, spots):
    blocks, part, width = parts[0].shape
    chunk = 256
    table = jnp.stack([jnp.asarray(x, jnp.int32) for row in spots for x in row])
    rows = len(parts) * blocks * part
    return pl.pallas_call(
        functools.partial(place_kernel, blocks),
        grid_spec=pltpu.PrefetchScalarGridSpec(
            num_scalar_prefetch=1,
            grid=(width // chunk,),
            in_specs=[pl.BlockSpec((blocks, part, chunk), lambda i, s: (0, 0, i))] * len(parts),
            out_specs=pl.BlockSpec((rows, chunk), lambda i, s: (0, i)),
        ),
        out_shape=jax.ShapeDtypeStruct((rows, width), BF),
        cost_estimate=pl.CostEstimate(flops=0, bytes_accessed=4 * rows * width, transcendentals=0),
        compiler_params=pltpu.CompilerParams(vmem_limit_bytes=56 << 20),
    )(table, *parts)


def column_cuts(shards, here, k):
    cuts = []
    for shard in shards:
        width = shard.shape[1] // HEADS
        cuts.append(lax.dynamic_slice_in_dim(shard, (here ^ k) * width, width, 1))
    return jnp.concatenate(cuts, axis=1)


def head_columns(shards, here):
    copies = lax.axis_size("r")
    turn = lax.axis_index("r")
    own = column_cuts(shards, here, 0)
    pieces = [own] + [swap(column_cuts(shards, here, k), "p", k) for k in range(1, HEADS)]
    parts, spots = [], []
    for k in range(HEADS):
        for m in range(copies):
            piece = pieces[k] if m == 0 else swap(pieces[k], "r", m)
            parts.append(piece[None])
            spots.append([(here ^ k) * copies + (turn ^ m)])
    return place(parts, spots), pieces[1:]


def seq_pieces(shards, here):
    count, spot = lax.axis_size("seq"), lax.axis_index("seq")
    rows = shards[0].shape[0] // count
    shards = [lax.dynamic_slice_in_dim(shard, spot * rows, rows, 0) for shard in shards]
    own = column_cuts(shards, here, 0)
    return jnp.stack([own] + [swap(column_cuts(shards, here, k), "p", k) for k in range(1, HEADS)])


def seq_columns(pieces, here):
    copies, count = lax.axis_size("r"), lax.axis_size("seq")
    turn, spot = lax.axis_index("r"), lax.axis_index("seq")
    parts, spots = [], []
    for j, part in enumerate(gather_seq(pieces)):
        for m in range(copies):
            parts.append(part if m == 0 else swap(part, "r", m))
            spots.append(
                [(((here ^ k) * copies + (turn ^ m)) * count + (spot ^ j)) for k in range(HEADS)]
            )
    return place(parts, spots)


def gather_small(packed, here, turn):
    copies = lax.axis_size("r")
    near = jnp.concatenate([packed] + [swap(packed, "r", m) for m in range(1, copies)])
    both = jnp.concatenate(gather_heads(near))
    heads = jnp.arange(HEADS, dtype=jnp.int32) ^ here
    turns = jnp.arange(copies, dtype=jnp.int32) ^ turn
    order = (heads[:, None] * copies + turns[None, :]).reshape(-1)
    return jnp.take(both, order, axis=0)


def sum_small(value, here, turn):
    mine = [lax.dynamic_index_in_dim(value, here ^ k, 0, False) for k in range(HEADS)]
    total = scatter_heads(mine)
    copies = lax.axis_size("r")
    kept = lax.dynamic_index_in_dim(total, turn, 0, True)
    for m in range(1, copies):
        kept = kept + swap(lax.dynamic_index_in_dim(total, turn ^ m, 0, True), "r", m)
    return kept[0]


def chain(state, decay, forward):
    count = lax.axis_size("seq")
    total = jnp.zeros_like(state)
    for hop in range(count - 1):
        pair = (hop, hop + 1) if forward else (count - 1 - hop, count - 2 - hop)
        sent = (decay * total + state).astype(BF)
        total = total + lax.ppermute(sent, "seq", [pair]).astype(F32)
    return total


def chain_pair(both, decay, forward):
    return jnp.concatenate(
        [chain(both[..., :HEAD], decay, forward), chain(both[..., HEAD:], decay, forward)], axis=-1
    )


def split_rows(left, turn, step, groups):
    copies, width = left.shape[2:]
    flat = left.reshape(left.shape[0], -1)
    cuts = [
        lax.dynamic_slice_in_dim(flat, (g * copies + (turn ^ step)) * width, width, 1)
        for g in groups
    ]
    return jnp.concatenate(cuts, axis=1)


def sum_copies(own, away):
    got = [swap(part, "r", m + 1) for m, part in enumerate(away)]
    total = own()
    for part in got:
        total = total + part.astype(F32)
    return total.astype(BF)


def gather_seq(value):
    count = lax.axis_size("seq")
    found = {0: value}
    step = count // 2
    while step >= 1:
        for j in list(found):
            found[j ^ step] = swap(found[j], "seq", step)
        step //= 2
    return [found[j] for j in range(count)]


def assemble_kernel(counts, spot_ref, *refs):
    n_in, n_out, part = counts
    ins, outs = refs[:n_in], refs[n_in:]
    width = outs[0].shape[1]
    for j in range(n_in):
        for o in range(n_out):
            cut = ins[j][0, :, o * width : (o + 1) * width]
            outs[o][j * part : (j + 1) * part, :] = cut.astype(F32)


def assemble(parts, columns, n_out):
    spans, blocks, part, width = parts.shape
    width //= n_out
    rows = part * spans
    spots = jnp.stack([jnp.asarray(c, jnp.int32) for c in columns])
    return pl.pallas_call(
        functools.partial(assemble_kernel, (spans, n_out, part)),
        grid_spec=pltpu.PrefetchScalarGridSpec(
            num_scalar_prefetch=1,
            grid=(blocks,),
            in_specs=[
                pl.BlockSpec((None, 1, part, n_out * width), lambda i, s, j=j: (j, i, 0, 0))
                for j in range(spans)
            ],
            out_specs=[pl.BlockSpec((rows, width), lambda i, s: (0, s[i]))] * n_out,
        ),
        out_shape=[jax.ShapeDtypeStruct((rows, blocks * width), F32)] * n_out,
        cost_estimate=pl.CostEstimate(
            flops=0, bytes_accessed=6 * n_out * rows * blocks * width, transcendentals=0
        ),
        compiler_params=pltpu.CompilerParams(vmem_limit_bytes=56 << 20),
    )(spots, *([parts] * spans))


def line_pairs(i):
    count = lax.axis_size("seq")
    return [(i, i + 1), (count - 1 - i, count - 2 - i)]


def inward(value, last):
    for i in range(lax.axis_size("seq") // 2 - 1):
        if i in last:
            value = after(value, last[i])
        last[i] = lax.ppermute(value, "seq", line_pairs(i))
        value = value + last[i]
    return value


def across(value, last):
    half = lax.axis_size("seq") // 2
    if "across" in last:
        value = after(value, last["across"])
    last["across"] = lax.ppermute(value, "seq", [(half - 1, half), (half, half - 1)])
    return value + last["across"]


def outward(value, last):
    count, spot = lax.axis_size("seq"), lax.axis_index("seq")
    for i in range(count // 2 - 2, -1, -1):
        if ("out", i) in last:
            value = after(value, last["out", i])
        got = lax.ppermute(value, "seq", [(b, a) for a, b in line_pairs(i)])
        last["out", i] = got
        value = jnp.where((spot == i) | (spot == count - 1 - i), got, value)
    return value


def spread_line(near, far, here):
    got = [far[0], swap(near[0], "p", 1), swap(far[1], "p", 2), swap(near[1], "p", 3)]
    return assemble(jnp.stack(got)[None], [here ^ k for k in range(HEADS)], 2)


def swap_diagonal(part):
    count = lax.axis_size("seq")
    sends = [(p * count + z, (p ^ z) * count + z) for p in range(HEADS) for z in range(count)]
    return lax.ppermute(part, ("p", "seq"), sends)


def body(
    tokens,
    seq_lengths,
    attn_gain,
    query_proj,
    key_proj,
    value_proj,
    decay_down,
    decay_up,
    decay_bias,
    swish_proj,
    slot_gain,
    out_proj,
    mlp_gain,
    mlp_gate,
    mlp_up,
    mlp_down,
    grad_out,
):
    rows = tokens.shape[0]
    copies = lax.axis_size("r")
    owners = HEADS * copies
    shard = D // owners
    here, turn, place = lax.axis_index("p"), lax.axis_index("r"), lax.axis_index("seq")
    group = HEADS * rows

    small = [attn_gain, decay_down, decay_up, decay_bias, slot_gain, mlp_gain, seq_lengths]
    packed = jnp.concatenate([a.astype(F32).reshape(-1) for a in small])
    packed = gather_small(packed[None], here, turn)
    fields, offset = [], 0
    for a in small:
        fields.append(packed[:, offset : offset + a.size])
        offset += a.size
    gain_one = fields[0].reshape(D)
    down_full = fields[1].reshape(D, RANK).astype(BF)
    up_full = fields[2].reshape(owners, RANK, -1).transpose(1, 0, 2).reshape(RANK, HEADS * SLOTS)
    up_head = lax.dynamic_slice_in_dim(up_full, here * SLOTS, SLOTS, 1)
    bias_head = lax.dynamic_slice_in_dim(fields[3].reshape(HEADS * SLOTS), here * SLOTS, SLOTS, 0)
    gain_head = lax.dynamic_slice_in_dim(fields[4].reshape(D), here * HEAD, HEAD, 0)
    gain_head8 = jnp.broadcast_to(gain_head[None], (8, HEAD))
    gain_two = fields[5].reshape(D)
    lengths = fields[6].reshape(HEADS, copies)
    positions = (place * rows + jnp.arange(rows, dtype=jnp.int32)).astype(F32)
    masks = [
        (positions < lax.dynamic_index_in_dim(lengths, here ^ k, 0, False)[turn]).astype(F32)
        for k in range(HEADS)
    ]
    mask_all = jnp.concatenate(masks)[:, None]
    mask_own = masks[0][:, None]

    token_blocks = gather_heads(tokens)
    weight_kv, kv_pieces = head_columns([key_proj, value_proj], here)
    late = lax.optimization_barrier((query_proj, swish_proj, mlp_gate, mlp_up) + tuple(kv_pieces))
    weight_qs, qs_pieces = head_columns(late[:2], here)
    gu_pieces = seq_pieces(late[2:4], here)
    grad_blocks = gather_heads(after(grad_out, *qs_pieces))
    weight_out = lax.all_gather(out_proj, "r", axis=0, tiled=True)
    weight_down = lax.all_gather(mlp_down, "r", axis=0, tiled=True)

    tokens_all = jnp.concatenate(token_blocks).astype(F32)
    normed = (tokens_all * inverse_rms(tokens_all) * gain_one).astype(BF)
    kv = mm(normed, weight_kv).astype(BF).reshape(HEADS, rows, 2 * HEAD)
    gate_low = mm(normed, down_full)
    forget = exact(gate_low, up_head) + bias_head
    log_sig = jax.nn.log_sigmoid(forget) / NORMALIZER
    li = jnp.concatenate([mask_all * log_sig, mask_all * -jnp.expm1(log_sig)], axis=1)
    li = li.reshape(HEADS, rows, 2 * SLOTS)
    state, decay = chunk_states(kv, li)
    decay = decay[:, :, :1]
    init = chain_pair(state, decay, True)
    init, gu_pieces = lax.optimization_barrier((init, gu_pieces))
    weight_gu = seq_columns(gu_pieces, here)
    qs = mm(normed, weight_qs).reshape(HEADS, rows, 2 * HEAD)
    gated, mixer_out, probs, mix = mixer_forward(qs, kv, li, init, gain_head8)
    gated = gated.reshape(group, HEAD)
    attn_part = mm(gated, weight_out).astype(BF).reshape(HEADS, rows, D)
    grad_mlp = (mask_all * jnp.concatenate(grad_blocks).astype(F32)).astype(BF)
    attn_out, grad_act = scatter_heads(
        [attn_part[k] for k in range(HEADS)], mm_nt(grad_mlp, weight_down)
    )

    tokens_f = tokens.astype(F32)
    residual = tokens_f + mask_own * attn_out
    scale_two = inverse_rms(residual)
    hat_two = residual * scale_two
    normed_two_own = (hat_two * gain_two).astype(BF)
    normed_two = jnp.concatenate(gather_heads(normed_two_own))

    hidden_width = weight_down.shape[0]
    gate_up = mm(normed_two, weight_gu)
    gate_pre, up_pre = gate_up[:, :hidden_width], gate_up[:, hidden_width:]
    hidden = (jax.nn.silu(gate_pre) * up_pre).astype(BF)
    grad_gate = (grad_act * up_pre * silu_slope(gate_pre)).astype(BF)
    grad_up = (grad_act * jax.nn.silu(gate_pre)).astype(BF)
    grad_gu = jnp.concatenate([grad_gate, grad_up], axis=1)
    order = [here ^ k for k in range(HEADS)]
    hops = range(1, copies)
    down_rows = mlp_down.shape[0]
    two_view = normed_two.reshape(group, HEADS, copies, shard)
    gu_away = [mm_tn(split_rows(two_view, turn, m, order), grad_gu).astype(BF) for m in hops]
    two_part = mm_nt(after(grad_gu, *gu_away), weight_gu).astype(BF)
    gu_total = sum_copies(
        lambda: mm_tn(split_rows(two_view, turn, 0, order), after(grad_gu, two_part)), gu_away
    )
    gu_part = lax.psum_scatter(
        gu_total.reshape(HEADS, shard, 2 * hidden_width), "seq", scatter_dimension=0, tiled=True
    )
    hidden_late = after(hidden, gu_total)

    def down_grad_part(m):
        cut = lax.dynamic_slice_in_dim(hidden_late, (turn ^ m) * down_rows, down_rows, 1)
        return mm_tn(cut, grad_mlp)

    down_total = sum_copies(
        lambda: down_grad_part(0), [down_grad_part(m).astype(BF) for m in hops]
    )
    two_part = two_part.reshape(HEADS, rows, D)
    grad_norm_two, down_total = scatter_heads([two_part[k] for k in range(HEADS)], down_total)
    gain_two_grad = jnp.sum(grad_norm_two * hat_two, axis=0)
    grad_rows = grad_out.astype(F32)
    grad_resid = grad_rows + norm_back(grad_norm_two * gain_two, hat_two, scale_two)
    grad_attn_own = (mask_own * grad_resid).astype(BF)
    attn_blocks = gather_heads(grad_attn_own)
    mlp_part = mm(hidden, weight_down).astype(BF)
    mlp_part, gu_part, *attn_blocks = lax.optimization_barrier((mlp_part, gu_part, *attn_blocks))
    gu_part = swap_diagonal(gu_part)
    grad_attn = jnp.concatenate(attn_blocks)
    mlp_part = mlp_part.reshape(HEADS, rows, D)
    mlp_part = jnp.stack(
        [lax.dynamic_index_in_dim(mlp_part, here ^ k, 0, False) for k in range(HEADS)]
    )

    grad_gated = mm_nt(grad_attn, weight_out).reshape(HEADS, rows, HEAD)
    grad_qs, grad_kv, grad_li, adjoint, slot_part = mixer_backward(
        qs, kv, li, init, gain_head8, mixer_out, probs, mix, grad_gated
    )
    adjoint, gu_part = lax.optimization_barrier((adjoint, gu_part))
    gu_whole = lax.all_gather(gu_part, "seq", axis=0, tiled=True)
    one_view = normed.reshape(group, HEADS, copies, shard)
    one_views = [split_rows(one_view, turn, m, order) for m in range(copies)]
    out_view = gated.reshape(group, 1, copies, shard)
    out_views = [split_rows(out_view, turn, m, [0]) for m in range(copies)]

    def weight_grad(views, right):
        return sum_copies(
            lambda: mm_tn(views[0], right), [mm_tn(views[m], right).astype(BF) for m in hops]
        )

    grad_qs = grad_qs.reshape(group, 2 * HEAD)
    out_total = weight_grad(out_views, grad_attn)
    qs_total = weight_grad(one_views, grad_qs)
    ends = chain_pair(adjoint, decay, False)
    ends, out_total, qs_total = lax.optimization_barrier((ends, out_total, qs_total))
    grad_kv, grad_li = mixer_finish(kv, li, init, ends, grad_kv, grad_li)
    half_rows, line = down_rows // 2, {}
    grad_kv, mlp_part, gu_whole, down_total = lax.optimization_barrier(
        (grad_kv, mlp_part, gu_whole, down_total)
    )
    mlp_out = lax.psum_scatter(mlp_part, "p", scatter_dimension=0, tiled=False).astype(F32)
    down_near = inward(down_total[:half_rows], line)
    grad_qs, down_near = lax.optimization_barrier((grad_qs, down_near))
    result = (residual + mask_own * mlp_out).astype(BF)
    grad_kv = grad_kv.reshape(group, 2 * HEAD)
    grad_li = grad_li.reshape(group, 2 * SLOTS)
    grad_decay = (
        mask_all
        * (grad_li[:, :SLOTS] - grad_li[:, SLOTS:] * jnp.exp(log_sig))
        / NORMALIZER
        * jax.nn.sigmoid(-forget)
    )
    bias_part = jnp.sum(grad_decay, axis=0)
    up_part = lax.dot_general(
        gate_low, grad_decay, (((0,), (0,)), ((), ())), precision=HIGHEST, preferred_element_type=F32
    )
    grad_low = lax.dot_general(
        grad_decay, up_head, (((1,), (1,)), ((), ())), precision=HIGHEST, preferred_element_type=F32
    ).astype(BF)
    down_low_part = mm_tn(normed, grad_low)

    one_part = (
        (mm_nt(grad_qs, weight_qs) + mm_nt(grad_kv, weight_kv) + mm_nt(grad_low, down_full))
        .astype(BF)
        .reshape(HEADS, rows, D)
    )
    kv_total = weight_grad(one_views, grad_kv)
    grad_norm_one, kv_total = scatter_heads([one_part[k] for k in range(HEADS)], kv_total)

    scale_one = inverse_rms(tokens_f)
    hat_one = tokens_f * scale_one
    gain_one_grad = jnp.sum(grad_norm_one * hat_one, axis=0)
    grad_tokens = (grad_resid + norm_back(grad_norm_one * gain_one, hat_one, scale_one)).astype(BF)

    def placed(part, width):
        whole = jnp.zeros(part.shape[:-1] + (HEADS * width,), F32)
        return lax.dynamic_update_slice_in_dim(whole, part, here * width, part.ndim - 1)

    up_sum = placed(up_part, SLOTS).reshape(RANK, HEADS, copies, -1).transpose(1, 2, 0, 3)
    sums = [
        gain_one_grad,
        down_low_part,
        up_sum,
        placed(bias_part, SLOTS),
        placed(slot_part[0], HEAD),
        gain_two_grad,
    ]
    flat = jnp.concatenate([a.reshape(HEADS, copies, -1) for a in sums], axis=2)
    flat = sum_small(flat, here, turn)
    lanes = D * 8
    flat = jnp.pad(flat, (0, -flat.size % lanes)).astype(BF).reshape(-1, D)

    qs_total = qs_total.reshape(HEADS, shard, 2 * HEAD)
    kv_total = kv_total.reshape(HEADS, shard, 2 * HEAD)
    chunks = [down_total[half_rows:], qs_total[1::2], qs_total[0::2]]
    chunks += [kv_total[1::2], kv_total[0::2], jnp.concatenate([out_total, flat])]
    summed = [outward(across(down_near, line), line)]
    for chunk in chunks:
        summed.append(outward(across(inward(chunk, line), line), line))
    near, far, *wide, tail = summed
    down_grad = jnp.concatenate([near, far])
    gate_grad, up_grad = assemble(after(gu_whole, wide[2])[None], order, 2)
    query_grad, swish_grad = spread_line(wide[0], wide[1], here)
    key_grad, value_grad = spread_line(wide[2], wide[3], here)
    out_grad = tail[:shard].astype(F32)
    flat = tail[shard:].reshape(-1).astype(F32)
    totals, offset = [], 0
    for a in sums:
        size = a.size // owners
        totals.append(flat[offset : offset + size])
        offset += size

    return (
        result,
        grad_tokens,
        totals[0],
        query_grad,
        key_grad,
        value_grad,
        totals[1].reshape(shard, RANK),
        totals[2].reshape(RANK, -1),
        totals[3],
        swish_grad,
        totals[4],
        out_grad,
        totals[5],
        gate_grad,
        up_grad,
        down_grad.astype(F32),
    )


def solution(mesh):
    count, span = mesh.devices.shape
    split = Mesh(mesh.devices.reshape(HEADS, count // HEADS, span), ("p", "r", "seq"))
    rows = P(("p", "r", "seq"), None)
    matrix, vector, last = P(("p", "r"), None), P(("p", "r")), P(None, ("p", "r"))
    in_specs = (
        rows, vector, vector, matrix, matrix, matrix, matrix, last, vector, matrix, vector, matrix,
        vector, matrix, matrix, matrix, rows,
    )
    out_specs = (
        rows, rows, vector, matrix, matrix, matrix, matrix, last, vector, matrix, vector, matrix,
        vector, matrix, matrix, matrix,
    )
    return jax.shard_map(body, mesh=split, in_specs=in_specs, out_specs=out_specs, check_vma=False)
```
